256 devices in a mesh: req: 16 (over y, z_lo, core), blk: 16 (over z_hi, x).
Axes of the slice: x: 4, y: 4, z: 8 (z_hi: 4, z_lo: 2; z = z_hi * 2 + z_lo), core: 2. Of those that a mesh axis runs over, the one named last changes fastest.
Arguments:
- queries: bfloat16 [2048, 8192], P('req', 'blk'), may hold values from -120 to 120
- suffix_key_value: bfloat16 [2048, 8, 256], P('req'), may hold values from -6 to 6
- residual: bfloat16 [2048, 8192], P('req', 'blk'), may hold values from -10 to 10
- gain: float32 [8192], P('blk'), may hold values from 0.1 to 1.9
- gate_up: bfloat16 [8192, 2, 14336], P('blk', None, 'req'), may hold values from -0.0625 to 0.0625
- prefix_cache_slots: bfloat16 [128, 128, 8, 256], P('req'), may hold values from -6 to 6
- prefix_page_slots: int32 [128], replicated, may hold values from 0 to 127, each once
- lengths: int32 [16, 4], replicated, may hold values from 1 to 64, 128 in all within a row
- counts: int32 [16], replicated, may hold values from 1 to 128, as said below
Outputs:
- hidden: bfloat16 [2048, 14336], P('blk', 'req')
- suffix_cache: bfloat16 [2048, 2048], P('req', 'blk')
The draws below stay inside these ranges and needn't reach their ends.
Inputs may be any that keep to these rules, and one draw needn't show every extreme that they name: `prefix_page_slots`: slot s of prefix_cache_slots lies on index s // 8 of req; every slot holds exactly one page. Each group's lengths sum to 128, and each group has one request of exactly 64 tokens. `counts`: some group reads all 128 pages.
All inputs are finite; a program needn't handle non-finite values.
Results may differ from the reference program's by a relative error of at most 0.034.
Values may be sent and summed in bfloat16 or wider, within the bound.
A program may use at most 256 MiB of HBM per device.

```python
import math
import jax
import jax.numpy as jnp
import numpy as np
from jax import lax

D = 8192
QUERY_HEADS = 64
KEY_VALUE_HEADS = 8
HEAD_SIZE = 128
FF = 14336
PAGE_TOKENS = 128
RPG = 4
GROUP_TOKENS = 128
GROUPS = 16
SUFFIX_TOKENS = 2048
PREFIX_PAGES = 128


def draw_queries(key, part):
    values = jax.random.normal(key, (SUFFIX_TOKENS, QUERY_HEADS * HEAD_SIZE), jnp.float32) * 3.0
    return jnp.clip(values, -120.0, 120.0).astype(jnp.bfloat16)


def draw_residual(key, part):
    rising = 0.5 * jnp.exp(math.log(3.0) * jnp.arange(D, dtype=jnp.float32) / D)
    values = jax.random.normal(key, (SUFFIX_TOKENS, D), jnp.float32) * rising[None, :]
    return jnp.clip(values, -10.0, 10.0).astype(jnp.bfloat16)


def draw_counts(key, part):
    key_vals, key_top = jax.random.split(jax.random.fold_in(key, 7))
    values = jax.random.randint(key_vals, (GROUPS,), 1, PREFIX_PAGES + 1)
    busiest = jax.random.randint(key_top, (), 0, GROUPS)
    return jnp.where(jnp.arange(GROUPS) == busiest, PREFIX_PAGES, values).astype(jnp.int32)


def level_of(stream_key, shape, pieces, least, top_value):
    level = 1.0
    for dim, blocks in pieces:
        heights = jax.random.uniform(jax.random.fold_in(jax.random.fold_in(stream_key, 6), dim), (blocks,), jnp.float32, least / len(pieces), top_value / len(pieces))
        level = level * jnp.repeat(jnp.exp(heights), shape[dim] // blocks).reshape((-1,) + (1,) * (len(shape) - 1 - dim))
    return level


def split_up(number_of, total, reach, lean):
    loads = [(1 << 20) // math.isqrt(standing ** lean) + 1 for standing in range(2, number_of + 1)]
    surplus, given = total - reach - (number_of - 1), [1] * (number_of - 1)
    while surplus > 0:
        free = [i for i in range(number_of - 1) if given[i] < reach]
        pool, budget = sum([loads[i] for i in free]), surplus
        for i in free:
            extra = min(reach - given[i], max(1, budget * loads[i] // pool), surplus)
            given[i] = given[i] + extra
            surplus = surplus - extra
    return np.array([reach] + given)


def uneven_parts(stream_key, amount, total, bound, skew):
    if amount == 2:
        one = jax.random.randint(stream_key, (), max(1, total - bound), min(bound, total - 1) + 1)
        return jnp.stack([one, total - one])
    sizes = jnp.asarray(split_up(amount, total, bound, skew), jnp.int32)
    twos = (amount - 1) // 2
    source_of, taker = sizes[1:1 + 2 * twos:2], sizes[2:2 + 2 * twos:2]
    room = jnp.minimum(source_of - 1, bound - taker)
    passed = jax.random.randint(jax.random.fold_in(stream_key, 1), (twos,), 0, 1 << 20) % (room + 1)
    sizes = sizes.at[1:1 + 2 * twos:2].set(source_of - passed).at[2:2 + 2 * twos:2].set(taker + passed)
    return sizes[jax.random.permutation(jax.random.fold_in(stream_key, 2), amount)]


def centred(own_key, extent, scale, most, shards=(), held_as=jnp.bfloat16):
    array = jax.random.normal(own_key, extent, jnp.float32) * scale
    if len(shards) > 0:
        array = level_of(own_key, extent, shards, -0.22, 0.18) * array
    return jnp.clip(array, min=-most, max=most).astype(held_as)


def setup_inputs(seed: int = 0) -> dict:
    key_of = jax.random.split(jax.random.key(seed), 10)
    queries = draw_queries(jax.random.fold_in(key_of[9], 71), 0)
    suffix_key_value = centred(key_of[1], (SUFFIX_TOKENS, KEY_VALUE_HEADS, 2 * HEAD_SIZE), 1.0, 6.0, ((0, 16),))
    residual = draw_residual(jax.random.fold_in(key_of[9], 71), 0)
    gain = jnp.clip(1.0 + 0.18 * jax.random.normal(key_of[3], (D,), jnp.float32), 0.1, 1.9)
    gate_up = centred(key_of[4], (D, 2, FF), D ** -0.5, 0.0625, ((0, 16), (2, 16)))
    prefix_cache_slots = centred(key_of[5], (PREFIX_PAGES, PAGE_TOKENS, KEY_VALUE_HEADS, 2 * HEAD_SIZE), 1.0, 6.0, ((0, 16),))
    prefix_page_slots = jax.random.permutation(key_of[6], PREFIX_PAGES).astype(jnp.int32)
    lengths = jax.vmap(lambda own: uneven_parts(own, RPG, GROUP_TOKENS, GROUP_TOKENS // 2, 2))(jax.random.split(key_of[7], GROUPS)).reshape((GROUPS, RPG)).astype(jnp.int32)
    counts = draw_counts(jax.random.fold_in(key_of[9], 71), 0)
    return {"queries": queries, "suffix_key_value": suffix_key_value, "residual": residual, "gain": gain, "gate_up": gate_up, "prefix_cache_slots": prefix_cache_slots, "prefix_page_slots": prefix_page_slots, "lengths": lengths, "counts": counts}


NEGATIVE = -1e+30
EPSILON = 1e-05
ROPE_BASE = 500000.0

def rope_tables(positions, half_dim):
    inverse = jnp.exp(-math.log(ROPE_BASE) * jnp.arange(half_dim, dtype=jnp.float32) * 2.0 / (2 * half_dim))
    angles = positions.astype(jnp.float32)[:, None] * inverse[None, :]
    return (jnp.cos(angles), jnp.sin(angles))

def rotate(vectors, cosines, sines):
    half_dim = vectors.shape[-1] // 2
    lower = vectors[..., :half_dim]
    upper = vectors[..., half_dim:]
    return jnp.concatenate([lower * cosines - upper * sines, upper * cosines + lower * sines], -1)

def suffix_layout(lengths_row, page_count, group_len, page_len):
    starts = (jnp.cumsum(lengths_row) - lengths_row).astype(jnp.int32)
    tokens_at = jnp.arange(group_len, dtype=jnp.int32)
    request = (lax.optimization_barrier(jnp.sum((tokens_at[:, None] >= starts[None, :]).astype(jnp.int32), 1)) - 1).astype(jnp.int32)
    slots_req = jnp.arange(lengths_row.shape[0], dtype=jnp.int32)
    request_begin = lax.optimization_barrier(jnp.sum(jnp.where(request[:, None] == slots_req[None, :], starts[None, :], 0), 1)).astype(jnp.int32)
    offset = (tokens_at - request_begin).astype(jnp.int32)
    return (request, offset, (page_count * page_len + offset).astype(jnp.int32))

def reference(queries, suffix_key_value, residual, gain, gate_up, prefix_cache_slots, prefix_page_slots, lengths, counts):
    heads_per_group = QUERY_HEADS // KEY_VALUE_HEADS
    score_scale = 1.0 / math.sqrt(HEAD_SIZE)
    sorted_rows = prefix_cache_slots[prefix_page_slots].reshape(PREFIX_PAGES * PAGE_TOKENS, KEY_VALUE_HEADS, 2 * HEAD_SIZE)
    prefix_keys = sorted_rows[:, :, :HEAD_SIZE].astype(jnp.float32)
    prefix_values = sorted_rows[:, :, HEAD_SIZE:].astype(jnp.float32)
    key_index = jnp.arange(PREFIX_PAGES * PAGE_TOKENS, dtype=jnp.int32)

    def one_group(group_index):
        query_rows = lax.dynamic_slice_in_dim(queries, group_index * GROUP_TOKENS, GROUP_TOKENS, 0)
        fresh_rows = lax.dynamic_slice_in_dim(suffix_key_value, group_index * GROUP_TOKENS, GROUP_TOKENS, 0)
        page_count = counts[group_index]
        request, offset, positions = suffix_layout(lengths[group_index], page_count, GROUP_TOKENS, PAGE_TOKENS)
        cosines, sines = rope_tables(positions, HEAD_SIZE // 2)
        rotated_query = rotate(query_rows.astype(jnp.float32).reshape(GROUP_TOKENS, QUERY_HEADS, HEAD_SIZE), cosines[:, None], sines[:, None]).astype(jnp.bfloat16)
        keys_new = rotate(fresh_rows[:, :, :HEAD_SIZE].astype(jnp.float32), cosines[:, None], sines[:, None]).astype(jnp.bfloat16)
        values_new = fresh_rows[:, :, HEAD_SIZE:]
        query_float32 = rotated_query.astype(jnp.float32).reshape(GROUP_TOKENS, KEY_VALUE_HEADS, heads_per_group, HEAD_SIZE)
        prefix_scores = jnp.einsum('tkgd,nkd->kgtn', query_float32, prefix_keys) * score_scale
        suffix_scores = jnp.einsum('tkgd,skd->kgts', query_float32, keys_new.astype(jnp.float32)) * score_scale
        prefix_ok = (key_index < page_count * PAGE_TOKENS)[None, None, None, :]
        suffix_ok = ((request[:, None] == request[None, :]) & (offset[None, :] <= offset[:, None]))[None, None]
        prefix_scores = jnp.where(prefix_ok, prefix_scores, NEGATIVE)
        suffix_scores = jnp.where(suffix_ok, suffix_scores, NEGATIVE)
        row_max = jnp.maximum(lax.optimization_barrier(jnp.max(prefix_scores, -1)), lax.optimization_barrier(jnp.max(suffix_scores, -1)))
        prefix_probs = jnp.where(prefix_ok, jnp.exp(prefix_scores - row_max[..., None]), 0.0)
        suffix_probs = jnp.where(suffix_ok, jnp.exp(suffix_scores - row_max[..., None]), 0.0)
        row_sum = lax.optimization_barrier(jnp.sum(prefix_probs, -1)) + lax.optimization_barrier(jnp.sum(suffix_probs, -1))
        weighted = jnp.einsum('kgtn,nkd->tkgd', prefix_probs.astype(jnp.bfloat16).astype(jnp.float32), prefix_values)
        weighted = weighted + jnp.einsum('kgts,skd->tkgd', suffix_probs.astype(jnp.bfloat16).astype(jnp.float32), values_new.astype(jnp.float32))
        attention_output = weighted / jnp.transpose(row_sum, (2, 0, 1))[..., None]
        updated_cache = jnp.concatenate([keys_new, values_new], -1)
        return (attention_output.reshape(GROUP_TOKENS, QUERY_HEADS * HEAD_SIZE), updated_cache.reshape(GROUP_TOKENS, 2 * KEY_VALUE_HEADS * HEAD_SIZE))
    attended_all, cache_list = lax.map(one_group, jnp.arange(GROUPS, dtype=jnp.int32))
    attended_all = attended_all.reshape(SUFFIX_TOKENS, D)
    stream = (residual.astype(jnp.float32) + attended_all).astype(jnp.bfloat16)
    stream_f32 = stream.astype(jnp.float32)
    mean_square = lax.optimization_barrier(jnp.mean(stream_f32 * stream_f32, 1, keepdims=True))
    normed = (stream_f32 * lax.rsqrt(mean_square + EPSILON) * gain.astype(jnp.float32)[None, :]).astype(jnp.bfloat16)
    gate_up_sum = jnp.dot(normed, gate_up.reshape(D, 2 * FF), preferred_element_type=jnp.float32)
    hidden = (jax.nn.silu(gate_up_sum[:, :FF]) * gate_up_sum[:, FF:]).astype(jnp.bfloat16)
    return (hidden, cache_list.reshape(SUFFIX_TOKENS, 2 * KEY_VALUE_HEADS * HEAD_SIZE))
```

```python
import math

import jax
import jax.numpy as jnp
from jax import lax
from jax.experimental import pallas as pl
from jax.experimental.pallas import tpu as pltpu
from jax.sharding import PartitionSpec as P

D = 8192

MESH = pl.DeviceIdType.MESH


NEGATIVE = -1e30
EPSILON = 1e-05
ROPE_BASE = 500000.0


def rope_tables(positions, half_dim):
    inverse = jnp.exp(
        -math.log(ROPE_BASE) * jnp.arange(half_dim, dtype=jnp.float32) * 2.0 / (2 * half_dim)
    )
    angles = positions.astype(jnp.float32)[:, None] * inverse[None, :]
    return (jnp.cos(angles), jnp.sin(angles))


def rotate(vectors, cosines, sines):
    half_dim = vectors.shape[-1] // 2
    lower = vectors[..., :half_dim]
    upper = vectors[..., half_dim:]
    return jnp.concatenate([lower * cosines - upper * sines, upper * cosines + lower * sines], -1)


def suffix_layout(lengths_row, page_count, group_len, page_len):
    starts = jnp.cumsum(lengths_row) - lengths_row
    tokens_at = jnp.arange(group_len, dtype=jnp.int32)
    request = jnp.sum((tokens_at[:, None] >= starts[None, :]).astype(jnp.int32), 1) - 1
    slots_req = jnp.arange(lengths_row.shape[0], dtype=jnp.int32)
    request_begin = jnp.sum(
        jnp.where(request[:, None] == slots_req[None, :], starts[None, :], 0), 1
    )
    offset = tokens_at - request_begin
    return (request, offset, page_count * page_len + offset)


def absorb(state, query, keys_in, values_in, usable, score_scale):
    weighted, running_max, weight_sum = state
    scores = (
        jnp.einsum("tqd,nd->tqn", query, keys_in, preferred_element_type=jnp.float32) * score_scale
    )
    scores = jnp.where(usable, scores, NEGATIVE)
    new_max = jnp.maximum(running_max, jnp.max(scores, -1))
    probs = jnp.where(usable, jnp.exp(scores - new_max[..., None]), 0.0)
    factor = jnp.exp(running_max - new_max)
    weight_sum = weight_sum * factor + jnp.sum(probs, -1)
    weighted = weighted * factor[..., None] + jnp.einsum(
        "tqn,nd->tqd", probs.astype(jnp.bfloat16), values_in, preferred_element_type=jnp.float32
    )
    return (weighted, new_max, weight_sum)


def absorb_pages(state, query, pages_in, page_numbers, limit, score_scale):
    n_pages, page_len, lanes = pages_in.shape
    head_dim = lanes // 2
    key_target = max(page_len, (1 << 20) // (query.shape[0] * query.shape[1]))
    per_block = math.gcd(n_pages, max(1, key_target // page_len))
    n_blocks = n_pages // per_block

    def step(index, carry):
        block = lax.dynamic_slice_in_dim(pages_in, index * per_block, per_block, 0).reshape(
            per_block * page_len, lanes
        )
        numbers = lax.dynamic_slice_in_dim(page_numbers, index * per_block, per_block, 0)
        usable = jnp.repeat(numbers, page_len)[None, None, :] < limit
        return absorb(carry, query, block[:, :head_dim], block[:, head_dim:], usable, score_scale)

    return lax.fori_loop(0, n_blocks, step, state)


def empty_state(rows_count, heads_here, head_dim):
    return (
        jnp.zeros((rows_count, heads_here, head_dim), jnp.float32),
        jnp.full((rows_count, heads_here), NEGATIVE, jnp.float32),
        jnp.zeros((rows_count, heads_here), jnp.float32),
    )


def remote(src, dst, send_sem, recv_sem, req, blk):
    return pltpu.make_async_remote_copy(
        src_ref=src,
        dst_ref=dst,
        send_sem=send_sem,
        recv_sem=recv_sem,
        device_id=(req, blk),
        device_id_type=MESH,
    )


def place():
    req, blk = lax.axis_index("req"), lax.axis_index("blk")
    y, zl, core = req // 4, (req // 2) % 2, req % 2
    return req, blk, y, zl, core, blk // 4, blk % 4


def weight_sends(w_ref, w_all, send, recv):
    req, blk, y, zl, core, zh, x = place()
    half = w_ref.shape[0] // 2
    out = []
    for j, (step, part) in enumerate(((1, 0), (-1, 1), (1, 1), (-1, 0))):
        rows = pl.ds(part * half, half)
        out.append(
            remote(
                w_ref.at[rows],
                w_all.at[x, rows],
                send.at[j],
                recv.at[x, part],
                req,
                zh * 4 + (x + 4 + step) % 4,
            )
        )
    return out


def weight_relays(w_all, send, recv):
    req, blk, y, zl, core, zh, x = place()
    half = w_all.shape[1] // 2
    out = []
    for j, (step, part) in enumerate(((1, 0), (-1, 1))):
        source = (x + 4 - step) % 4
        rows = pl.ds(part * half, half)
        piece = w_all.at[source, rows]
        out.append(
            remote(
                piece,
                piece,
                send.at[4 + j],
                recv.at[source, part],
                req,
                zh * 4 + (x + 4 + step) % 4,
            )
        )
    return out


def weight_wait(w_all, send, recv, source, part):
    req, blk, y, zl, core, zh, x = place()
    half = w_all.shape[1] // 2
    piece = w_all.at[source, pl.ds(part * half, half)]
    remote(piece, piece, send.at[0], recv.at[source, part], req, zh * 4 + (x + 1) % 4).wait_recv()


def spread_features(u_ref, a_all, x_send, z_send, y_send, on_send, core_send, recv):
    req, blk, y, zl, core, zh, x = place()
    target = zl * 2 + core
    home = core == x % 2
    root = x == target
    over_z = y * 4 + (1 - zl) * 2 + core
    sibling = y * 4 + zl * 2 + (1 - core)
    up, down = (y + 1) % 4, (y + 3) % 4
    far = (y + 2) % 4
    req_up, req_down = up * 4 + zl * 2 + core, down * 4 + zl * 2 + core

    def block_copy(yy, xx, send, to_req, to_blk):
        piece = a_all.at[yy, xx]
        return remote(piece, piece, send, recv.at[yy, xx], to_req, to_blk)

    hop = remote(u_ref, a_all.at[y, x], x_send, recv.at[y, x], req, zh * 4 + target)
    keep = pltpu.make_async_copy(u_ref, a_all.at[y, x], recv.at[y, x])

    @pl.when(root)
    def _():
        keep.start()

    @pl.when(jnp.logical_not(root))
    def _():
        hop.start()

    def to_core(yy, xx):
        return block_copy(yy, xx, core_send.at[yy, xx], sibling, blk)

    def to_z(xx):
        return block_copy(y, xx, z_send.at[xx], over_z, blk)

    def to_y(xx, way):
        return block_copy(y, xx, y_send.at[xx, way], (req_up, req_down)[way], blk)

    def onward(xx, way):
        return block_copy((down, up)[way], xx, on_send.at[xx], (req_up, req_down)[way], blk)

    def arrived(yy, xx):
        block_copy(yy, xx, x_send, over_z, blk).wait_recv()

    @pl.when(home)
    def _():
        def own(xx, carry):
            @pl.when(root & (xx == x))
            def _():
                keep.wait()

            @pl.when(jnp.logical_not(root & (xx == x)))
            def _():
                arrived(y, xx)

            @pl.when(root)
            def _():
                to_z(xx).start()

            to_y(xx, 0).start()
            to_y(xx, 1).start()
            to_core(y, xx).start()
            return carry

        lax.fori_loop(0, 4, own, 0)

        def near(xx, carry):
            arrived(down, xx)

            @pl.when(xx < 2)
            def _():
                onward(xx, 0).start()

            to_core(down, xx).start()
            arrived(up, xx)

            @pl.when(xx >= 2)
            def _():
                onward(xx, 1).start()

            to_core(up, xx).start()
            return carry

        lax.fori_loop(0, 4, near, 0)

        def last(xx, carry):
            arrived(far, xx)
            to_core(far, xx).start()
            return carry

        lax.fori_loop(0, 4, last, 0)

    @pl.when(jnp.logical_not(home))
    def _():
        def take(i, carry):
            arrived(i // 4, i % 4)
            return carry

        lax.fori_loop(0, 16, take, 0)

    def drain():
        @pl.when(jnp.logical_not(root))
        def _():
            hop.wait_send()

        @pl.when(home)
        def _():
            def step(xx, carry):
                @pl.when(root)
                def _():
                    to_z(xx).wait_send()

                to_y(xx, 0).wait_send()
                to_y(xx, 1).wait_send()

                @pl.when(xx < 2)
                def _():
                    onward(xx, 0).wait_send()

                @pl.when(xx >= 2)
                def _():
                    onward(xx, 1).wait_send()

                return carry

            lax.fori_loop(0, 4, step, 0)

            def core_step(i, carry):
                to_core(i // 4, i % 4).wait_send()
                return carry

            lax.fori_loop(0, 16, core_step, 0)

    return drain


def ffn_kernel(
    u_ref,
    w_ref,
    hidden_ref,
    w_all,
    a_all,
    product,
    relay,
    final,
    own_sum,
    square_out,
    square_in,
    w_send,
    w_recv,
    w_local,
    x_send,
    z_send,
    y_send,
    on_send,
    core_send,
    a_recv,
    r_send,
    relay_recv,
    final_recv,
    q_send,
    q_recv,
):
    req, blk, y, zl, core, zh, x = place()
    tokens, features = 128, u_ref.shape[1]
    width = hidden_ref.shape[1]
    tiles = 2 * width // 256
    over_z = y * 4 + (1 - zl) * 2 + core
    sibling = y * 4 + zl * 2 + (1 - core)
    req_up = ((y + 1) % 4) * 4 + zl * 2 + core
    req_down = ((y + 3) % 4) * 4 + zl * 2 + core
    blk_up, blk_far, blk_down = [((zh + i) % 4) * 4 + x for i in (1, 2, 3)]

    barrier = pltpu.get_barrier_semaphore()
    peers = [(req, zh * 4 + (x + i) % 4) for i in (1, 2, 3)]
    peers += [(over_z, blk), (sibling, blk), (req_up, blk), (req_down, blk)]
    peers += [(req, blk_up), (req, blk_far), (req, blk_down)]
    for peer in peers:
        pl.semaphore_signal(barrier, inc=1, device_id=peer, device_id_type=MESH)
    pl.semaphore_wait(barrier, len(peers))

    sends = weight_sends(w_ref, w_all, w_send, w_recv)
    for copy in sends:
        copy.start()
    local = pltpu.make_async_copy(w_ref, w_all.at[x], w_local)
    local.start()

    drain = spread_features(u_ref, a_all, x_send, z_send, y_send, on_send, core_send, a_recv)

    relays = weight_relays(w_all, w_send, w_recv)
    for (step, part), copy in zip(((1, 0), (-1, 1)), relays):
        weight_wait(w_all, w_send, w_recv, (x + 4 - step) % 4, part)
        copy.start()

    def squares(zt, carry):
        total = jnp.zeros((8, 128), jnp.float32)
        for xx in range(4):
            rows = a_all[zt, xx, tokens : tokens + 16, 0:256].astype(jnp.float32)
            total = total + rows[0:8, 0:128] + rows[0:8, 128:256]
        square_out[zt] = total
        return carry

    lax.fori_loop(0, 4, squares, 0)
    square_copies = []
    for i in (1, 2, 3):
        there = (zh + i) % 4
        square_copies.append(
            remote(
                square_out.at[there],
                square_in.at[i - 1],
                q_send.at[i - 1],
                q_recv.at[i - 1],
                req,
                there * 4 + x,
            )
        )
    for copy in square_copies:
        copy.start()

    weight_wait(w_all, w_send, w_recv, (x + 3) % 4, 1)
    weight_wait(w_all, w_send, w_recv, (x + 1) % 4, 0)
    weight_wait(w_all, w_send, w_recv, (x + 2) % 4, 0)
    weight_wait(w_all, w_send, w_recv, (x + 2) % 4, 1)
    local.wait()

    def multiply(zt, target):
        def tile(n, carry):
            cols = pl.ds(pl.multiple_of(n * 256, 256), 256)
            total = jnp.dot(
                a_all[zt, 0, 0:tokens, :], w_all[0, :, cols], preferred_element_type=jnp.float32
            )
            for xx in range(1, 4):
                total = total + jnp.dot(
                    a_all[zt, xx, 0:tokens, :],
                    w_all[xx, :, cols],
                    preferred_element_type=jnp.float32,
                )
            target[:, cols] = total.astype(target.dtype)
            return carry

        lax.fori_loop(0, tiles, tile, 0)

    half = tokens // 2
    top, bottom = pl.ds(0, half), pl.ds(half, half)
    far_up = remote(
        product.at[0, top], relay.at[0], r_send.at[0], relay_recv.at[0], req, blk_up
    )
    far_down = remote(
        product.at[0, bottom], relay.at[1], r_send.at[1], relay_recv.at[1], req, blk_down
    )
    up_bottom = remote(
        product.at[1, bottom], final.at[0, bottom], r_send.at[2], final_recv.at[0, 1], req, blk_up
    )
    up_top = remote(
        product.at[1, top], final.at[0, top], r_send.at[3], final_recv.at[0, 0], req, blk_up
    )
    down_top = remote(
        product.at[2, top], final.at[1, top], r_send.at[4], final_recv.at[1, 0], req, blk_down
    )
    down_bottom = remote(
        product.at[2, bottom], final.at[1, bottom], r_send.at[5], final_recv.at[1, 1], req, blk_down
    )
    multiply((zh + 2) % 4, product.at[0])
    far_up.start()
    far_down.start()
    multiply((zh + 1) % 4, product.at[1])
    up_bottom.start()
    multiply((zh + 3) % 4, product.at[2])
    down_top.start()

    def add_relay(slot, rows, index):
        def tile(n, carry):
            cols = pl.ds(pl.multiple_of(n * 256, 256), 256)
            total = product[slot, rows, cols].astype(jnp.float32) + relay[index, :, cols].astype(
                jnp.float32
            )
            product[slot, rows, cols] = total.astype(jnp.bfloat16)
            return carry

        lax.fori_loop(0, tiles, tile, 0)

    far_up.wait_recv()
    add_relay(1, top, 0)
    up_top.start()
    far_down.wait_recv()
    add_relay(2, bottom, 1)
    down_bottom.start()
    multiply(zh, own_sum)

    for copy in square_copies:
        copy.wait_recv()
    row = square_out[zh] + square_in[0] + square_in[1] + square_in[2]
    spread = jnp.broadcast_to(row[0:1, :], (tokens, tokens))
    diagonal = lax.broadcasted_iota(jnp.int32, (tokens, tokens), 0) == lax.broadcasted_iota(
        jnp.int32, (tokens, tokens), 1
    )
    square_sum = jnp.sum(jnp.where(diagonal, spread, 0.0), 1, keepdims=True)
    scale = jnp.broadcast_to(lax.rsqrt(square_sum / D + EPSILON), (tokens, 128))

    up_bottom.wait_recv()
    down_top.wait_recv()
    up_top.wait_recv()
    down_bottom.wait_recv()

    def finish(n, carry):
        def column_sum(start):
            cols = pl.ds(pl.multiple_of(start, 128), 128)
            total = own_sum[:, cols] + final[0, :, cols].astype(jnp.float32)
            return (total + final[1, :, cols].astype(jnp.float32)) * scale

        gate, up = column_sum(n * 128), column_sum(width + n * 128)
        value = gate / (1.0 + jnp.exp(-gate)) * up
        hidden_ref[:, pl.ds(pl.multiple_of(n * 128, 128), 128)] = value.astype(jnp.bfloat16)
        return carry

    lax.fori_loop(0, width // 128, finish, 0)

    for copy in sends + relays + square_copies:
        copy.wait_send()
    for copy in (far_up, far_down, up_bottom, up_top, down_top, down_bottom):
        copy.wait_send()
    drain()


def ffn(u_ext, weights):
    depth, wide = weights.shape
    dma = pltpu.SemaphoreType.DMA
    bf16, f32 = jnp.bfloat16, jnp.float32
    return pl.pallas_call(
        ffn_kernel,
        out_shape=jax.ShapeDtypeStruct((128, wide // 2), bf16),
        in_specs=[
            pl.BlockSpec(memory_space=pltpu.VMEM),
            pl.BlockSpec(memory_space=pl.ANY),
        ],
        out_specs=pl.BlockSpec(memory_space=pltpu.VMEM),
        scratch_shapes=[
            pltpu.VMEM((4, depth, wide), bf16),
            pltpu.VMEM((4, 4) + u_ext.shape, bf16),
            pltpu.VMEM((3, 128, wide), bf16),
            pltpu.VMEM((2, 64, wide), bf16),
            pltpu.VMEM((2, 128, wide), bf16),
            pltpu.VMEM((128, wide), f32),
            pltpu.VMEM((4, 8, 128), f32),
            pltpu.VMEM((3, 8, 128), f32),
            dma((6,)),
            dma((4, 2)),
            dma,
            dma,
            dma((4,)),
            dma((4, 2)),
            dma((4,)),
            dma((4, 4)),
            dma((4, 4)),
            dma((6,)),
            dma((2,)),
            dma((2, 2)),
            dma((3,)),
            dma((3,)),
        ],
        compiler_params=pltpu.CompilerParams(collective_id=1, has_side_effects=True),
        name="ffn",
    )(u_ext, weights)


def on_device(
    queries,
    suffix_key_value,
    residual,
    gain,
    gate_up,
    prefix_cache_slots,
    prefix_page_slots,
    lengths,
    counts,
):
    blocks = lax.axis_size("blk")
    column = lax.axis_index("blk")
    group_index = lax.axis_index("req")
    group_len = queries.shape[0]
    heads_kv = suffix_key_value.shape[1]
    head_dim = suffix_key_value.shape[2] // 2
    heads_here = queries.shape[1] // head_dim
    page_len = prefix_cache_slots.shape[1]
    score_scale = 1.0 / math.sqrt(head_dim)
    kv_head = column * heads_kv // blocks
    page_count = counts[group_index]
    request, offset, positions = suffix_layout(
        lengths[group_index], page_count, group_len, page_len
    )
    cosines, sines = rope_tables(positions, head_dim // 2)
    rotated_query = rotate(
        queries.astype(jnp.float32).reshape(group_len, heads_here, head_dim),
        cosines[:, None],
        sines[:, None],
    ).astype(jnp.bfloat16)
    own_head = lax.dynamic_index_in_dim(suffix_key_value, kv_head, 1, keepdims=False)
    keys_new = rotate(own_head[:, :head_dim].astype(jnp.float32), cosines, sines).astype(
        jnp.bfloat16
    )
    values_new = own_head[:, head_dim:]
    both_new = jnp.concatenate([keys_new, values_new], 1)
    lane_width = 2 * heads_kv * head_dim // blocks
    updated_cache = lax.dynamic_slice_in_dim(
        both_new, column * lane_width % (2 * head_dim), lane_width, 1
    )
    allowed = (request[:, None] == request[None, :]) & (offset[None, :] <= offset[:, None])
    state = absorb(
        empty_state(group_len, heads_here, head_dim),
        rotated_query,
        keys_new,
        values_new,
        allowed[:, None, :],
        score_scale,
    )
    pages_total = prefix_page_slots.shape[0]
    page_ids = jnp.arange(pages_total, dtype=jnp.int32)
    own_slots = lax.dynamic_index_in_dim(prefix_cache_slots, kv_head, 2, keepdims=False)
    shard_piece = lax.all_gather(own_slots, "req", axis=0, tiled=True)
    slot_ids = jnp.arange(shard_piece.shape[0], dtype=jnp.int32)
    match = prefix_page_slots[None, :] == slot_ids[:, None]
    state = absorb_pages(
        state,
        rotated_query,
        shard_piece,
        jnp.sum(jnp.where(match, page_ids[None, :], 0), 1),
        page_count,
        score_scale,
    )
    attention_output = (state[0] / state[2][..., None]).reshape(group_len, heads_here * head_dim)
    stream = (residual.astype(jnp.float32) + attention_output).astype(jnp.bfloat16)
    stream_f32 = stream.astype(jnp.float32)
    square_sum = jnp.sum(stream_f32 * stream_f32, 1)
    scaled = (stream_f32 * gain[None, :]).astype(jnp.bfloat16)
    high = square_sum.astype(jnp.bfloat16)
    low = (square_sum - high.astype(jnp.float32)).astype(jnp.bfloat16)
    row = jnp.concatenate([high, low, jnp.zeros((gain.shape[0] - 2 * group_len,), jnp.bfloat16)])
    u_ext = jnp.concatenate([scaled, jnp.broadcast_to(row[None, :], (16, row.shape[0]))], 0)
    weights = gate_up.reshape(gate_up.shape[0], 2 * gate_up.shape[2])
    return (ffn(u_ext, weights), updated_cache)


def solution(mesh):
    placed = (
        P("req", "blk"),
        P("req", None, None),
        P("req", "blk"),
        P("blk"),
        P("blk", None, "req"),
        P("req", None, None, None),
        P(),
        P(),
        P(),
    )
    return jax.shard_map(
        on_device,
        mesh=mesh,
        in_specs=placed,
        out_specs=(P("blk", "req"), P("req", "blk")),
        check_vma=False,
    )
```

```python
import math

import jax
import jax.numpy as jnp
from jax import lax
from jax.experimental import pallas as pl
from jax.experimental.pallas import tpu as pltpu
from jax.sharding import PartitionSpec as P

D = 8192

MESH = pl.DeviceIdType.MESH

NEGATIVE = -1e30
EPSILON = 1e-05
ROPE_BASE = 500000.0


def rope_tables(positions, half_dim):
    inverse = jnp.exp(
        -math.log(ROPE_BASE) * jnp.arange(half_dim, dtype=jnp.float32) * 2.0 / (2 * half_dim)
    )
    angles = positions.astype(jnp.float32)[:, None] * inverse[None, :]
    return (jnp.cos(angles), jnp.sin(angles))


def rotate(vectors, cosines, sines):
    half_dim = vectors.shape[-1] // 2
    lower = vectors[..., :half_dim]
    upper = vectors[..., half_dim:]
    return jnp.concatenate([lower * cosines - upper * sines, upper * cosines + lower * sines], -1)


def suffix_layout(lengths_row, page_count, group_len, page_len):
    starts = jnp.cumsum(lengths_row) - lengths_row
    tokens_at = jnp.arange(group_len, dtype=jnp.int32)
    request = jnp.sum((tokens_at[:, None] >= starts[None, :]).astype(jnp.int32), 1) - 1
    slots_req = jnp.arange(lengths_row.shape[0], dtype=jnp.int32)
    request_begin = jnp.sum(
        jnp.where(request[:, None] == slots_req[None, :], starts[None, :], 0), 1
    )
    offset = tokens_at - request_begin
    return (request, offset, page_count * page_len + offset)


def remote(src, dst, send_sem, recv_sem, req, blk):
    return pltpu.make_async_remote_copy(
        src_ref=src,
        dst_ref=dst,
        send_sem=send_sem,
        recv_sem=recv_sem,
        device_id=(req, blk),
        device_id_type=MESH,
    )


def place():
    req, blk = lax.axis_index("req"), lax.axis_index("blk")
    y, zl, core = req // 4, (req // 2) % 2, req % 2
    return req, blk, y, zl, core, blk // 4, blk % 4


def weight_sends(w_ref, w_all, send, recv):
    req, blk, y, zl, core, zh, x = place()
    half = w_ref.shape[0] // 2
    out = []
    for j, (step, part) in enumerate(((1, 0), (-1, 1), (1, 1), (-1, 0))):
        rows = pl.ds(part * half, half)
        out.append(
            remote(
                w_ref.at[rows],
                w_all.at[x, rows],
                send.at[j],
                recv.at[x, part],
                req,
                zh * 4 + (x + 4 + step) % 4,
            )
        )
    return out


def weight_relays(w_all, send, recv):
    req, blk, y, zl, core, zh, x = place()
    half = w_all.shape[1] // 2
    out = []
    for j, (step, part) in enumerate(((1, 0), (-1, 1))):
        source = (x + 4 - step) % 4
        rows = pl.ds(part * half, half)
        piece = w_all.at[source, rows]
        out.append(
            remote(
                piece,
                piece,
                send.at[4 + j],
                recv.at[source, part],
                req,
                zh * 4 + (x + 4 + step) % 4,
            )
        )
    return out


def weight_wait(w_all, send, recv, source, part):
    req, blk, y, zl, core, zh, x = place()
    half = w_all.shape[1] // 2
    piece = w_all.at[source, pl.ds(part * half, half)]
    remote(piece, piece, send.at[0], recv.at[source, part], req, zh * 4 + (x + 1) % 4).wait_recv()


def spread_features(u_ref, a_all, x_send, z_send, y_send, on_send, core_send, recv):
    req, blk, y, zl, core, zh, x = place()
    target = zl * 2 + core
    home = core == x % 2
    root = x == target
    over_z = y * 4 + (1 - zl) * 2 + core
    sibling = y * 4 + zl * 2 + (1 - core)
    up, down = (y + 1) % 4, (y + 3) % 4
    far = (y + 2) % 4
    req_up, req_down = up * 4 + zl * 2 + core, down * 4 + zl * 2 + core

    def block_copy(yy, xx, send, to_req, to_blk):
        piece = a_all.at[yy, xx]
        return remote(piece, piece, send, recv.at[yy, xx], to_req, to_blk)

    hop = remote(u_ref, a_all.at[y, x], x_send, recv.at[y, x], req, zh * 4 + target)
    keep = pltpu.make_async_copy(u_ref, a_all.at[y, x], recv.at[y, x])

    @pl.when(root)
    def _():
        keep.start()

    @pl.when(jnp.logical_not(root))
    def _():
        hop.start()

    def to_core(yy, xx):
        return block_copy(yy, xx, core_send.at[yy, xx], sibling, blk)

    def to_z(xx):
        return block_copy(y, xx, z_send.at[xx], over_z, blk)

    def to_y(xx, way):
        return block_copy(y, xx, y_send.at[xx, way], (req_up, req_down)[way], blk)

    def onward(xx, way):
        return block_copy((down, up)[way], xx, on_send.at[xx], (req_up, req_down)[way], blk)

    def arrived(yy, xx):
        block_copy(yy, xx, x_send, over_z, blk).wait_recv()

    @pl.when(home)
    def _():
        def own(xx, carry):
            @pl.when(root & (xx == x))
            def _():
                keep.wait()

            @pl.when(jnp.logical_not(root & (xx == x)))
            def _():
                arrived(y, xx)

            @pl.when(root)
            def _():
                to_z(xx).start()

            to_y(xx, 0).start()
            to_y(xx, 1).start()
            to_core(y, xx).start()
            return carry

        lax.fori_loop(0, 4, own, 0)

        def near(xx, carry):
            arrived(down, xx)

            @pl.when(xx < 2)
            def _():
                onward(xx, 0).start()

            to_core(down, xx).start()
            arrived(up, xx)

            @pl.when(xx >= 2)
            def _():
                onward(xx, 1).start()

            to_core(up, xx).start()
            return carry

        lax.fori_loop(0, 4, near, 0)

        def last(xx, carry):
            arrived(far, xx)
            to_core(far, xx).start()
            return carry

        lax.fori_loop(0, 4, last, 0)

    @pl.when(jnp.logical_not(home))
    def _():
        def take(i, carry):
            arrived(i // 4, i % 4)
            return carry

        lax.fori_loop(0, 16, take, 0)

    def drain():
        @pl.when(jnp.logical_not(root))
        def _():
            hop.wait_send()

        @pl.when(home)
        def _():
            def step(xx, carry):
                @pl.when(root)
                def _():
                    to_z(xx).wait_send()

                to_y(xx, 0).wait_send()
                to_y(xx, 1).wait_send()

                @pl.when(xx < 2)
                def _():
                    onward(xx, 0).wait_send()

                @pl.when(xx >= 2)
                def _():
                    onward(xx, 1).wait_send()

                return carry

            lax.fori_loop(0, 4, step, 0)

            def core_step(i, carry):
                to_core(i // 4, i % 4).wait_send()
                return carry

            lax.fori_loop(0, 16, core_step, 0)

    return drain


def group_at(j):
    h = j // 2
    return h + h // 2 - 2 * (h // 3), j % 2


def layer_kernel(
    q_ref,
    cos_ref,
    sin_ref,
    fresh_ref,
    allowed_ref,
    hide_ref,
    pages_ref,
    residual_ref,
    gain_ref,
    w_ref,
    hidden_ref,
    q_all,
    kv_all,
    values_t,
    scores,
    probs,
    part_out,
    stat_out,
    part_in,
    stat_in,
    u_ref,
    w_all,
    a_all,
    product,
    relay,
    final,
    own_sum,
    square_out,
    square_in,
    query_send,
    query_recv,
    page_send,
    page_recv,
    part_send,
    part_recv,
    stat_send,
    stat_recv,
    w_send,
    w_recv,
    w_local,
    x_send,
    z_send,
    y_send,
    on_send,
    core_send,
    a_recv,
    r_send,
    relay_recv,
    final_recv,
    q_send,
    q_recv,
):
    req, blk, y, zl, core, zh, x = place()
    tokens, features = q_ref.shape
    heads = features // 128
    keys_here = pages_ref.shape[0]
    rows_all = heads * tokens
    width = hidden_ref.shape[1]
    tiles = 2 * width // 256
    sibling = y * 4 + zl * 2 + (1 - core)
    blk_up, blk_far, blk_down = [((zh + i) % 4) * 4 + x for i in (1, 2, 3)]
    turn = (1.0 / math.sqrt(128)) * math.log2(math.e)

    def ahead(j):
        dy, dz = group_at(j)
        return ((y + dy) % 4) * 4 + ((zl + dz) % 2) * 2 + core

    def behind(j):
        dy, dz = group_at(j)
        return ((y + 4 - dy) % 4) * 4 + ((zl + dz) % 2) * 2 + core

    barrier = pltpu.get_barrier_semaphore()
    peers = [(req, zh * 4 + (x + i) % 4) for i in (1, 2, 3)]
    peers += [(sibling, blk), (req, blk_up), (req, blk_far), (req, blk_down)]
    peers += [(ahead(j), blk) for j in range(1, 8)]
    for peer in peers:
        pl.semaphore_signal(barrier, inc=1, device_id=peer, device_id_type=MESH)

    cosines, sines = cos_ref[...], sin_ref[...]
    for h in range(heads):
        vector = q_ref[:, h * 128 : (h + 1) * 128].astype(jnp.float32)
        turned = vector * cosines + pltpu.roll(vector, 64, 1) * sines
        q_all[0, h * tokens : (h + 1) * tokens, :] = turned.astype(jnp.bfloat16)
    pl.semaphore_wait(barrier, len(peers))

    page_copy = remote(pages_ref, kv_all.at[core], page_send, page_recv, sibling, blk)
    page_copy.start()
    query_copies = [
        remote(q_all.at[0], q_all.at[j], query_send.at[j], query_recv.at[j], ahead(j), blk)
        for j in range(1, 8)
    ]
    for copy in query_copies:
        copy.start()
    sends = weight_sends(w_ref, w_all, w_send, w_recv)
    for copy in sends:
        copy.start()
    local = pltpu.make_async_copy(w_ref, w_all.at[x], w_local)
    local.start()
    kv_all[core] = pages_ref[...]

    def fold(block, op):
        parts = [block[i * 8 : (i + 1) * 8] for i in range(block.shape[0] // 8)]
        while len(parts) > 1:
            parts = [op(a, b) for a, b in zip(parts[::2], parts[1::2])]
        return parts[0]

    def last_fold(rows, op):
        return op(rows, 0, keepdims=True)

    fresh_t = jnp.transpose(fresh_ref[:, 128:256].astype(jnp.float32)).astype(jnp.bfloat16)
    raw = lax.dot_general(
        fresh_ref[:, 0:128],
        q_all[0],
        (((1,), (1,)), ((), ())),
        preferred_element_type=jnp.float32,
    )
    mask = jnp.concatenate([allowed_ref[...]] * heads, 1)
    raw = jnp.where(mask > 0, raw, NEGATIVE)
    suffix_max = last_fold(fold(raw, jnp.maximum), jnp.max)
    suffix_probs = jnp.exp2((raw - suffix_max) * turn)
    suffix_sum = last_fold(fold(suffix_probs, jnp.add), jnp.sum)
    suffix_part = jnp.dot(
        fresh_t, suffix_probs.astype(jnp.bfloat16), preferred_element_type=jnp.float32
    )

    def turn_values(which):
        for p in range(keys_here // 128):
            block = kv_all[which, p * 128 : (p + 1) * 128, 128:256].astype(jnp.float32)
            where = pl.ds(pl.multiple_of(which * keys_here + p * 128, 128), 128)
            values_t[:, where] = jnp.transpose(block).astype(jnp.bfloat16)

    turn_values(core)
    remote(pages_ref, kv_all.at[1 - core], page_send, page_recv, sibling, blk).wait_recv()
    turn_values(1 - core)

    chunk = 512
    chunks = 2 * keys_here // chunk
    per_core = keys_here // chunk

    def score_chunk(c, j, slot, top):
        keys = kv_all[c // per_core, (c % per_core) * chunk : (c % per_core + 1) * chunk, 0:128]
        raw = lax.dot_general(
            keys, q_all[j], (((1,), (1,)), ((), ())), preferred_element_type=jnp.float32
        )
        scores[slot, c * chunk : (c + 1) * chunk, :] = raw
        for p in range(chunk // 128):
            page = c * (chunk // 128) + p
            folded = fold(raw[p * 128 : (p + 1) * 128], jnp.maximum)
            top = jnp.maximum(top, folded + hide_ref[page, j])
        return top

    def weigh_chunk(c, j, slot, top, total, weighted):
        for p in range(chunk // 128):
            page = c * (chunk // 128) + p
            rows = slice(page * 128, (page + 1) * 128)
            level = top - 4.0 * hide_ref[page, j]
            weights = jnp.exp2((scores[slot, rows, :] - level) * turn)
            total = total + fold(weights, jnp.add)
            probs[rows, :] = weights.astype(jnp.bfloat16)
        part = jnp.dot(
            values_t[:, c * chunk : (c + 1) * chunk],
            probs[c * chunk : (c + 1) * chunk, :],
            preferred_element_type=jnp.float32,
        )
        return total, part if weighted is None else weighted + part

    def store_part(j, top, total, weighted):
        part_out[j] = weighted.astype(jnp.bfloat16)
        first = lax.broadcasted_iota(jnp.int32, (8, rows_all), 0) == 0
        stat_out[j] = jnp.where(first, top, last_fold(total, jnp.sum))

    def part_copies(j):
        return (
            remote(
                part_out.at[j], part_in.at[j], part_send.at[j], part_recv.at[j], behind(j), blk
            ),
            remote(
                stat_out.at[j], stat_in.at[j], stat_send.at[j], stat_recv.at[j], behind(j), blk
            ),
        )

    low = jnp.full((8, rows_all), NEGATIVE, jnp.float32)
    zero = jnp.zeros((8, rows_all), jnp.float32)
    top = low
    for c in range(chunks):
        top = score_chunk(c, 0, 0, top)
    first_top = last_fold(top, jnp.max)

    def group_step(j, done_top):
        remote(
            q_all.at[0], q_all.at[j], query_send.at[1], query_recv.at[j], ahead(1), blk
        ).wait_recv()
        top, total, weighted = low, zero, None
        for c in range(chunks):
            top = score_chunk(c, j, j % 2, top)
            total, weighted = weigh_chunk(c, j - 1, (j - 1) % 2, done_top, total, weighted)
        store_part(j - 1, done_top, total, weighted)

        @pl.when(j >= 2)
        def _():
            for copy in part_copies(j - 1):
                copy.start()

        return last_fold(top, jnp.max)

    last_top = lax.fori_loop(1, 8, group_step, first_top)
    total, weighted = zero, None
    for c in range(chunks):
        total, weighted = weigh_chunk(c, 7, 1, last_top, total, weighted)
    store_part(7, last_top, total, weighted)
    for copy in part_copies(7):
        copy.start()

    relays = weight_relays(w_all, w_send, w_recv)
    for (step, part), copy in zip(((1, 0), (-1, 1)), relays):
        weight_wait(w_all, w_send, w_recv, (x + 4 - step) % 4, part)
        copy.start()

    for j in range(1, 8):
        part_copies(j)[1].wait_recv()
    tops = [stat_out[0, 0:1, :]] + [stat_in[j, 0:1, :] for j in range(1, 8)]
    sums = [stat_out[0, 1:2, :]] + [stat_in[j, 1:2, :] for j in range(1, 8)]
    joint = suffix_max
    for row in tops:
        joint = jnp.maximum(joint, row)
    factor = jnp.exp2((suffix_max - joint) * turn)
    joint_sum = suffix_sum * factor
    attended = suffix_part * factor
    for j in range(8):
        factor = jnp.exp2((tops[j] - joint) * turn)
        joint_sum = joint_sum + sums[j] * factor
        if j:
            part_copies(j)[0].wait_recv()
        part = part_in[j] if j else part_out[0]
        attended = attended + part.astype(jnp.float32) * factor
    attended = attended / joint_sum

    squares_here = jnp.zeros((tokens, 128), jnp.float32)
    for h in range(heads):
        cols = slice(h * 128, (h + 1) * 128)
        own = jnp.transpose(attended[:, h * tokens : (h + 1) * tokens])
        stream = (residual_ref[:, cols].astype(jnp.float32) + own).astype(jnp.bfloat16)
        stream = stream.astype(jnp.float32)
        squares_here = squares_here + stream * stream
        u_ref[0:tokens, cols] = (stream * gain_ref[:, cols]).astype(jnp.bfloat16)
    square_row = jnp.sum(jnp.transpose(squares_here), 0, keepdims=True)
    high = square_row.astype(jnp.bfloat16)
    below = (square_row - high.astype(jnp.float32)).astype(jnp.bfloat16)
    u_ref[tokens : tokens + 16, 0:128] = jnp.broadcast_to(high, (16, 128))
    u_ref[tokens : tokens + 16, 128:256] = jnp.broadcast_to(below, (16, 128))
    u_ref[tokens : tokens + 16, 256:features] = jnp.zeros((16, features - 256), jnp.bfloat16)

    drain = spread_features(u_ref, a_all, x_send, z_send, y_send, on_send, core_send, a_recv)

    def squares(zt, carry):
        total = jnp.zeros((8, 128), jnp.float32)
        for xx in range(4):
            rows = a_all[zt, xx, tokens : tokens + 16, 0:256].astype(jnp.float32)
            total = total + rows[0:8, 0:128] + rows[0:8, 128:256]
        square_out[zt] = total
        return carry

    lax.fori_loop(0, 4, squares, 0)
    square_copies = []
    for i in (1, 2, 3):
        there = (zh + i) % 4
        square_copies.append(
            remote(
                square_out.at[there],
                square_in.at[i - 1],
                q_send.at[i - 1],
                q_recv.at[i - 1],
                req,
                there * 4 + x,
            )
        )
    for copy in square_copies:
        copy.start()

    weight_wait(w_all, w_send, w_recv, (x + 3) % 4, 1)
    weight_wait(w_all, w_send, w_recv, (x + 1) % 4, 0)
    weight_wait(w_all, w_send, w_recv, (x + 2) % 4, 0)
    weight_wait(w_all, w_send, w_recv, (x + 2) % 4, 1)
    local.wait()

    def multiply(zt, target):
        def tile(n, carry):
            cols = pl.ds(pl.multiple_of(n * 256, 256), 256)
            total = jnp.dot(
                a_all[zt, 0, 0:tokens, :], w_all[0, :, cols], preferred_element_type=jnp.float32
            )
            for xx in range(1, 4):
                total = total + jnp.dot(
                    a_all[zt, xx, 0:tokens, :],
                    w_all[xx, :, cols],
                    preferred_element_type=jnp.float32,
                )
            target[:, cols] = total.astype(target.dtype)
            return carry

        lax.fori_loop(0, tiles, tile, 0)

    half = tokens // 2
    top, bottom = pl.ds(0, half), pl.ds(half, half)
    far_up = remote(
        product.at[0, top], relay.at[0], r_send.at[0], relay_recv.at[0], req, blk_up
    )
    far_down = remote(
        product.at[0, bottom], relay.at[1], r_send.at[1], relay_recv.at[1], req, blk_down
    )
    up_bottom = remote(
        product.at[1, bottom], final.at[0, bottom], r_send.at[2], final_recv.at[0, 1], req, blk_up
    )
    up_top = remote(
        product.at[1, top], final.at[0, top], r_send.at[3], final_recv.at[0, 0], req, blk_up
    )
    down_top = remote(
        product.at[2, top], final.at[1, top], r_send.at[4], final_recv.at[1, 0], req, blk_down
    )
    down_bottom = remote(
        product.at[2, bottom], final.at[1, bottom], r_send.at[5], final_recv.at[1, 1], req, blk_down
    )
    multiply((zh + 2) % 4, product.at[0])
    far_up.start()
    far_down.start()
    multiply((zh + 1) % 4, product.at[1])
    up_bottom.start()
    multiply((zh + 3) % 4, product.at[2])
    down_top.start()

    def add_relay(slot, rows, index):
        def tile(n, carry):
            cols = pl.ds(pl.multiple_of(n * 256, 256), 256)
            total = product[slot, rows, cols].astype(jnp.float32) + relay[index, :, cols].astype(
                jnp.float32
            )
            product[slot, rows, cols] = total.astype(jnp.bfloat16)
            return carry

        lax.fori_loop(0, tiles, tile, 0)

    far_up.wait_recv()
    add_relay(1, top, 0)
    up_top.start()
    far_down.wait_recv()
    add_relay(2, bottom, 1)
    down_bottom.start()
    multiply(zh, own_sum)

    for copy in square_copies:
        copy.wait_recv()
    row = square_out[zh] + square_in[0] + square_in[1] + square_in[2]
    spread = jnp.broadcast_to(row[0:1, :], (tokens, tokens))
    diagonal = lax.broadcasted_iota(jnp.int32, (tokens, tokens), 0) == lax.broadcasted_iota(
        jnp.int32, (tokens, tokens), 1
    )
    square_sum = jnp.sum(jnp.where(diagonal, spread, 0.0), 1, keepdims=True)
    scale = jnp.broadcast_to(lax.rsqrt(square_sum / D + EPSILON), (tokens, 128))

    up_bottom.wait_recv()
    down_top.wait_recv()
    up_top.wait_recv()
    down_bottom.wait_recv()

    def finish(n, carry):
        def column_sum(start):
            cols = pl.ds(pl.multiple_of(start, 128), 128)
            total = own_sum[:, cols] + final[0, :, cols].astype(jnp.float32)
            return (total + final[1, :, cols].astype(jnp.float32)) * scale

        gate, up = column_sum(n * 128), column_sum(width + n * 128)
        value = gate / (1.0 + jnp.exp(-gate)) * up
        hidden_ref[:, pl.ds(pl.multiple_of(n * 128, 128), 128)] = value.astype(jnp.bfloat16)
        return carry

    lax.fori_loop(0, width // 128, finish, 0)

    for copy in sends + relays + square_copies:
        copy.wait_send()
    for copy in (far_up, far_down, up_bottom, up_top, down_top, down_bottom):
        copy.wait_send()
    drain()


    for copy in query_copies:
        copy.wait_send()
    page_copy.wait_send()
    for j in range(1, 8):
        for copy in part_copies(j):
            copy.wait_send()


def layer(q, cosines, sines, fresh, allowed, hide, pages, residual, gain, weights):
    depth, wide = weights.shape
    tokens, features = q.shape
    rows_all = tokens * features // 128
    keys = 2 * pages.shape[0]
    dma = pltpu.SemaphoreType.DMA
    bf16, f32 = jnp.bfloat16, jnp.float32
    vmem = pl.BlockSpec(memory_space=pltpu.VMEM)
    return pl.pallas_call(
        layer_kernel,
        out_shape=jax.ShapeDtypeStruct((tokens, wide // 2), bf16),
        in_specs=[vmem] * 5
        + [pl.BlockSpec(memory_space=pltpu.SMEM)]
        + [vmem] * 3
        + [pl.BlockSpec(memory_space=pl.ANY)],
        out_specs=vmem,
        scratch_shapes=[
            pltpu.VMEM((8, rows_all, 128), bf16),
            pltpu.VMEM((2,) + pages.shape, bf16),
            pltpu.VMEM((128, keys), bf16),
            pltpu.VMEM((2, keys, rows_all), f32),
            pltpu.VMEM((keys, rows_all), bf16),
            pltpu.VMEM((8, 128, rows_all), bf16),
            pltpu.VMEM((8, 8, rows_all), f32),
            pltpu.VMEM((8, 128, rows_all), bf16),
            pltpu.VMEM((8, 8, rows_all), f32),
            pltpu.VMEM((tokens + 16, features), bf16),
            pltpu.VMEM((4, depth, wide), bf16),
            pltpu.VMEM((4, 4, tokens + 16, features), bf16),
            pltpu.VMEM((3, tokens, wide), bf16),
            pltpu.VMEM((2, tokens // 2, wide), bf16),
            pltpu.VMEM((2, tokens, wide), bf16),
            pltpu.VMEM((tokens, wide), f32),
            pltpu.VMEM((4, 8, 128), f32),
            pltpu.VMEM((3, 8, 128), f32),
            dma((8,)),
            dma((8,)),
            dma,
            dma,
            dma((8,)),
            dma((8,)),
            dma((8,)),
            dma((8,)),
            dma((6,)),
            dma((4, 2)),
            dma,
            dma,
            dma((4,)),
            dma((4, 2)),
            dma((4,)),
            dma((4, 4)),
            dma((4, 4)),
            dma((6,)),
            dma((2,)),
            dma((2, 2)),
            dma((3,)),
            dma((3,)),
        ],
        compiler_params=pltpu.CompilerParams(collective_id=1, has_side_effects=True),
        name="layer",
    )(q, cosines, sines, fresh, allowed, hide, pages, residual, gain, weights)


def on_device(
    queries,
    suffix_key_value,
    residual,
    gain,
    gate_up,
    prefix_cache_slots,
    prefix_page_slots,
    lengths,
    counts,
):
    blocks = lax.axis_size("blk")
    column = lax.axis_index("blk")
    group_index = lax.axis_index("req")
    group_len = queries.shape[0]
    heads_kv = suffix_key_value.shape[1]
    head_dim = suffix_key_value.shape[2] // 2
    page_len = prefix_cache_slots.shape[1]
    kv_head = column * heads_kv // blocks
    page_count = counts[group_index]
    request, offset, positions = suffix_layout(
        lengths[group_index], page_count, group_len, page_len
    )
    cosines, sines = rope_tables(positions, head_dim // 2)
    own_head = lax.dynamic_index_in_dim(suffix_key_value, kv_head, 1, keepdims=False)
    keys_new = rotate(own_head[:, :head_dim].astype(jnp.float32), cosines, sines).astype(
        jnp.bfloat16
    )
    values_new = own_head[:, head_dim:]
    both_new = jnp.concatenate([keys_new, values_new], 1)
    lane_width = 2 * heads_kv * head_dim // blocks
    updated_cache = lax.dynamic_slice_in_dim(
        both_new, column * lane_width % (2 * head_dim), lane_width, 1
    )
    allowed = (request[:, None] == request[None, :]) & (offset[:, None] <= offset[None, :])
    own_slots = lax.dynamic_index_in_dim(prefix_cache_slots, kv_head, 2, keepdims=False)
    pages = own_slots.reshape(own_slots.shape[0] * page_len, 2 * head_dim)
    chip_pages = 2 * own_slots.shape[0]
    slot_ids = (group_index // 2) * chip_pages + jnp.arange(chip_pages, dtype=jnp.int32)
    match = prefix_page_slots[None, :] == slot_ids[:, None]
    page_ids = jnp.arange(prefix_page_slots.shape[0], dtype=jnp.int32)
    page_of = jnp.sum(jnp.where(match, page_ids[None, :], 0), 1)
    dy, dz = group_at(jnp.arange(8, dtype=jnp.int32))
    source = (
        ((group_index // 4 + 4 - dy) % 4) * 4
        + ((group_index // 2 + dz) % 2) * 2
        + group_index % 2
    )
    group_ids = jnp.arange(counts.shape[0], dtype=jnp.int32)
    seen = jnp.sum(jnp.where(source[:, None] == group_ids[None, :], counts[None, :], 0), 1)
    hide = jnp.where(page_of[:, None] < seen[None, :], 0.0, NEGATIVE).astype(jnp.float32)
    hidden = layer(
        queries,
        jnp.concatenate([cosines, cosines], 1),
        jnp.concatenate([-sines, sines], 1),
        both_new,
        allowed.astype(jnp.float32),
        hide,
        pages,
        residual,
        gain[None, :],
        gate_up.reshape(gate_up.shape[0], 2 * gate_up.shape[2]),
    )
    return (hidden, updated_cache)


def solution(mesh):
    placed = (
        P("req", "blk"),
        P("req", None, None),
        P("req", "blk"),
        P("blk"),
        P("blk", None, "req"),
        P("req", None, None, None),
        P(),
        P(),
        P(),
    )
    return jax.shard_map(
        on_device,
        mesh=mesh,
        in_specs=placed,
        out_specs=(P("blk", "req"), P("req", "blk")),
        check_vma=False,
    )
```

```python
import math

import jax
import jax.numpy as jnp
from jax import lax
from jax.experimental import pallas as pl
from jax.experimental.pallas import tpu as pltpu
from jax.sharding import PartitionSpec as P

D = 8192

MESH = pl.DeviceIdType.MESH

NEGATIVE = -1e30
EPSILON = 1e-05
ROPE_BASE = 500000.0


def rope_tables(positions, half_dim):
    inverse = jnp.exp(
        -math.log(ROPE_BASE) * jnp.arange(half_dim, dtype=jnp.float32) * 2.0 / (2 * half_dim)
    )
    angles = positions.astype(jnp.float32)[:, None] * inverse[None, :]
    return (jnp.cos(angles), jnp.sin(angles))


def rotate(vectors, cosines, sines):
    half_dim = vectors.shape[-1] // 2
    lower = vectors[..., :half_dim]
    upper = vectors[..., half_dim:]
    return jnp.concatenate([lower * cosines - upper * sines, upper * cosines + lower * sines], -1)


def suffix_layout(lengths_row, page_count, group_len, page_len):
    starts = jnp.cumsum(lengths_row) - lengths_row
    tokens_at = jnp.arange(group_len, dtype=jnp.int32)
    request = jnp.sum((tokens_at[:, None] >= starts[None, :]).astype(jnp.int32), 1) - 1
    slots_req = jnp.arange(lengths_row.shape[0], dtype=jnp.int32)
    request_begin = jnp.sum(
        jnp.where(request[:, None] == slots_req[None, :], starts[None, :], 0), 1
    )
    offset = tokens_at - request_begin
    return (request, offset, page_count * page_len + offset)


def remote(src, dst, send_sem, recv_sem, req, blk):
    return pltpu.make_async_remote_copy(
        src_ref=src,
        dst_ref=dst,
        send_sem=send_sem,
        recv_sem=recv_sem,
        device_id=(req, blk),
        device_id_type=MESH,
    )


def place():
    req, blk = lax.axis_index("req"), lax.axis_index("blk")
    y, zl, core = req // 4, (req // 2) % 2, req % 2
    return req, blk, y, zl, core, blk // 4, blk % 4


def weight_pieces(w_ref, w_all, chunk):
    half = w_ref.shape[0] // 2

    def own(part):
        return w_ref.at[pl.ds(part * half, half), chunk]

    def slot(source, part):
        return w_all.at[source, pl.ds(part * half, half), chunk]

    return own, slot


def weight_sends(w_ref, w_all, send, recv, q, chunk):
    req, blk, y, zl, core, zh, x = place()
    own, slot = weight_pieces(w_ref, w_all, chunk)
    return [
        remote(
            own(part),
            slot(x, part),
            send.at[j, q],
            recv.at[x, part, q],
            req,
            zh * 4 + (x + 4 + step) % 4,
        )
        for j, (step, part) in enumerate(((1, 0), (-1, 1), (1, 1), (-1, 0)))
    ]


def weight_relays(w_ref, w_all, send, recv, q, chunk):
    req, blk, y, zl, core, zh, x = place()
    own, slot = weight_pieces(w_ref, w_all, chunk)
    out = []
    for j, (step, part) in enumerate(((1, 0), (-1, 1))):
        source = (x + 4 - step) % 4
        piece = slot(source, part)
        to_blk = zh * 4 + (x + 4 + step) % 4
        out.append(remote(piece, piece, send.at[4 + j, q], recv.at[source, part, q], req, to_blk))
    return out


def weight_wait(w_ref, w_all, send, recv, q, chunk, source, part):
    req, blk, y, zl, core, zh, x = place()
    piece = weight_pieces(w_ref, w_all, chunk)[1](source, part)
    to_blk = zh * 4 + (x + 1) % 4
    remote(piece, piece, send.at[0, q], recv.at[source, part, q], req, to_blk).wait_recv()


def spread_features(u_ref, a_all, x_send, z_send, y_send, on_send, core_send, recv):
    req, blk, y, zl, core, zh, x = place()
    target = zl * 2 + core
    home = core == x % 2
    root = x == target
    over_z = y * 4 + (1 - zl) * 2 + core
    sibling = y * 4 + zl * 2 + (1 - core)
    up, down = (y + 1) % 4, (y + 3) % 4
    far = (y + 2) % 4
    req_up, req_down = up * 4 + zl * 2 + core, down * 4 + zl * 2 + core

    def block_copy(yy, xx, send, to_req, to_blk):
        piece = a_all.at[yy, xx]
        return remote(piece, piece, send, recv.at[yy, xx], to_req, to_blk)

    hop = remote(u_ref, a_all.at[y, x], x_send, recv.at[y, x], req, zh * 4 + target)
    keep = pltpu.make_async_copy(u_ref, a_all.at[y, x], recv.at[y, x])

    @pl.when(root)
    def _():
        keep.start()

    @pl.when(jnp.logical_not(root))
    def _():
        hop.start()

    def to_core(yy, xx):
        return block_copy(yy, xx, core_send.at[yy, xx], sibling, blk)

    def to_z(xx):
        return block_copy(y, xx, z_send.at[xx], over_z, blk)

    def to_y(xx, way):
        return block_copy(y, xx, y_send.at[xx, way], (req_up, req_down)[way], blk)

    def onward(xx, way):
        return block_copy((down, up)[way], xx, on_send.at[xx], (req_up, req_down)[way], blk)

    def arrived(yy, xx):
        block_copy(yy, xx, x_send, over_z, blk).wait_recv()

    @pl.when(home)
    def _():
        def own(xx, carry):
            @pl.when(root & (xx == x))
            def _():
                keep.wait()

            @pl.when(jnp.logical_not(root & (xx == x)))
            def _():
                arrived(y, xx)

            @pl.when(root)
            def _():
                to_z(xx).start()

            to_y(xx, 0).start()
            to_y(xx, 1).start()
            to_core(y, xx).start()
            return carry

        lax.fori_loop(0, 4, own, 0)

        def near(xx, carry):
            arrived(down, xx)

            @pl.when(xx < 2)
            def _():
                onward(xx, 0).start()

            to_core(down, xx).start()
            arrived(up, xx)

            @pl.when(xx >= 2)
            def _():
                onward(xx, 1).start()

            to_core(up, xx).start()
            return carry

        lax.fori_loop(0, 4, near, 0)

        def last(xx, carry):
            arrived(far, xx)
            to_core(far, xx).start()
            return carry

        lax.fori_loop(0, 4, last, 0)

    @pl.when(jnp.logical_not(home))
    def _():
        def take(i, carry):
            arrived(i // 4, i % 4)
            return carry

        lax.fori_loop(0, 16, take, 0)

    def drain():
        @pl.when(jnp.logical_not(root))
        def _():
            hop.wait_send()

        @pl.when(home)
        def _():
            def step(xx, carry):
                @pl.when(root)
                def _():
                    to_z(xx).wait_send()

                to_y(xx, 0).wait_send()
                to_y(xx, 1).wait_send()

                @pl.when(xx < 2)
                def _():
                    onward(xx, 0).wait_send()

                @pl.when(xx >= 2)
                def _():
                    onward(xx, 1).wait_send()

                return carry

            lax.fori_loop(0, 4, step, 0)

            def core_step(i, carry):
                to_core(i // 4, i % 4).wait_send()
                return carry

            lax.fori_loop(0, 16, core_step, 0)

    return drain


def group_at(j):
    return j + j // 2 - 2 * (j // 3)


def layer_kernel(
    q_ref,
    cos_ref,
    sin_ref,
    fresh_ref,
    allowed_ref,
    hide_ref,
    pages_ref,
    residual_ref,
    gain_ref,
    w_ref,
    hidden_ref,
    q_all,
    kv_all,
    values_t,
    scores,
    probs,
    part_out,
    stat_out,
    part_in,
    stat_in,
    held_part,
    held_stat,
    u_ref,
    w_all,
    a_all,
    product,
    relay,
    final,
    own_sum,
    square_out,
    square_in,
    query_send,
    query_recv,
    page_send,
    page_recv,
    part_send,
    part_recv,
    stat_send,
    stat_recv,
    w_send,
    w_recv,
    w_local,
    x_send,
    z_send,
    y_send,
    on_send,
    core_send,
    a_recv,
    r_send,
    relay_recv,
    final_recv,
    q_send,
    q_recv,
):
    req, blk, y, zl, core, zh, x = place()
    tokens, features = q_ref.shape
    heads = features // 128
    keys_here = pages_ref.shape[0]
    rows_all = heads * tokens
    width = hidden_ref.shape[1]
    tiles = 2 * width // 256
    sibling = y * 4 + zl * 2 + (1 - core)
    blk_up, blk_far, blk_down = [((zh + i) % 4) * 4 + x for i in (1, 2, 3)]
    turn = (1.0 / math.sqrt(128)) * math.log2(math.e)

    chunks_w = (pl.ds(0, 1024), pl.ds(1024, 2 * width - 1024))
    tiles_w = ((0, 4), (4, tiles))
    over_z = y * 4 + (1 - zl) * 2 + core

    def ahead(j):
        return ((y + group_at(j)) % 4) * 4 + zl * 2 + core

    def behind(j):
        return ((y + 4 - group_at(j)) % 4) * 4 + zl * 2 + core

    barrier = pltpu.get_barrier_semaphore()
    peers = [(req, zh * 4 + (x + i) % 4) for i in (1, 2, 3)]
    peers += [(sibling, blk), (req, blk_up), (req, blk_far), (req, blk_down)]
    peers += [(over_z, blk)] + [(ahead(j), blk) for j in range(1, 4)]
    for peer in peers:
        pl.semaphore_signal(barrier, inc=1, device_id=peer, device_id_type=MESH)

    cosines, sines = cos_ref[...], sin_ref[...]
    for h in range(heads):
        vector = q_ref[:, h * 128 : (h + 1) * 128].astype(jnp.float32)
        turned = vector * cosines + pltpu.roll(vector, 64, 1) * sines
        q_all[0, h * tokens : (h + 1) * tokens, :] = turned.astype(jnp.bfloat16)
    pl.semaphore_wait(barrier, len(peers))

    def part_of(r):
        return ((zl + r // 2) % 2) * 2 + (core + r % 2) % 2

    def page_piece(r, send, to_req):
        piece = kv_all.at[part_of(r)]
        return remote(piece, piece, page_send.at[send], page_recv.at[part_of(r)], to_req, blk)

    own_pages = kv_all.at[part_of(0)]
    page_copies = [
        remote(pages_ref, own_pages, page_send.at[i], page_recv.at[part_of(0)], to_req, blk)
        for i, to_req in enumerate((sibling, over_z))
    ]
    page_on = page_piece(2, 2, sibling)
    query_copies = [
        remote(q_all.at[0], q_all.at[j], query_send.at[j], query_recv.at[j], ahead(j), blk)
        for j in range(1, 4)
    ]
    for copy in query_copies + page_copies:
        copy.start()
    sends = []
    for q in range(2):
        sends += weight_sends(w_ref, w_all, w_send, w_recv, q, chunks_w[q])
    for copy in sends:
        copy.start()
    local = pltpu.make_async_copy(w_ref, w_all.at[x], w_local)
    local.start()
    kv_all[part_of(0)] = pages_ref[...]

    def fold(block, op):
        parts = [block[i * 8 : (i + 1) * 8] for i in range(block.shape[0] // 8)]
        while len(parts) > 1:
            parts = [op(a, b) for a, b in zip(parts[::2], parts[1::2])]
        return parts[0]

    def last_fold(rows, op):
        return op(rows, 0, keepdims=True)

    fresh_t = jnp.transpose(fresh_ref[:, 128:256].astype(jnp.float32)).astype(jnp.bfloat16)
    raw = lax.dot_general(
        fresh_ref[:, 0:128],
        q_all[0],
        (((1,), (1,)), ((), ())),
        preferred_element_type=jnp.float32,
    )
    mask = jnp.concatenate([allowed_ref[...]] * heads, 1)
    raw = jnp.where(mask > 0, raw, NEGATIVE)
    suffix_max = last_fold(fold(raw, jnp.maximum), jnp.max)
    suffix_probs = jnp.exp2((raw - suffix_max) * turn)
    suffix_sum = last_fold(fold(suffix_probs, jnp.add), jnp.sum)
    suffix_part = jnp.dot(
        fresh_t, suffix_probs.astype(jnp.bfloat16), preferred_element_type=jnp.float32
    )

    def turn_values(r):
        for p in range(keys_here // 128):
            block = kv_all[part_of(r), p * 128 : (p + 1) * 128, 128:256].astype(jnp.float32)
            start = r * keys_here + p * 128
            values_t[:, start : start + 128] = jnp.transpose(block).astype(jnp.bfloat16)

    turn_values(0)
    page_piece(1, 2, sibling).wait_recv()
    turn_values(1)

    chunk = 512
    chunks = 2 * keys_here // chunk
    per_core = keys_here // chunk
    pages_per_core = keys_here // 128

    def score_chunk(c, j, a, slot, top):
        part = part_of(2 * a + c // per_core)
        inside = c % per_core
        keys = kv_all[part, inside * chunk : (inside + 1) * chunk, 0:128]
        raw = lax.dot_general(
            keys, q_all[j], (((1,), (1,)), ((), ())), preferred_element_type=jnp.float32
        )
        scores[slot, c * chunk : (c + 1) * chunk, :] = raw
        for p in range(chunk // 128):
            page = part * pages_per_core + inside * (chunk // 128) + p
            folded = fold(raw[p * 128 : (p + 1) * 128], jnp.maximum)
            top = jnp.maximum(top, folded + hide_ref[page, j])
        return top

    def weigh_chunk(c, j, a, slot, top, total, weighted):
        part = part_of(2 * a + c // per_core)
        for p in range(chunk // 128):
            page = part * pages_per_core + (c % per_core) * (chunk // 128) + p
            rows = slice(c * chunk + p * 128, c * chunk + (p + 1) * 128)
            level = top - 4.0 * hide_ref[page, j]
            weights = jnp.exp2((scores[slot, rows, :] - level) * turn)
            total = total + fold(weights, jnp.add)
            probs[rows, :] = weights.astype(jnp.bfloat16)
        columns = pl.ds(pl.multiple_of(a * 2 * keys_here + c * chunk, chunk), chunk)
        product_here = jnp.dot(
            values_t[:, columns],
            probs[c * chunk : (c + 1) * chunk, :],
            preferred_element_type=jnp.float32,
        )
        return total, product_here if weighted is None else weighted + product_here

    first_row = lax.broadcasted_iota(jnp.int32, (8, rows_all), 0) == 0

    def merge(j, top, total, weighted):
        other_top, other_sum = held_stat[j, 0:1, :], held_stat[j, 1:2, :]
        joint = jnp.maximum(top, other_top)
        here, there = jnp.exp2((top - joint) * turn), jnp.exp2((other_top - joint) * turn)
        return joint, total * here + other_sum * there, weighted * here + held_part[j] * there

    def part_copies(j):
        return (
            remote(
                part_out.at[j], part_in.at[j], part_send.at[j], part_recv.at[j], behind(j), blk
            ),
            remote(
                stat_out.at[j], stat_in.at[j], stat_send.at[j], stat_recv.at[j], behind(j), blk
            ),
        )

    def unit(u):
        v = u - 4
        later = jnp.where(v == 0, 3, jnp.where(v == 3, 0, v))
        return jnp.where(u < 4, u, later), jnp.where(u < 4, 0, 1)

    low = jnp.full((8, rows_all), NEGATIVE, jnp.float32)
    zero = jnp.zeros((8, rows_all), jnp.float32)
    top = low
    for c in range(chunks):
        top = score_chunk(c, 0, 0, 0, top)
    first_top = last_fold(top, jnp.max)

    def unit_step(u, done_top):
        j, a = unit(u)
        before, before_half = unit(u - 1)

        @pl.when(u < 4)
        def _():
            remote(
                q_all.at[0], q_all.at[j], query_send.at[1], query_recv.at[j], ahead(1), blk
            ).wait_recv()

        @pl.when(u == 3)
        def _():
            page_piece(2, 2, over_z).wait_recv()
            page_on.start()
            turn_values(2)

        @pl.when(u == 4)
        def _():
            page_piece(3, 2, sibling).wait_recv()
            turn_values(3)

        top, total, weighted = low, zero, None
        for c in range(chunks):
            top = score_chunk(c, j, a, u % 2, top)
            total, weighted = weigh_chunk(
                c, before, before_half, (u - 1) % 2, done_top, total, weighted
            )
        total = last_fold(total, jnp.sum)

        @pl.when(u <= 4)
        def _():
            held_part[before] = weighted
            held_stat[before] = jnp.where(first_row, done_top, total)

        @pl.when(u > 4)
        def _():
            joint, joint_sum, joint_part = merge(before, done_top, total, weighted)
            part_out[before] = joint_part.astype(jnp.bfloat16)
            stat_out[before] = jnp.where(first_row, joint, joint_sum)
            for copy in part_copies(before):
                copy.start()

        return last_fold(top, jnp.max)

    last_top = lax.fori_loop(1, 8, unit_step, first_top)

    relays = []

    def relay_chunk(q):
        copies = weight_relays(w_ref, w_all, w_send, w_recv, q, chunks_w[q])
        for (step, part), copy in zip(((1, 0), (-1, 1)), copies):
            source = (x + 4 - step) % 4
            weight_wait(w_ref, w_all, w_send, w_recv, q, chunks_w[q], source, part)
            copy.start()
        relays.extend(copies)

    relay_chunk(0)
    total, weighted = zero, None
    for c in range(chunks):
        total, weighted = weigh_chunk(c, 0, 1, 1, last_top, total, weighted)
    own_top, own_total, own_part = merge(0, last_top, last_fold(total, jnp.sum), weighted)

    order = (1, 2, 3)
    for j in order:
        part_copies(j)[1].wait_recv()
    tops = [stat_in[j, 0:1, :] for j in order]
    sums = [stat_in[j, 1:2, :] for j in order]
    joint = jnp.maximum(suffix_max, own_top)
    for row in tops:
        joint = jnp.maximum(joint, row)
    factor, own_factor = (jnp.exp2((row - joint) * turn) for row in (suffix_max, own_top))
    joint_sum = suffix_sum * factor + own_total * own_factor
    attended = suffix_part * factor + own_part * own_factor
    for j, row, row_sum in zip(order, tops, sums):
        factor = jnp.exp2((row - joint) * turn)
        joint_sum = joint_sum + row_sum * factor
        part_copies(j)[0].wait_recv()
        attended = attended + part_in[j].astype(jnp.float32) * factor
    attended = attended / joint_sum

    squares_here = jnp.zeros((tokens, 128), jnp.float32)
    for h in range(heads):
        cols = slice(h * 128, (h + 1) * 128)
        own = jnp.transpose(attended[:, h * tokens : (h + 1) * tokens])
        stream = (residual_ref[:, cols].astype(jnp.float32) + own).astype(jnp.bfloat16)
        stream = stream.astype(jnp.float32)
        squares_here = squares_here + stream * stream
        u_ref[0:tokens, cols] = (stream * gain_ref[:, cols]).astype(jnp.bfloat16)
    square_row = jnp.sum(jnp.transpose(squares_here), 0, keepdims=True)
    high = square_row.astype(jnp.bfloat16)
    below = (square_row - high.astype(jnp.float32)).astype(jnp.bfloat16)
    u_ref[tokens : tokens + 16, 0:128] = jnp.broadcast_to(high, (16, 128))
    u_ref[tokens : tokens + 16, 128:256] = jnp.broadcast_to(below, (16, 128))
    u_ref[tokens : tokens + 16, 256:features] = jnp.zeros((16, features - 256), jnp.bfloat16)

    relay_chunk(1)
    drain = spread_features(u_ref, a_all, x_send, z_send, y_send, on_send, core_send, a_recv)

    def squares(zt, carry):
        total = jnp.zeros((8, 128), jnp.float32)
        for xx in range(4):
            rows = a_all[zt, xx, tokens : tokens + 16, 0:256].astype(jnp.float32)
            total = total + rows[0:8, 0:128] + rows[0:8, 128:256]
        square_out[zt] = total
        return carry

    lax.fori_loop(0, 4, squares, 0)
    square_copies = []
    for i in (1, 2, 3):
        there = (zh + i) % 4
        square_copies.append(
            remote(
                square_out.at[there],
                square_in.at[i - 1],
                q_send.at[i - 1],
                q_recv.at[i - 1],
                req,
                there * 4 + x,
            )
        )
    for copy in square_copies:
        copy.start()

    def multiply(zt, target, q):
        def tile(n, carry):
            cols = pl.ds(pl.multiple_of(n * 256, 256), 256)
            total = jnp.dot(
                a_all[zt, 0, 0:tokens, :], w_all[0, :, cols], preferred_element_type=jnp.float32
            )
            for xx in range(1, 4):
                total = total + jnp.dot(
                    a_all[zt, xx, 0:tokens, :],
                    w_all[xx, :, cols],
                    preferred_element_type=jnp.float32,
                )
            target[:, cols] = total.astype(target.dtype)
            return carry

        lax.fori_loop(*tiles_w[q], tile, 0)

    half = tokens // 2
    top_rows, bottom_rows = pl.ds(0, half), pl.ds(half, half)

    def exchange(q):
        cols = chunks_w[q]

        def piece(i, slot, rows, target, recv, to_blk):
            source = product.at[slot, rows, cols]
            return remote(source, target, r_send.at[i, q], recv, req, to_blk)

        def landing(side, rows):
            return final.at[side, rows, cols]

        return (
            piece(0, 0, top_rows, relay.at[0, :, cols], relay_recv.at[0, q], blk_up),
            piece(1, 0, bottom_rows, relay.at[1, :, cols], relay_recv.at[1, q], blk_down),
            piece(2, 1, bottom_rows, landing(0, bottom_rows), final_recv.at[0, 1, q], blk_up),
            piece(3, 2, top_rows, landing(1, top_rows), final_recv.at[1, 0, q], blk_down),
            piece(4, 1, top_rows, landing(0, top_rows), final_recv.at[0, 0, q], blk_up),
            piece(5, 2, bottom_rows, landing(1, bottom_rows), final_recv.at[1, 1, q], blk_down),
        )

    exchanges = [exchange(0), exchange(1)]

    def wait_weights(q):
        for step, part in ((3, 0), (3, 1), (1, 0), (1, 1), (2, 0), (2, 1)):
            if (step, part) not in ((3, 0), (1, 1)):
                source = (x + step) % 4
                weight_wait(w_ref, w_all, w_send, w_recv, q, chunks_w[q], source, part)

    def add_relay(slot, rows, index, q):
        def tile(n, carry):
            cols = pl.ds(pl.multiple_of(n * 256, 256), 256)
            total = product[slot, rows, cols].astype(jnp.float32) + relay[index, :, cols].astype(
                jnp.float32
            )
            product[slot, rows, cols] = total.astype(jnp.bfloat16)
            return carry

        lax.fori_loop(*tiles_w[q], tile, 0)

    def send_far(q):
        wait_weights(q)
        multiply((zh + 2) % 4, product.at[0], q)
        exchanges[q][0].start()
        exchanges[q][1].start()

    def send_near(q):
        multiply((zh + 1) % 4, product.at[1], q)
        exchanges[q][2].start()
        multiply((zh + 3) % 4, product.at[2], q)
        exchanges[q][3].start()

    def send_sums(q):
        exchanges[q][0].wait_recv()
        add_relay(1, top_rows, 0, q)
        exchanges[q][4].start()
        exchanges[q][1].wait_recv()
        add_relay(2, bottom_rows, 1, q)
        exchanges[q][5].start()

    local.wait()
    send_far(0)
    send_near(0)
    send_far(1)
    send_sums(0)
    send_near(1)
    send_sums(1)
    multiply(zh, own_sum, 0)
    multiply(zh, own_sum, 1)

    for copy in square_copies:
        copy.wait_recv()
    row = square_out[zh] + square_in[0] + square_in[1] + square_in[2]
    spread = jnp.broadcast_to(row[0:1, :], (tokens, tokens))
    diagonal = lax.broadcasted_iota(jnp.int32, (tokens, tokens), 0) == lax.broadcasted_iota(
        jnp.int32, (tokens, tokens), 1
    )
    square_sum = jnp.sum(jnp.where(diagonal, spread, 0.0), 1, keepdims=True)
    scale = jnp.broadcast_to(lax.rsqrt(square_sum / D + EPSILON), (tokens, 128))

    def finish(n, carry):
        def column_sum(start):
            cols = pl.ds(pl.multiple_of(start, 128), 128)
            total = own_sum[:, cols] + final[0, :, cols].astype(jnp.float32)
            return (total + final[1, :, cols].astype(jnp.float32)) * scale

        gate, up = column_sum(n * 256), column_sum(n * 256 + 128)
        value = gate / (1.0 + jnp.exp(-gate)) * up
        hidden_ref[:, pl.ds(pl.multiple_of(n * 128, 128), 128)] = value.astype(jnp.bfloat16)
        return carry

    for q in range(2):
        for copy in exchanges[q][2:]:
            copy.wait_recv()
        lax.fori_loop(*tiles_w[q], finish, 0)

    for copy in sends + relays + square_copies:
        copy.wait_send()
    for q in range(2):
        for copy in exchanges[q]:
            copy.wait_send()
    drain()
    for copy in query_copies + page_copies + [page_on]:
        copy.wait_send()
    for j in order:
        for copy in part_copies(j):
            copy.wait_send()


def layer(q, cosines, sines, fresh, allowed, hide, pages, residual, gain, weights):
    depth, wide = weights.shape
    tokens, features = q.shape
    rows_all = tokens * features // 128
    keys = 2 * pages.shape[0]
    groups = 4
    dma = pltpu.SemaphoreType.DMA
    bf16, f32 = jnp.bfloat16, jnp.float32
    vmem = pl.BlockSpec(memory_space=pltpu.VMEM)
    return pl.pallas_call(
        layer_kernel,
        out_shape=jax.ShapeDtypeStruct((tokens, wide // 2), bf16),
        in_specs=[vmem] * 5
        + [pl.BlockSpec(memory_space=pltpu.SMEM)]
        + [vmem] * 3
        + [pl.BlockSpec(memory_space=pl.ANY)],
        out_specs=vmem,
        scratch_shapes=[
            pltpu.VMEM((groups, rows_all, 128), bf16),
            pltpu.VMEM((4,) + pages.shape, bf16),
            pltpu.VMEM((128, 2 * keys), bf16),
            pltpu.VMEM((2, keys, rows_all), f32),
            pltpu.VMEM((keys, rows_all), bf16),
            pltpu.VMEM((groups, 128, rows_all), bf16),
            pltpu.VMEM((groups, 8, rows_all), f32),
            pltpu.VMEM((groups, 128, rows_all), bf16),
            pltpu.VMEM((groups, 8, rows_all), f32),
            pltpu.VMEM((groups, 128, rows_all), f32),
            pltpu.VMEM((groups, 8, rows_all), f32),
            pltpu.VMEM((tokens + 16, features), bf16),
            pltpu.VMEM((4, depth, wide), bf16),
            pltpu.VMEM((4, 4, tokens + 16, features), bf16),
            pltpu.VMEM((3, tokens, wide), bf16),
            pltpu.VMEM((2, tokens // 2, wide), bf16),
            pltpu.VMEM((2, tokens, wide), bf16),
            pltpu.VMEM((tokens, wide), f32),
            pltpu.VMEM((4, 8, 128), f32),
            pltpu.VMEM((3, 8, 128), f32),
            dma((groups,)),
            dma((groups,)),
            dma((3,)),
            dma((4,)),
            dma((groups,)),
            dma((groups,)),
            dma((groups,)),
            dma((groups,)),
            dma((6, 2)),
            dma((4, 2, 2)),
            dma,
            dma,
            dma((4,)),
            dma((4, 2)),
            dma((4,)),
            dma((4, 4)),
            dma((4, 4)),
            dma((6, 2)),
            dma((2, 2)),
            dma((2, 2, 2)),
            dma((3,)),
            dma((3,)),
        ],
        compiler_params=pltpu.CompilerParams(collective_id=1, has_side_effects=True),
        name="layer",
    )(q, cosines, sines, fresh, allowed, hide, pages, residual, gain, weights)


def on_device(
    queries,
    suffix_key_value,
    residual,
    gain,
    gate_up,
    prefix_cache_slots,
    prefix_page_slots,
    lengths,
    counts,
):
    blocks = lax.axis_size("blk")
    column = lax.axis_index("blk")
    group_index = lax.axis_index("req")
    group_len = queries.shape[0]
    heads_kv = suffix_key_value.shape[1]
    head_dim = suffix_key_value.shape[2] // 2
    page_len = prefix_cache_slots.shape[1]
    kv_head = column * heads_kv // blocks
    page_count = counts[group_index]
    request, offset, positions = suffix_layout(
        lengths[group_index], page_count, group_len, page_len
    )
    cosines, sines = rope_tables(positions, head_dim // 2)
    own_head = lax.dynamic_index_in_dim(suffix_key_value, kv_head, 1, keepdims=False)
    keys_new = rotate(own_head[:, :head_dim].astype(jnp.float32), cosines, sines).astype(
        jnp.bfloat16
    )
    values_new = own_head[:, head_dim:]
    both_new = jnp.concatenate([keys_new, values_new], 1)
    lane_width = 2 * heads_kv * head_dim // blocks
    updated_cache = lax.dynamic_slice_in_dim(
        both_new, column * lane_width % (2 * head_dim), lane_width, 1
    )
    allowed = (request[:, None] == request[None, :]) & (offset[:, None] <= offset[None, :])
    own_slots = lax.dynamic_index_in_dim(prefix_cache_slots, kv_head, 2, keepdims=False)
    pages = own_slots.reshape(own_slots.shape[0] * page_len, 2 * head_dim)
    near_pages = 4 * own_slots.shape[0]
    slot_ids = (group_index // 4) * near_pages + jnp.arange(near_pages, dtype=jnp.int32)
    match = prefix_page_slots[None, :] == slot_ids[:, None]
    page_ids = jnp.arange(prefix_page_slots.shape[0], dtype=jnp.int32)
    page_of = jnp.sum(jnp.where(match, page_ids[None, :], 0), 1)
    dy = group_at(jnp.arange(4, dtype=jnp.int32))
    source = ((group_index // 4 + 4 - dy) % 4) * 4 + group_index % 4
    group_ids = jnp.arange(counts.shape[0], dtype=jnp.int32)
    seen = jnp.sum(jnp.where(source[:, None] == group_ids[None, :], counts[None, :], 0), 1)
    hide = jnp.where(page_of[:, None] < seen[None, :], 0.0, NEGATIVE).astype(jnp.float32)
    depth, _, width = gate_up.shape
    weights = gate_up.reshape(depth, 2, width // 128, 128).transpose(0, 2, 1, 3)
    weights = weights.reshape(depth, 2 * width)
    hidden = layer(
        queries,
        jnp.concatenate([cosines, cosines], 1),
        jnp.concatenate([-sines, sines], 1),
        both_new,
        allowed.astype(jnp.float32),
        hide,
        pages,
        residual,
        gain[None, :],
        weights,
    )
    return (hidden, updated_cache)


def solution(mesh):
    placed = (
        P("req", "blk"),
        P("req", None, None),
        P("req", "blk"),
        P("blk"),
        P("blk", None, "req"),
        P("req", None, None, None),
        P(),
        P(),
        P(),
    )
    return jax.shard_map(
        on_device,
        mesh=mesh,
        in_specs=placed,
        out_specs=(P("blk", "req"), P("req", "blk")),
        check_vma=False,
    )
```

```python
import math

import jax
import jax.numpy as jnp
from jax import lax
from jax.experimental import pallas as pl
from jax.experimental.pallas import tpu as pltpu
from jax.sharding import PartitionSpec as P
import numpy as np

D = 8192

MESH = pl.DeviceIdType.MESH

NEGATIVE = -1e30
EPSILON = 1e-05
ROPE_BASE = 500000.0


def inverse_frequencies(half_dim):
    exponent = np.float32(-math.log(ROPE_BASE)) * np.arange(half_dim, dtype=np.float32)
    exponent = exponent * np.float32(2.0) / np.float32(2 * half_dim)
    inverse = np.exp(exponent.astype(np.float64)).astype(np.float32)
    return np.concatenate([inverse, inverse])[None, :]


def remote(src, dst, send_sem, recv_sem, req, blk):
    return pltpu.make_async_remote_copy(
        src_ref=src,
        dst_ref=dst,
        send_sem=send_sem,
        recv_sem=recv_sem,
        device_id=(req, blk),
        device_id_type=MESH,
    )


def place():
    req, blk = lax.axis_index("req"), lax.axis_index("blk")
    y, zl, core = req // 4, (req // 2) % 2, req % 2
    return req, blk, y, zl, core, blk // 4, blk % 4


def weight_pieces(w_ref, w_all, chunk):
    half = w_ref.shape[0] // 2

    def own(part):
        return w_ref.at[pl.ds(part * half, half), chunk]

    def slot(source, part):
        return w_all.at[source, pl.ds(part * half, half), chunk]

    return own, slot


def weight_sends(w_ref, w_all, send, recv, q, chunk):
    req, blk, y, zl, core, zh, x = place()
    own, slot = weight_pieces(w_ref, w_all, chunk)
    return [
        remote(
            own(part),
            slot(x, part),
            send.at[j, q],
            recv.at[x, part, q],
            req,
            zh * 4 + (x + 4 + step) % 4,
        )
        for j, (step, part) in enumerate(((1, 0), (-1, 1), (1, 1), (-1, 0)))
    ]


def weight_relays(w_ref, w_all, send, recv, q, chunk):
    req, blk, y, zl, core, zh, x = place()
    own, slot = weight_pieces(w_ref, w_all, chunk)
    out = []
    for j, (step, part) in enumerate(((1, 0), (-1, 1))):
        source = (x + 4 - step) % 4
        piece = slot(source, part)
        to_blk = zh * 4 + (x + 4 + step) % 4
        out.append(remote(piece, piece, send.at[4 + j, q], recv.at[source, part, q], req, to_blk))
    return out


def weight_wait(w_ref, w_all, send, recv, q, chunk, source, part):
    req, blk, y, zl, core, zh, x = place()
    piece = weight_pieces(w_ref, w_all, chunk)[1](source, part)
    to_blk = zh * 4 + (x + 1) % 4
    remote(piece, piece, send.at[0, q], recv.at[source, part, q], req, to_blk).wait_recv()


def spread_features(
    u_ref, a_all, x_send, z_send, y_send, on_send, core_send, recv, after_hop
):
    req, blk, y, zl, core, zh, x = place()
    target = zl * 2 + core
    home = core == x % 2
    root = x == target
    over_z = y * 4 + (1 - zl) * 2 + core
    sibling = y * 4 + zl * 2 + (1 - core)
    up, down = (y + 1) % 4, (y + 3) % 4
    far = (y + 2) % 4
    req_up, req_down = up * 4 + zl * 2 + core, down * 4 + zl * 2 + core

    def block_copy(yy, xx, send, to_req, to_blk):
        piece = a_all.at[yy, xx]
        return remote(piece, piece, send, recv.at[yy, xx], to_req, to_blk)

    hop = remote(u_ref, a_all.at[y, x], x_send, recv.at[y, x], req, zh * 4 + target)
    keep = pltpu.make_async_copy(u_ref, a_all.at[y, x], recv.at[y, x])

    @pl.when(root)
    def _():
        keep.start()

    @pl.when(jnp.logical_not(root))
    def _():
        hop.start()

    after_hop()

    def to_core(yy, xx):
        return block_copy(yy, xx, core_send.at[yy, xx], sibling, blk)

    def to_z(xx):
        return block_copy(y, xx, z_send.at[xx], over_z, blk)

    def to_y(xx, way):
        return block_copy(y, xx, y_send.at[xx, way], (req_up, req_down)[way], blk)

    def onward(xx, way):
        return block_copy((down, up)[way], xx, on_send.at[xx], (req_up, req_down)[way], blk)

    def arrived(yy, xx):
        block_copy(yy, xx, x_send, over_z, blk).wait_recv()

    @pl.when(home)
    def _():
        def own(xx, carry):
            @pl.when(root & (xx == x))
            def _():
                keep.wait()

            @pl.when(jnp.logical_not(root & (xx == x)))
            def _():
                arrived(y, xx)

            @pl.when(root)
            def _():
                to_z(xx).start()

            to_y(xx, 0).start()
            to_y(xx, 1).start()
            to_core(y, xx).start()
            return carry

        lax.fori_loop(0, 4, own, 0)

        def near(xx, carry):
            arrived(down, xx)

            @pl.when(xx < 2)
            def _():
                onward(xx, 0).start()

            to_core(down, xx).start()
            arrived(up, xx)

            @pl.when(xx >= 2)
            def _():
                onward(xx, 1).start()

            to_core(up, xx).start()
            return carry

        lax.fori_loop(0, 4, near, 0)

        def last(xx, carry):
            arrived(far, xx)
            to_core(far, xx).start()
            return carry

        lax.fori_loop(0, 4, last, 0)

    @pl.when(jnp.logical_not(home))
    def _():
        def take(i, carry):
            arrived(i // 4, i % 4)
            return carry

        lax.fori_loop(0, 16, take, 0)

    def drain():
        @pl.when(jnp.logical_not(root))
        def _():
            hop.wait_send()

        @pl.when(home)
        def _():
            def step(xx, carry):
                @pl.when(root)
                def _():
                    to_z(xx).wait_send()

                to_y(xx, 0).wait_send()
                to_y(xx, 1).wait_send()

                @pl.when(xx < 2)
                def _():
                    onward(xx, 0).wait_send()

                @pl.when(xx >= 2)
                def _():
                    onward(xx, 1).wait_send()

                return carry

            lax.fori_loop(0, 4, step, 0)

            def core_step(i, carry):
                to_core(i // 4, i % 4).wait_send()
                return carry

            lax.fori_loop(0, 16, core_step, 0)

    return drain


def group_at(j):
    return j + j // 2 - 2 * (j // 3)


def layer_kernel(
    lengths_ref,
    counts_ref,
    q_ref,
    inverse_ref,
    page_slots_ref,
    suffix_ref,
    residual_ref,
    gain_ref,
    cache_ref,
    w_ref,
    hidden_ref,
    updated_ref,
    slab,
    pages_ref,
    fresh_ref,
    hide,
    q_all,
    kv_all,
    values_t,
    scores,
    probs,
    part_out,
    stat_out,
    part_in,
    stat_in,
    held_part,
    held_stat,
    u_ref,
    w_all,
    a_all,
    product,
    relay,
    final,
    own_sum,
    square_out,
    square_in,
    query_send,
    query_recv,
    page_send,
    page_recv,
    part_send,
    part_recv,
    stat_send,
    stat_recv,
    w_send,
    w_recv,
    w_local,
    x_send,
    z_send,
    y_send,
    on_send,
    core_send,
    a_recv,
    r_send,
    relay_recv,
    final_recv,
    q_send,
    q_recv,
    slab_recv,
):
    req, blk, y, zl, core, zh, x = place()
    tokens, features = q_ref.shape
    heads = features // 128
    keys_here = slab.shape[0]
    rows_all = heads * tokens
    width = hidden_ref.shape[1]
    sibling = y * 4 + zl * 2 + (1 - core)
    blk_up, blk_far, blk_down = [((zh + i) % 4) * 4 + x for i in (1, 2, 3)]
    turn = (1.0 / math.sqrt(128)) * math.log2(math.e)

    chunks_w = (pl.ds(0, width), pl.ds(width, width))
    over_z = y * 4 + (1 - zl) * 2 + core

    def ahead(j):
        return ((y + group_at(j)) % 4) * 4 + zl * 2 + core

    def behind(j):
        return ((y + 4 - group_at(j)) % 4) * 4 + zl * 2 + core

    barrier = pltpu.get_barrier_semaphore()
    peers = [(req, zh * 4 + (x + i) % 4) for i in (1, 2, 3)]
    peers += [(sibling, blk), (req, blk_up), (req, blk_far), (req, blk_down)]
    peers += [(over_z, blk)] + [(ahead(j), blk) for j in range(1, 4)]
    for peer in peers:
        pl.semaphore_signal(barrier, inc=1, device_id=peer, device_id_type=MESH)

    pieces = slab_recv.shape[0]
    keys_piece = keys_here // pieces
    slab_copies = [
        pltpu.make_async_copy(
            cache_ref.at[pl.ds(i * keys_piece, keys_piece)],
            slab.at[pl.ds(i * keys_piece, keys_piece)],
            slab_recv.at[i],
        )
        for i in range(pieces)
    ]
    for copy in slab_copies:
        copy.start()

    own_lengths = [lengths_ref[i, req] for i in range(3)]
    starts = [own_lengths[0], own_lengths[0] + own_lengths[1]]
    starts.append(starts[1] + own_lengths[2])
    down_rows = lax.broadcasted_iota(jnp.int32, (tokens, 128), 0)
    along = lax.broadcasted_iota(jnp.int32, (tokens, 128), 1)

    def begin_of(token):
        begin = jnp.zeros_like(token)
        for start in starts:
            begin = jnp.where(token >= start, start, begin)
        return begin

    begin = begin_of(down_rows)
    position = counts_ref[req] * 128 + (down_rows - begin)
    angle = position.astype(jnp.float32) * inverse_ref[...]
    cosines = jnp.cos(angle)
    sines = jnp.where(along < 64, -1.0, 1.0) * jnp.sin(angle)
    allowed = (begin == begin_of(along)) & (down_rows <= along)

    def turned(vector):
        return (vector * cosines + pltpu.roll(vector, 64, 1) * sines).astype(jnp.bfloat16)

    head = blk // 2
    chosen = lax.broadcasted_iota(jnp.int32, (1, 8, 256), 1) == head
    chosen = chosen.astype(jnp.bfloat16)

    def pick_head(block):
        block = block * chosen
        block = block[:, 0:4] + block[:, 4:8]
        block = block[:, 0:2] + block[:, 2:4]
        return block[:, 0] + block[:, 1]

    for h in range(heads):
        vector = q_ref[:, h * 128 : (h + 1) * 128].astype(jnp.float32)
        q_all[0, h * tokens : (h + 1) * tokens, :] = turned(vector)
    pl.semaphore_wait(barrier, len(peers))

    def part_of(r):
        return ((zl + r // 2) % 2) * 2 + (core + r % 2) % 2

    def page_piece(r, send, to_req):
        piece = kv_all.at[part_of(r)]
        return remote(piece, piece, page_send.at[send], page_recv.at[part_of(r)], to_req, blk)

    own_pages = kv_all.at[part_of(0)]
    page_copies = [
        remote(pages_ref, own_pages, page_send.at[i], page_recv.at[part_of(0)], to_req, blk)
        for i, to_req in enumerate((sibling, over_z))
    ]
    page_on = page_piece(2, 2, sibling)
    query_copies = [
        remote(q_all.at[0], q_all.at[j], query_send.at[j], query_recv.at[j], ahead(j), blk)
        for j in range(1, 4)
    ]
    sends = [weight_sends(w_ref, w_all, w_send, w_recv, q, chunks_w[q]) for q in range(2)]
    for copy in query_copies + sends[0]:
        copy.start()
    local = pltpu.make_async_copy(w_ref, w_all.at[x], w_local)
    local.start()
    for i, copy in enumerate(slab_copies):
        copy.wait()

        def pick(p, carry):
            rows = pl.ds(pl.multiple_of(i * keys_piece + p * 128, 128), 128)
            pages_ref[rows, :] = pick_head(slab[rows])
            return carry

        lax.fori_loop(0, keys_piece // 128, pick, 0)
    for copy in page_copies:
        copy.start()
    kv_all[part_of(0)] = pages_ref[...]

    suffix = pick_head(suffix_ref[...])
    fresh_ref[:, 0:128] = turned(suffix[:, 0:128].astype(jnp.float32))
    fresh_ref[:, 128:256] = suffix[:, 128:256]

    @pl.when(blk % 2 == 0)
    def _():
        updated_ref[...] = fresh_ref[:, 0:128]

    @pl.when(blk % 2 == 1)
    def _():
        updated_ref[...] = fresh_ref[:, 128:256]

    slots_here = 4 * keys_here // 128
    slot_ids = (req // 4) * slots_here + lax.broadcasted_iota(jnp.int32, (slots_here, 128), 0)
    page_ids = lax.broadcasted_iota(jnp.int32, (slots_here, 128), 1).astype(jnp.float32)
    match = page_slots_ref[...] == slot_ids
    page_of = jnp.sum(jnp.where(match, page_ids, 0.0), 1, keepdims=True)
    for j in range(4):
        seen = counts_ref[behind(j)].astype(jnp.float32)
        level = jnp.where(page_of < seen, 0.0, NEGATIVE)
        for part in range(4):
            rows = slice(part * slots_here // 4, (part + 1) * slots_here // 4)
            hide[j, part] = jnp.broadcast_to(level[rows], (slots_here // 4, rows_all))

    def fold(block, op):
        parts = [block[i * 8 : (i + 1) * 8] for i in range(block.shape[0] // 8)]
        while len(parts) > 1:
            parts = [op(a, b) for a, b in zip(parts[::2], parts[1::2])]
        return parts[0]

    def last_fold(rows, op):
        return op(rows, 0, keepdims=True)

    fresh_t = jnp.transpose(fresh_ref[:, 128:256].astype(jnp.float32)).astype(jnp.bfloat16)
    raw = lax.dot_general(
        fresh_ref[:, 0:128],
        q_all[0],
        (((1,), (1,)), ((), ())),
        preferred_element_type=jnp.float32,
    )
    mask = jnp.concatenate([allowed.astype(jnp.float32)] * heads, 1)
    raw = jnp.where(mask > 0, raw, NEGATIVE)
    suffix_max = last_fold(fold(raw, jnp.maximum), jnp.max)
    suffix_probs = jnp.exp2((raw - suffix_max) * turn)
    suffix_sum = last_fold(fold(suffix_probs, jnp.add), jnp.sum)
    suffix_part = jnp.dot(
        fresh_t, suffix_probs.astype(jnp.bfloat16), preferred_element_type=jnp.float32
    )

    def turn_values(r):
        for p in range(keys_here // 128):
            block = kv_all[part_of(r), p * 128 : (p + 1) * 128, 128:256].astype(jnp.float32)
            start = r * keys_here + p * 128
            values_t[:, start : start + 128] = jnp.transpose(block).astype(jnp.bfloat16)

    turn_values(0)
    page_piece(1, 2, sibling).wait_recv()
    turn_values(1)

    chunk = 512
    chunks = 2 * keys_here // chunk
    per_core = keys_here // chunk

    def score_chunk(c, j, a, top):
        part = part_of(2 * a + c // per_core)
        inside = c % per_core
        keys = kv_all[part, inside * chunk : (inside + 1) * chunk, 0:128]
        raw = lax.dot_general(
            keys, q_all[j], (((1,), (1,)), ((), ())), preferred_element_type=jnp.float32
        )
        scores[c * chunk : (c + 1) * chunk, :] = raw
        for p in range(chunk // 128):
            page = inside * (chunk // 128) + p
            folded = fold(raw[p * 128 : (p + 1) * 128], jnp.maximum)
            top = jnp.maximum(top, folded + hide[j, part, page : page + 1, :])
        return top

    def weigh_chunk(c, j, a, top, total, weighted):
        part = part_of(2 * a + c // per_core)
        for p in range(chunk // 128):
            page = (c % per_core) * (chunk // 128) + p
            rows = slice(c * chunk + p * 128, c * chunk + (p + 1) * 128)
            level = top - 4.0 * hide[j, part, page : page + 1, :]
            weights = jnp.exp2((scores[rows, :] - level) * turn)
            total = total + fold(weights, jnp.add)
            probs[rows, :] = weights.astype(jnp.bfloat16)
        columns = pl.ds(pl.multiple_of(a * 2 * keys_here + c * chunk, chunk), chunk)
        product_here = jnp.dot(
            values_t[:, columns],
            probs[c * chunk : (c + 1) * chunk, :],
            preferred_element_type=jnp.float32,
        )
        return total, product_here if weighted is None else weighted + product_here

    first_row = lax.broadcasted_iota(jnp.int32, (8, rows_all), 0) == 0

    def merge(j, top, total, weighted):
        other_top, other_sum = held_stat[j, 0:1, :], held_stat[j, 1:2, :]
        joint = jnp.maximum(top, other_top)
        here, there = jnp.exp2((top - joint) * turn), jnp.exp2((other_top - joint) * turn)
        return joint, total * here + other_sum * there, weighted * here + held_part[j] * there

    def part_copies(j):
        return (
            remote(
                part_out.at[j], part_in.at[j], part_send.at[j], part_recv.at[j], behind(j), blk
            ),
            remote(
                stat_out.at[j], stat_in.at[j], stat_send.at[j], stat_recv.at[j], behind(j), blk
            ),
        )

    def unit(u):
        v = u - 4
        later = jnp.where(v == 0, 3, jnp.where(v == 3, 0, v))
        return jnp.where(u < 4, u, later), jnp.where(u < 4, 0, 1)

    low = jnp.full((8, rows_all), NEGATIVE, jnp.float32)
    zero = jnp.zeros((8, rows_all), jnp.float32)

    relays = [weight_relays(w_ref, w_all, w_send, w_recv, q, chunks_w[q]) for q in range(2)]

    def relay_chunk(q):
        for (step, part), copy in zip(((1, 0), (-1, 1)), relays[q]):
            source = (x + 4 - step) % 4
            weight_wait(w_ref, w_all, w_send, w_recv, q, chunks_w[q], source, part)
            copy.start()

    def second_weights():
        for copy in sends[1]:
            copy.start()

    def unit_step(u, carry):
        j, a = unit(u)

        @pl.when(u == 7)
        def _():
            relay_chunk(0)

        @pl.when((u > 0) & (u < 4))
        def _():
            remote(
                q_all.at[0], q_all.at[j], query_send.at[1], query_recv.at[j], ahead(1), blk
            ).wait_recv()

        @pl.when(u == 3)
        def _():
            page_piece(2, 2, over_z).wait_recv()
            page_on.start()
            turn_values(2)

        @pl.when(u == 4)
        def _():
            page_piece(3, 2, sibling).wait_recv()
            turn_values(3)

        top, total, weighted = low, zero, None
        for c in range(chunks):
            top = score_chunk(c, j, a, top)
        top = last_fold(top, jnp.max)
        for c in range(chunks):
            total, weighted = weigh_chunk(c, j, a, top, total, weighted)
        total = last_fold(total, jnp.sum)

        @pl.when(u < 4)
        def _():
            held_part[j] = weighted
            held_stat[j] = jnp.where(first_row, top, total)

        @pl.when(u >= 4)
        def _():
            joint, joint_sum, joint_part = merge(j, top, total, weighted)

            @pl.when(u < 7)
            def _():
                part_out[j] = joint_part.astype(jnp.bfloat16)
                stat_out[j] = jnp.where(first_row, joint, joint_sum)
                for copy in part_copies(j):
                    copy.start()

            @pl.when(u == 7)
            def _():
                held_part[0] = joint_part
                held_stat[0] = jnp.where(first_row, joint, joint_sum)

        return carry

    lax.fori_loop(0, 8, unit_step, 0)

    order = (1, 2, 3)
    for j in order:
        part_copies(j)[1].wait_recv()
    tops = [stat_in[j, 0:1, :] for j in order]
    sums = [stat_in[j, 1:2, :] for j in order]
    own_top, own_total = held_stat[0, 0:1, :], held_stat[0, 1:2, :]
    joint = jnp.maximum(suffix_max, own_top)
    for row in tops:
        joint = jnp.maximum(joint, row)
    factor, own_factor = (jnp.exp2((row - joint) * turn) for row in (suffix_max, own_top))
    joint_sum = suffix_sum * factor + own_total * own_factor
    attended = suffix_part * factor + held_part[0] * own_factor
    for j, row, row_sum in zip(order, tops, sums):
        factor = jnp.exp2((row - joint) * turn)
        joint_sum = joint_sum + row_sum * factor
        part_copies(j)[0].wait_recv()
        attended = attended + part_in[j].astype(jnp.float32) * factor
    attended = attended / joint_sum

    squares_here = jnp.zeros((tokens, 128), jnp.float32)
    for h in range(heads):
        cols = slice(h * 128, (h + 1) * 128)
        own = jnp.transpose(attended[:, h * tokens : (h + 1) * tokens])
        stream = (residual_ref[:, cols].astype(jnp.float32) + own).astype(jnp.bfloat16)
        stream = stream.astype(jnp.float32)
        squares_here = squares_here + stream * stream
        u_ref[0:tokens, cols] = (stream * gain_ref[:, cols]).astype(jnp.bfloat16)
    square_row = jnp.sum(jnp.transpose(squares_here), 0, keepdims=True)
    high = square_row.astype(jnp.bfloat16)
    below = (square_row - high.astype(jnp.float32)).astype(jnp.bfloat16)
    u_ref[tokens : tokens + 16, 0:128] = jnp.broadcast_to(high, (16, 128))
    u_ref[tokens : tokens + 16, 128:256] = jnp.broadcast_to(below, (16, 128))
    u_ref[tokens : tokens + 16, 256:features] = jnp.zeros((16, features - 256), jnp.bfloat16)

    drain = spread_features(
        u_ref, a_all, x_send, z_send, y_send, on_send, core_send, a_recv, second_weights
    )

    def squares(zt, carry):
        total = jnp.zeros((8, 128), jnp.float32)
        for xx in range(4):
            rows = a_all[zt, xx, tokens : tokens + 16, 0:256].astype(jnp.float32)
            total = total + rows[0:8, 0:128] + rows[0:8, 128:256]
        square_out[zt] = total
        return carry

    lax.fori_loop(0, 4, squares, 0)
    square_copies = []
    for i in (1, 2, 3):
        there = (zh + i) % 4
        square_copies.append(
            remote(
                square_out.at[there],
                square_in.at[i - 1],
                q_send.at[i - 1],
                q_recv.at[i - 1],
                req,
                there * 4 + x,
            )
        )
    for copy in square_copies:
        copy.start()

    def multiply(zt, target, q):
        for start, size in ((0, 512), (512, width - 512)):
            cols = pl.ds(q * width + start, size)
            total = jnp.dot(
                a_all[zt, 0, 0:tokens, :], w_all[0, :, cols], preferred_element_type=jnp.float32
            )
            for xx in range(1, 4):
                total = total + jnp.dot(
                    a_all[zt, xx, 0:tokens, :],
                    w_all[xx, :, cols],
                    preferred_element_type=jnp.float32,
                )
            target[:, cols] = total.astype(target.dtype)

    half = tokens // 2
    top_rows, bottom_rows = pl.ds(0, half), pl.ds(half, half)

    def exchange(q):
        cols = chunks_w[q]

        def piece(i, slot, rows, target, recv, to_blk):
            source = product.at[slot, rows, cols]
            return remote(source, target, r_send.at[i, q], recv, req, to_blk)

        def landing(side, rows):
            return final.at[side, rows, cols]

        return (
            piece(0, 0, top_rows, relay.at[0, :, cols], relay_recv.at[0, q], blk_up),
            piece(1, 0, bottom_rows, relay.at[1, :, cols], relay_recv.at[1, q], blk_down),
            piece(2, 1, bottom_rows, landing(0, bottom_rows), final_recv.at[0, 1, q], blk_up),
            piece(3, 2, top_rows, landing(1, top_rows), final_recv.at[1, 0, q], blk_down),
            piece(4, 1, top_rows, landing(0, top_rows), final_recv.at[0, 0, q], blk_up),
            piece(5, 2, bottom_rows, landing(1, bottom_rows), final_recv.at[1, 1, q], blk_down),
        )

    exchanges = [exchange(0), exchange(1)]

    def wait_weights(q):
        for step, part in ((3, 0), (3, 1), (1, 0), (1, 1), (2, 0), (2, 1)):
            if (step, part) not in ((3, 0), (1, 1)):
                source = (x + step) % 4
                weight_wait(w_ref, w_all, w_send, w_recv, q, chunks_w[q], source, part)

    def add_relay(slot, rows, index, q):
        def tile(n, carry):
            cols = pl.ds(pl.multiple_of(q * width + n * 128, 128), 128)
            total = product[slot, rows, cols].astype(jnp.float32) + relay[index, :, cols].astype(
                jnp.float32
            )
            product[slot, rows, cols] = total.astype(jnp.bfloat16)
            return carry

        lax.fori_loop(0, width // 128, tile, 0)

    def send_far(q):
        wait_weights(q)
        multiply((zh + 2) % 4, product.at[0], q)
        exchanges[q][0].start()
        exchanges[q][1].start()

    def send_near(q):
        multiply((zh + 1) % 4, product.at[1], q)
        exchanges[q][2].start()
        multiply((zh + 3) % 4, product.at[2], q)
        exchanges[q][3].start()

    def send_sums(q):
        exchanges[q][0].wait_recv()
        add_relay(1, top_rows, 0, q)
        exchanges[q][4].start()
        exchanges[q][1].wait_recv()
        add_relay(2, bottom_rows, 1, q)
        exchanges[q][5].start()

    local.wait()
    send_far(0)
    send_near(0)
    relay_chunk(1)
    send_sums(0)
    send_far(1)
    send_near(1)
    send_sums(1)
    multiply(zh, own_sum, 0)
    multiply(zh, own_sum, 1)

    for copy in square_copies:
        copy.wait_recv()
    row = square_out[zh] + square_in[0] + square_in[1] + square_in[2]
    spread = jnp.broadcast_to(row[0:1, :], (tokens, tokens))
    diagonal = lax.broadcasted_iota(jnp.int32, (tokens, tokens), 0) == lax.broadcasted_iota(
        jnp.int32, (tokens, tokens), 1
    )
    square_sum = jnp.sum(jnp.where(diagonal, spread, 0.0), 1, keepdims=True)
    scale = jnp.broadcast_to(lax.rsqrt(square_sum / D + EPSILON), (tokens, 128))

    def finish(n, carry):
        def column_sum(start):
            cols = pl.ds(pl.multiple_of(start, 128), 128)
            total = own_sum[:, cols] + final[0, :, cols].astype(jnp.float32)
            return (total + final[1, :, cols].astype(jnp.float32)) * scale

        gate, up = column_sum(n * 128), column_sum(width + n * 128)
        value = gate / (1.0 + jnp.exp(-gate)) * up
        hidden_ref[:, pl.ds(pl.multiple_of(n * 128, 128), 128)] = value.astype(jnp.bfloat16)
        return carry

    for q in range(2):
        for copy in exchanges[q][2:]:
            copy.wait_recv()
    lax.fori_loop(0, width // 128, finish, 0)

    for copy in sends[0] + sends[1] + relays[0] + relays[1] + square_copies:
        copy.wait_send()
    for q in range(2):
        for copy in exchanges[q]:
            copy.wait_send()
    drain()
    for copy in query_copies + page_copies + [page_on]:
        copy.wait_send()
    for j in order:
        for copy in part_copies(j):
            copy.wait_send()


def layer(lengths, counts, q, page_slots, suffix, residual, gain, cache, weights):
    depth, wide = weights.shape
    tokens, features = q.shape
    rows_all = tokens * features // 128
    keys_here, _, lanes = cache.shape
    keys = 2 * keys_here
    groups = 4
    dma = pltpu.SemaphoreType.DMA
    bf16, f32 = jnp.bfloat16, jnp.float32
    vmem = pl.BlockSpec(memory_space=pltpu.VMEM)
    return pl.pallas_call(
        layer_kernel,
        out_shape=(
            jax.ShapeDtypeStruct((tokens, wide // 2), bf16),
            jax.ShapeDtypeStruct((tokens, 128), bf16),
        ),
        in_specs=[pl.BlockSpec(memory_space=pltpu.SMEM)] * 2
        + [vmem] * 6
        + [pl.BlockSpec(memory_space=pl.ANY)] * 2,
        out_specs=(vmem, vmem),
        scratch_shapes=[
            pltpu.VMEM(cache.shape, bf16),
            pltpu.VMEM((keys_here, lanes), bf16),
            pltpu.VMEM((tokens, lanes), bf16),
            pltpu.VMEM((groups, 4, keys_here // 128, rows_all), f32),
            pltpu.VMEM((groups, rows_all, 128), bf16),
            pltpu.VMEM((4, keys_here, lanes), bf16),
            pltpu.VMEM((128, 2 * keys), bf16),
            pltpu.VMEM((keys, rows_all), f32),
            pltpu.VMEM((keys, rows_all), bf16),
            pltpu.VMEM((groups, 128, rows_all), bf16),
            pltpu.VMEM((groups, 8, rows_all), f32),
            pltpu.VMEM((groups, 128, rows_all), bf16),
            pltpu.VMEM((groups, 8, rows_all), f32),
            pltpu.VMEM((groups, 128, rows_all), f32),
            pltpu.VMEM((groups, 8, rows_all), f32),
            pltpu.VMEM((tokens + 16, features), bf16),
            pltpu.VMEM((4, depth, wide), bf16),
            pltpu.VMEM((4, 4, tokens + 16, features), bf16),
            pltpu.VMEM((3, tokens, wide), bf16),
            pltpu.VMEM((2, tokens // 2, wide), bf16),
            pltpu.VMEM((2, tokens, wide), bf16),
            pltpu.VMEM((tokens, wide), f32),
            pltpu.VMEM((4, 8, 128), f32),
            pltpu.VMEM((3, 8, 128), f32),
            dma((groups,)),
            dma((groups,)),
            dma((3,)),
            dma((4,)),
            dma((groups,)),
            dma((groups,)),
            dma((groups,)),
            dma((groups,)),
            dma((6, 2)),
            dma((4, 2, 2)),
            dma,
            dma,
            dma((4,)),
            dma((4, 2)),
            dma((4,)),
            dma((4, 4)),
            dma((4, 4)),
            dma((6, 2)),
            dma((2, 2)),
            dma((2, 2, 2)),
            dma((3,)),
            dma((3,)),
            dma((4,)),
        ],
        compiler_params=pltpu.CompilerParams(collective_id=1, has_side_effects=True),
        name="layer",
    )(
        lengths,
        counts,
        q,
        jnp.asarray(inverse_frequencies(64)),
        page_slots,
        suffix,
        residual,
        gain,
        cache,
        weights,
    )


def on_device(
    queries,
    suffix_key_value,
    residual,
    gain,
    gate_up,
    prefix_cache_slots,
    prefix_page_slots,
    lengths,
    counts,
):
    slots, page_len, heads_kv, lanes = prefix_cache_slots.shape
    return layer(
        lengths.T,
        counts,
        queries,
        prefix_page_slots[None, :],
        suffix_key_value,
        residual,
        gain[None, :],
        prefix_cache_slots.reshape(slots * page_len, heads_kv, lanes),
        gate_up.reshape(gate_up.shape[0], 2 * gate_up.shape[2]),
    )


def solution(mesh):
    placed = (
        P("req", "blk"),
        P("req", None, None),
        P("req", "blk"),
        P("blk"),
        P("blk", None, "req"),
        P("req", None, None, None),
        P(),
        P(),
        P(),
    )
    return jax.shard_map(
        on_device,
        mesh=mesh,
        in_specs=placed,
        out_specs=(P("blk", "req"), P("req", "blk")),
        check_vma=False,
    )
```

```python
import math

import jax
import jax.numpy as jnp
from jax import lax
from jax.experimental import pallas as pl
from jax.experimental.pallas import tpu as pltpu
from jax.sharding import PartitionSpec as P
import numpy as np

D = 8192

MESH = pl.DeviceIdType.MESH

NEGATIVE = -1e30
EPSILON = 1e-05
ROPE_BASE = 500000.0


def inverse_frequencies(half_dim):
    exponent = np.float32(-math.log(ROPE_BASE)) * np.arange(half_dim, dtype=np.float32)
    exponent = exponent * np.float32(2.0) / np.float32(2 * half_dim)
    inverse = np.exp(exponent.astype(np.float64)).astype(np.float32)
    return np.concatenate([inverse, inverse])[None, :]


def remote(src, dst, send_sem, recv_sem, req, blk):
    return pltpu.make_async_remote_copy(
        src_ref=src,
        dst_ref=dst,
        send_sem=send_sem,
        recv_sem=recv_sem,
        device_id=(req, blk),
        device_id_type=MESH,
    )


def place():
    req, blk = lax.axis_index("req"), lax.axis_index("blk")
    y, zl, core = req // 4, (req // 2) % 2, req % 2
    return req, blk, y, zl, core, blk // 4, blk % 4


def weight_pieces(w_ref, w_all, chunk):
    half = w_ref.shape[0] // 2

    def own(part):
        return w_ref.at[pl.ds(part * half, half), chunk]

    def slot(source, part):
        return w_all.at[source, pl.ds(part * half, half), chunk]

    return own, slot


def weight_sends(w_ref, w_all, send, recv, q, chunk):
    req, blk, y, zl, core, zh, x = place()
    own, slot = weight_pieces(w_ref, w_all, chunk)
    return [
        remote(
            own(part),
            slot(x, part),
            send.at[j, q],
            recv.at[x, part, q],
            req,
            zh * 4 + (x + 4 + step) % 4,
        )
        for j, (step, part) in enumerate(((1, 0), (-1, 1), (1, 1), (-1, 0)))
    ]


def weight_relays(w_ref, w_all, send, recv, q, chunk):
    req, blk, y, zl, core, zh, x = place()
    own, slot = weight_pieces(w_ref, w_all, chunk)
    out = []
    for j, (step, part) in enumerate(((1, 0), (-1, 1))):
        source = (x + 4 - step) % 4
        piece = slot(source, part)
        to_blk = zh * 4 + (x + 4 + step) % 4
        out.append(remote(piece, piece, send.at[4 + j, q], recv.at[source, part, q], req, to_blk))
    return out


def weight_wait(w_ref, w_all, send, recv, q, chunk, source, part):
    req, blk, y, zl, core, zh, x = place()
    piece = weight_pieces(w_ref, w_all, chunk)[1](source, part)
    to_blk = zh * 4 + (x + 1) % 4
    remote(piece, piece, send.at[0, q], recv.at[source, part, q], req, to_blk).wait_recv()


def spread_features(
    u_ref, a_all, x_send, z_send, y_send, on_send, core_send, recv, after_hop
):
    req, blk, y, zl, core, zh, x = place()
    target = zl * 2 + core
    home = core == x % 2
    root = x == target
    over_z = y * 4 + (1 - zl) * 2 + core
    sibling = y * 4 + zl * 2 + (1 - core)
    up, down = (y + 1) % 4, (y + 3) % 4
    far = (y + 2) % 4
    req_up, req_down = up * 4 + zl * 2 + core, down * 4 + zl * 2 + core

    rows = u_ref.shape[0]
    halves = (pl.ds(0, 64), pl.ds(64, rows - 64))
    both = range(2)

    def block_copy(yy, xx, h, send, to_req, to_blk):
        piece = a_all.at[yy, xx, halves[h]]
        return remote(piece, piece, send, recv.at[yy, xx, h], to_req, to_blk)

    hops = [
        remote(
            u_ref.at[halves[h]],
            a_all.at[y, x, halves[h]],
            x_send.at[h],
            recv.at[y, x, h],
            req,
            zh * 4 + target,
        )
        for h in both
    ]
    keeps = [
        pltpu.make_async_copy(u_ref.at[halves[h]], a_all.at[y, x, halves[h]], recv.at[y, x, h])
        for h in both
    ]

    @pl.when(root)
    def _():
        for keep in keeps:
            keep.start()

    @pl.when(jnp.logical_not(root))
    def _():
        for hop in hops:
            hop.start()

    after_hop()

    def to_core(yy, xx, h):
        return block_copy(yy, xx, h, core_send.at[yy, xx, h], sibling, blk)

    def to_z(xx, h):
        return block_copy(y, xx, h, z_send.at[xx, h], over_z, blk)

    def to_y(xx, h, way):
        return block_copy(y, xx, h, y_send.at[xx, way, h], (req_up, req_down)[way], blk)

    def onward(xx, h, way):
        return block_copy((down, up)[way], xx, h, on_send.at[xx, h], (req_up, req_down)[way], blk)

    def arrived(yy, xx, h):
        block_copy(yy, xx, h, x_send.at[0], over_z, blk).wait_recv()

    def nearest(i):
        return (x + group_at(i)) % 4

    def own_stage():
        @pl.when(home)
        def _():
            def step(i, carry):
                xx = nearest(i)

                for h in both:

                    @pl.when(root & (i == 0))
                    def _():
                        keeps[h].wait()

                    @pl.when(jnp.logical_not(root & (i == 0)))
                    def _():
                        arrived(y, xx, h)

                    to_y(xx, h, 0).start()
                    to_y(xx, h, 1).start()

                    @pl.when(root)
                    def _():
                        to_z(xx, h).start()

                    to_core(y, xx, h).start()
                return carry

            lax.fori_loop(0, 4, step, 0)

        take(y)

    def near_stage():
        @pl.when(home)
        def _():
            def step(i, carry):
                xx = nearest(i)
                for h in both:
                    arrived(down, xx, h)

                    @pl.when(i % 2 == 0)
                    def _():
                        onward(xx, h, 0).start()

                    to_core(down, xx, h).start()
                    arrived(up, xx, h)

                    @pl.when(i % 2 == 1)
                    def _():
                        onward(xx, h, 1).start()

                    to_core(up, xx, h).start()
                return carry

            lax.fori_loop(0, 4, step, 0)

        take(down)
        take(up)

    def last_stage():
        @pl.when(home)
        def _():
            def step(i, carry):
                xx = nearest(i)
                for h in both:
                    arrived(far, xx, h)
                    to_core(far, xx, h).start()
                return carry

            lax.fori_loop(0, 4, step, 0)

        take(far)

    def take(yy):
        @pl.when(jnp.logical_not(home))
        def _():
            def step(i, carry):
                for h in both:
                    arrived(yy, nearest(i), h)
                return carry

            lax.fori_loop(0, 4, step, 0)

    def drain():
        @pl.when(jnp.logical_not(root))
        def _():
            for hop in hops:
                hop.wait_send()

        @pl.when(home)
        def _():
            def step(i, carry):
                xx = nearest(i)

                for h in both:

                    @pl.when(root)
                    def _():
                        to_z(xx, h).wait_send()

                    to_y(xx, h, 0).wait_send()
                    to_y(xx, h, 1).wait_send()

                    @pl.when(i % 2 == 0)
                    def _():
                        onward(xx, h, 0).wait_send()

                    @pl.when(i % 2 == 1)
                    def _():
                        onward(xx, h, 1).wait_send()

                return carry

            lax.fori_loop(0, 4, step, 0)

            def core_step(i, carry):
                for h in both:
                    to_core(i // 4, i % 4, h).wait_send()
                return carry

            lax.fori_loop(0, 16, core_step, 0)

    return own_stage, near_stage, last_stage, drain


def group_at(j):
    return j + j // 2 - 2 * (j // 3)


def layer_kernel(
    lengths_ref,
    counts_ref,
    q_ref,
    inverse_ref,
    page_slots_ref,
    suffix_ref,
    residual_ref,
    gain_ref,
    cache_ref,
    w_ref,
    hidden_ref,
    updated_ref,
    slab,
    pages_ref,
    fresh_ref,
    hide,
    q_all,
    kv_all,
    values_t,
    scores,
    probs,
    part_out,
    stat_out,
    part_in,
    stat_in,
    held_part,
    held_stat,
    u_ref,
    w_all,
    a_all,
    product,
    relay,
    final,
    square_out,
    square_in,
    query_send,
    query_recv,
    page_send,
    page_recv,
    part_send,
    part_recv,
    stat_send,
    stat_recv,
    w_send,
    w_recv,
    w_local,
    x_send,
    z_send,
    y_send,
    on_send,
    core_send,
    a_recv,
    r_send,
    relay_recv,
    final_recv,
    q_send,
    q_recv,
    slab_recv,
):
    req, blk, y, zl, core, zh, x = place()
    tokens, features = q_ref.shape
    heads = features // 128
    keys_here = slab.shape[0]
    rows_all = heads * tokens
    width = hidden_ref.shape[1]
    sibling = y * 4 + zl * 2 + (1 - core)
    blk_up, blk_far, blk_down = [((zh + i) % 4) * 4 + x for i in (1, 2, 3)]
    turn = (1.0 / math.sqrt(128)) * math.log2(math.e)

    bounds_w = ((0, width), (width, 2 * width))
    chunks_w = tuple(pl.ds(low, high - low) for low, high in bounds_w)
    over_z = y * 4 + (1 - zl) * 2 + core

    def ahead(j):
        return ((y + group_at(j)) % 4) * 4 + zl * 2 + core

    def behind(j):
        return ((y + 4 - group_at(j)) % 4) * 4 + zl * 2 + core

    barrier = pltpu.get_barrier_semaphore()
    peers = [(req, zh * 4 + (x + i) % 4) for i in (1, 2, 3)]
    peers += [(sibling, blk), (req, blk_up), (req, blk_far), (req, blk_down)]
    peers += [(over_z, blk)] + [(ahead(j), blk) for j in range(1, 4)]
    for peer in peers:
        pl.semaphore_signal(barrier, inc=1, device_id=peer, device_id_type=MESH)

    pieces = slab_recv.shape[0]
    keys_piece = keys_here // pieces
    slab_copies = [
        pltpu.make_async_copy(
            cache_ref.at[pl.ds(i * keys_piece, keys_piece)],
            slab.at[pl.ds(i * keys_piece, keys_piece)],
            slab_recv.at[i],
        )
        for i in range(pieces)
    ]
    for copy in slab_copies:
        copy.start()

    own_lengths = [lengths_ref[i, req] for i in range(3)]
    starts = [own_lengths[0], own_lengths[0] + own_lengths[1]]
    starts.append(starts[1] + own_lengths[2])
    down_rows = lax.broadcasted_iota(jnp.int32, (tokens, 128), 0)
    along = lax.broadcasted_iota(jnp.int32, (tokens, 128), 1)

    def begin_of(token):
        begin = jnp.zeros_like(token)
        for start in starts:
            begin = jnp.where(token >= start, start, begin)
        return begin

    begin = begin_of(down_rows)
    position = counts_ref[req] * 128 + (down_rows - begin)
    angle = position.astype(jnp.float32) * inverse_ref[...]
    cosines = jnp.cos(angle)
    sines = jnp.where(along < 64, -1.0, 1.0) * jnp.sin(angle)
    allowed = (begin == begin_of(along)) & (down_rows <= along)

    def turned(vector):
        return (vector * cosines + pltpu.roll(vector, 64, 1) * sines).astype(jnp.bfloat16)

    head = blk // 2
    chosen = lax.broadcasted_iota(jnp.int32, (1, 8, 256), 1) == head
    chosen = chosen.astype(jnp.bfloat16)

    def pick_head(block):
        block = block * chosen
        block = block[:, 0:4] + block[:, 4:8]
        block = block[:, 0:2] + block[:, 2:4]
        return block[:, 0] + block[:, 1]

    for h in range(heads):
        vector = q_ref[:, h * 128 : (h + 1) * 128].astype(jnp.float32)
        q_all[0, h * tokens : (h + 1) * tokens, :] = turned(vector)
    pl.semaphore_wait(barrier, len(peers))

    def part_of(r):
        return ((zl + r // 2) % 2) * 2 + (core + r % 2) % 2

    def page_piece(r, send, to_req):
        piece = kv_all.at[part_of(r)]
        return remote(piece, piece, page_send.at[send], page_recv.at[part_of(r)], to_req, blk)

    own_pages = kv_all.at[part_of(0)]
    page_copies = [
        remote(pages_ref, own_pages, page_send.at[i], page_recv.at[part_of(0)], to_req, blk)
        for i, to_req in enumerate((sibling, over_z))
    ]
    page_on = page_piece(2, 2, sibling)
    query_copies = [
        remote(q_all.at[0], q_all.at[j], query_send.at[j], query_recv.at[j], ahead(j), blk)
        for j in range(1, 4)
    ]
    sends = [weight_sends(w_ref, w_all, w_send, w_recv, q, chunks_w[q]) for q in range(2)]
    for copy in query_copies + sends[0]:
        copy.start()
    local = pltpu.make_async_copy(w_ref, w_all.at[x], w_local)
    local.start()
    for i, copy in enumerate(slab_copies):
        copy.wait()

        def pick(p, carry):
            rows = pl.ds(pl.multiple_of(i * keys_piece + p * 128, 128), 128)
            pages_ref[rows, :] = pick_head(slab[rows])
            return carry

        lax.fori_loop(0, keys_piece // 128, pick, 0)
    for copy in page_copies:
        copy.start()
    kv_all[part_of(0)] = pages_ref[...]

    suffix = pick_head(suffix_ref[...])
    fresh_ref[:, 0:128] = turned(suffix[:, 0:128].astype(jnp.float32))
    fresh_ref[:, 128:256] = suffix[:, 128:256]

    @pl.when(blk % 2 == 0)
    def _():
        updated_ref[...] = fresh_ref[:, 0:128]

    @pl.when(blk % 2 == 1)
    def _():
        updated_ref[...] = fresh_ref[:, 128:256]

    slots_here = 4 * keys_here // 128
    slot_ids = (req // 4) * slots_here + lax.broadcasted_iota(jnp.int32, (slots_here, 128), 0)
    page_ids = lax.broadcasted_iota(jnp.int32, (slots_here, 128), 1).astype(jnp.float32)
    match = page_slots_ref[...] == slot_ids
    page_of = jnp.sum(jnp.where(match, page_ids, 0.0), 1, keepdims=True)
    for j in range(4):
        seen = counts_ref[behind(j)].astype(jnp.float32)
        level = jnp.where(page_of < seen, 0.0, NEGATIVE)
        for part in range(4):
            rows = slice(part * slots_here // 4, (part + 1) * slots_here // 4)
            hide[j, part] = jnp.broadcast_to(level[rows], (slots_here // 4, rows_all))

    def fold(block, op):
        parts = [block[i * 8 : (i + 1) * 8] for i in range(block.shape[0] // 8)]
        while len(parts) > 1:
            parts = [op(a, b) for a, b in zip(parts[::2], parts[1::2])]
        return parts[0]

    def last_fold(rows, op):
        return op(rows, 0, keepdims=True)

    fresh_t = jnp.transpose(fresh_ref[:, 128:256].astype(jnp.float32)).astype(jnp.bfloat16)
    raw = lax.dot_general(
        fresh_ref[:, 0:128],
        q_all[0],
        (((1,), (1,)), ((), ())),
        preferred_element_type=jnp.float32,
    )
    mask = jnp.concatenate([allowed.astype(jnp.float32)] * heads, 1)
    raw = jnp.where(mask > 0, raw, NEGATIVE)
    suffix_max = last_fold(fold(raw, jnp.maximum), jnp.max)
    suffix_probs = jnp.exp2((raw - suffix_max) * turn)
    suffix_sum = last_fold(fold(suffix_probs, jnp.add), jnp.sum)
    suffix_part = jnp.dot(
        fresh_t, suffix_probs.astype(jnp.bfloat16), preferred_element_type=jnp.float32
    )

    def turn_values(r):
        for p in range(keys_here // 128):
            block = kv_all[part_of(r), p * 128 : (p + 1) * 128, 128:256].astype(jnp.float32)
            start = r * keys_here + p * 128
            values_t[0:128, start : start + 128] = jnp.transpose(block).astype(jnp.bfloat16)

    values_t[128:144, :] = jnp.ones((16, values_t.shape[1]), jnp.bfloat16)
    turn_values(0)
    page_piece(1, 2, sibling).wait_recv()
    turn_values(1)

    chunk = 512
    chunks = 2 * keys_here // chunk
    per_core = keys_here // chunk

    def score_chunk(c, j, a, top):
        part = part_of(2 * a + c // per_core)
        inside = c % per_core
        keys = kv_all[part, inside * chunk : (inside + 1) * chunk, 0:128]
        raw = lax.dot_general(
            keys, q_all[j], (((1,), (1,)), ((), ())), preferred_element_type=jnp.float32
        )
        scores[c * chunk : (c + 1) * chunk, :] = raw
        for p in range(chunk // 128):
            page = inside * (chunk // 128) + p
            folded = fold(raw[p * 128 : (p + 1) * 128], jnp.maximum)
            top = jnp.maximum(top, folded + hide[j, part, page : page + 1, :])
        return top

    def weigh_chunk(c, j, a, top, weighted):
        part = part_of(2 * a + c // per_core)
        for p in range(chunk // 128):
            page = (c % per_core) * (chunk // 128) + p
            rows = slice(c * chunk + p * 128, c * chunk + (p + 1) * 128)
            level = top - 4.0 * hide[j, part, page : page + 1, :]
            weights = jnp.exp2((scores[rows, :] - level) * turn)
            probs[rows, :] = weights.astype(jnp.bfloat16)
        columns = pl.ds(pl.multiple_of(a * 2 * keys_here + c * chunk, chunk), chunk)
        product_here = jnp.dot(
            values_t[:, columns],
            probs[c * chunk : (c + 1) * chunk, :],
            preferred_element_type=jnp.float32,
        )
        return product_here if weighted is None else weighted + product_here

    first_row = lax.broadcasted_iota(jnp.int32, (8, rows_all), 0) == 0

    def merge(j, top, total, weighted):
        other_top, other_sum = held_stat[j, 0:1, :], held_stat[j, 1:2, :]
        joint = jnp.maximum(top, other_top)
        here, there = jnp.exp2((top - joint) * turn), jnp.exp2((other_top - joint) * turn)
        return joint, total * here + other_sum * there, weighted * here + held_part[j] * there

    def part_copies(j):
        return (
            remote(
                part_out.at[j], part_in.at[j], part_send.at[j], part_recv.at[j], behind(j), blk
            ),
            remote(
                stat_out.at[j], stat_in.at[j], stat_send.at[j], stat_recv.at[j], behind(j), blk
            ),
        )

    def unit(u):
        v = u - 4
        later = jnp.where(v == 0, 3, jnp.where(v == 3, 0, v))
        return jnp.where(u < 4, u, later), jnp.where(u < 4, 0, 1)

    low = jnp.full((8, rows_all), NEGATIVE, jnp.float32)

    relays = [weight_relays(w_ref, w_all, w_send, w_recv, q, chunks_w[q]) for q in range(2)]

    def relay_chunk(q):
        for (step, part), copy in zip(((1, 0), (-1, 1)), relays[q]):
            source = (x + 4 - step) % 4
            weight_wait(w_ref, w_all, w_send, w_recv, q, chunks_w[q], source, part)
            copy.start()

    def more_weights():
        for copy in sends[1]:
            copy.start()

    def unit_step(u, carry):
        j, a = unit(u)

        @pl.when(u == 4)
        def _():
            relay_chunk(0)

        @pl.when((u > 0) & (u < 4))
        def _():
            remote(
                q_all.at[0], q_all.at[j], query_send.at[1], query_recv.at[j], ahead(1), blk
            ).wait_recv()

        @pl.when(u == 3)
        def _():
            page_piece(2, 2, over_z).wait_recv()
            page_on.start()
            turn_values(2)

        @pl.when(u == 4)
        def _():
            page_piece(3, 2, sibling).wait_recv()
            turn_values(3)

        top, weighted = low, None
        for c in range(chunks):
            top = score_chunk(c, j, a, top)
        top = last_fold(top, jnp.max)
        for c in range(chunks):
            weighted = weigh_chunk(c, j, a, top, weighted)
        total, weighted = weighted[128:129], weighted[0:128]

        @pl.when(u < 4)
        def _():
            held_part[j] = weighted
            held_stat[j] = jnp.where(first_row, top, total)

        @pl.when(u >= 4)
        def _():
            joint, joint_sum, joint_part = merge(j, top, total, weighted)

            @pl.when(u < 7)
            def _():
                part_out[j] = joint_part.astype(jnp.bfloat16)
                stat_out[j] = jnp.where(first_row, joint, joint_sum)
                for copy in part_copies(j):
                    copy.start()

            @pl.when(u == 7)
            def _():
                held_part[0] = joint_part
                held_stat[0] = jnp.where(first_row, joint, joint_sum)

        return carry

    lax.fori_loop(0, 8, unit_step, 0)

    order = (1, 2, 3)
    for j in order:
        part_copies(j)[1].wait_recv()
    tops = [stat_in[j, 0:1, :] for j in order]
    sums = [stat_in[j, 1:2, :] for j in order]
    own_top, own_total = held_stat[0, 0:1, :], held_stat[0, 1:2, :]
    joint = jnp.maximum(suffix_max, own_top)
    for row in tops:
        joint = jnp.maximum(joint, row)
    factor, own_factor = (jnp.exp2((row - joint) * turn) for row in (suffix_max, own_top))
    joint_sum = suffix_sum * factor + own_total * own_factor
    attended = suffix_part * factor + held_part[0] * own_factor
    for j, row, row_sum in zip(order, tops, sums):
        factor = jnp.exp2((row - joint) * turn)
        joint_sum = joint_sum + row_sum * factor
        part_copies(j)[0].wait_recv()
        attended = attended + part_in[j].astype(jnp.float32) * factor
    attended = attended / joint_sum

    squares_here = jnp.zeros((tokens, 128), jnp.float32)
    for h in range(heads):
        cols = slice(h * 128, (h + 1) * 128)
        own = jnp.transpose(attended[:, h * tokens : (h + 1) * tokens])
        stream = (residual_ref[:, cols].astype(jnp.float32) + own).astype(jnp.bfloat16)
        stream = stream.astype(jnp.float32)
        squares_here = squares_here + stream * stream
        u_ref[0:tokens, cols] = (stream * gain_ref[:, cols]).astype(jnp.bfloat16)
    square_row = jnp.sum(jnp.transpose(squares_here), 0, keepdims=True)
    high = square_row.astype(jnp.bfloat16)
    below = (square_row - high.astype(jnp.float32)).astype(jnp.bfloat16)
    u_ref[tokens : tokens + 16, 0:128] = jnp.broadcast_to(high, (16, 128))
    u_ref[tokens : tokens + 16, 128:256] = jnp.broadcast_to(below, (16, 128))
    u_ref[tokens : tokens + 16, 256:features] = jnp.zeros((16, features - 256), jnp.bfloat16)

    own_stage, near_stage, last_stage, drain = spread_features(
        u_ref, a_all, x_send, z_send, y_send, on_send, core_send, a_recv, more_weights
    )

    def multiply(zt, target, q):
        first, end = bounds_w[q]
        for start in range(first, end, 512):
            cols = pl.ds(start, min(512, end - start))
            total = jnp.dot(
                a_all[zt, 0, 0:tokens, :], w_all[0, :, cols], preferred_element_type=jnp.float32
            )
            for xx in range(1, 4):
                total = total + jnp.dot(
                    a_all[zt, xx, 0:tokens, :],
                    w_all[xx, :, cols],
                    preferred_element_type=jnp.float32,
                )
            target[:, cols] = total.astype(target.dtype)

    half = tokens // 2
    top_rows, bottom_rows = pl.ds(0, half), pl.ds(half, half)

    def exchange(q):
        cols = chunks_w[q]

        def piece(i, slot, rows, target, recv, to_blk):
            source = product.at[slot, rows, cols]
            return remote(source, target, r_send.at[i, q], recv, req, to_blk)

        def landing(side, rows):
            return final.at[side, rows, cols]

        return (
            piece(0, 2, top_rows, relay.at[0, :, cols], relay_recv.at[0, q], blk_up),
            piece(1, 2, bottom_rows, relay.at[1, :, cols], relay_recv.at[1, q], blk_down),
            piece(2, 1, bottom_rows, landing(0, bottom_rows), final_recv.at[0, 1, q], blk_up),
            piece(3, 3, top_rows, landing(1, top_rows), final_recv.at[1, 0, q], blk_down),
            piece(4, 1, top_rows, landing(0, top_rows), final_recv.at[0, 0, q], blk_up),
            piece(5, 3, bottom_rows, landing(1, bottom_rows), final_recv.at[1, 1, q], blk_down),
        )

    exchanges = [exchange(0), exchange(1)]

    def wait_weights(q):
        for step, part in ((3, 0), (3, 1), (1, 0), (1, 1), (2, 0), (2, 1)):
            if (step, part) not in ((3, 0), (1, 1)):
                source = (x + step) % 4
                weight_wait(w_ref, w_all, w_send, w_recv, q, chunks_w[q], source, part)

    def add_relay(slot, rows, index, q):
        def tile(n, carry):
            cols = pl.ds(pl.multiple_of(n * 128, 128), 128)
            total = product[slot, rows, cols].astype(jnp.float32) + relay[index, :, cols].astype(
                jnp.float32
            )
            product[slot, rows, cols] = total.astype(jnp.bfloat16)
            return carry

        first, end = bounds_w[q]
        lax.fori_loop(first // 128, end // 128, tile, 0)

    def send_sums(q):
        exchanges[q][0].wait_recv()
        add_relay(1, top_rows, 0, q)
        exchanges[q][4].start()
        exchanges[q][1].wait_recv()
        add_relay(3, bottom_rows, 1, q)
        exchanges[q][5].start()

    def first_step(i, carry):
        @pl.when(i == 0)
        def _():
            own_stage()
            local.wait()
            wait_weights(0)

        @pl.when(i == 1)
        def _():
            near_stage()

        @pl.when(i == 3)
        def _():
            last_stage()

        zt = (y + group_at(i)) % 4
        distance = (zt + 4 - zh) % 4
        multiply(zt, product.at[distance], 0)

        @pl.when(distance == 2)
        def _():
            exchanges[0][0].start()
            exchanges[0][1].start()

        @pl.when(distance == 1)
        def _():
            exchanges[0][2].start()

        @pl.when(distance == 3)
        def _():
            exchanges[0][3].start()

        return carry

    lax.fori_loop(0, 4, first_step, 0)

    def squares(zt, carry):
        total = jnp.zeros((8, 128), jnp.float32)
        for xx in range(4):
            rows = a_all[zt, xx, tokens : tokens + 16, 0:256].astype(jnp.float32)
            total = total + rows[0:8, 0:128] + rows[0:8, 128:256]
        square_out[zt] = total
        return carry

    lax.fori_loop(0, 4, squares, 0)
    square_copies = []
    for i in (1, 2, 3):
        there = (zh + i) % 4
        square_copies.append(
            remote(
                square_out.at[there],
                square_in.at[i - 1],
                q_send.at[i - 1],
                q_recv.at[i - 1],
                req,
                there * 4 + x,
            )
        )
    for copy in square_copies:
        copy.start()

    relay_chunk(1)
    send_sums(0)
    wait_weights(1)
    multiply((zh + 2) % 4, product.at[2], 1)
    exchanges[1][0].start()
    exchanges[1][1].start()
    multiply((zh + 1) % 4, product.at[1], 1)
    exchanges[1][2].start()
    multiply((zh + 3) % 4, product.at[3], 1)
    exchanges[1][3].start()
    multiply(zh, product.at[0], 1)
    send_sums(1)

    for copy in square_copies:
        copy.wait_recv()
    row = square_out[zh] + square_in[0] + square_in[1] + square_in[2]
    spread = jnp.broadcast_to(row[0:1, :], (tokens, tokens))
    diagonal = lax.broadcasted_iota(jnp.int32, (tokens, tokens), 0) == lax.broadcasted_iota(
        jnp.int32, (tokens, tokens), 1
    )
    square_sum = jnp.sum(jnp.where(diagonal, spread, 0.0), 1, keepdims=True)
    scale = jnp.broadcast_to(lax.rsqrt(square_sum / D + EPSILON), (tokens, 128))

    def finish(n, carry):
        def column_sum(start):
            cols = pl.ds(pl.multiple_of(start, 128), 128)
            total = product[0, :, cols].astype(jnp.float32) + final[0, :, cols].astype(jnp.float32)
            return (total + final[1, :, cols].astype(jnp.float32)) * scale

        gate, up = column_sum(n * 128), column_sum(width + n * 128)
        value = gate / (1.0 + jnp.exp(-gate)) * up
        hidden_ref[:, pl.ds(pl.multiple_of(n * 128, 128), 128)] = value.astype(jnp.bfloat16)
        return carry

    for q in range(2):
        for copy in exchanges[q][2:]:
            copy.wait_recv()
    lax.fori_loop(0, width // 128, finish, 0)

    for copy in sends[0] + sends[1] + relays[0] + relays[1] + square_copies:
        copy.wait_send()
    for q in range(2):
        for copy in exchanges[q]:
            copy.wait_send()
    drain()
    for copy in query_copies + page_copies + [page_on]:
        copy.wait_send()
    for j in order:
        for copy in part_copies(j):
            copy.wait_send()


def layer(lengths, counts, q, page_slots, suffix, residual, gain, cache, weights):
    depth, wide = weights.shape
    tokens, features = q.shape
    rows_all = tokens * features // 128
    keys_here, _, lanes = cache.shape
    keys = 2 * keys_here
    groups = 4
    dma = pltpu.SemaphoreType.DMA
    bf16, f32 = jnp.bfloat16, jnp.float32
    vmem = pl.BlockSpec(memory_space=pltpu.VMEM)
    return pl.pallas_call(
        layer_kernel,
        out_shape=(
            jax.ShapeDtypeStruct((tokens, wide // 2), bf16),
            jax.ShapeDtypeStruct((tokens, 128), bf16),
        ),
        in_specs=[pl.BlockSpec(memory_space=pltpu.SMEM)] * 2
        + [vmem] * 6
        + [pl.BlockSpec(memory_space=pl.ANY)] * 2,
        out_specs=(vmem, vmem),
        scratch_shapes=[
            pltpu.VMEM(cache.shape, bf16),
            pltpu.VMEM((keys_here, lanes), bf16),
            pltpu.VMEM((tokens, lanes), bf16),
            pltpu.VMEM((groups, 4, keys_here // 128, rows_all), f32),
            pltpu.VMEM((groups, rows_all, 128), bf16),
            pltpu.VMEM((4, keys_here, lanes), bf16),
            pltpu.VMEM((144, 2 * keys), bf16),
            pltpu.VMEM((keys, rows_all), f32),
            pltpu.VMEM((keys, rows_all), bf16),
            pltpu.VMEM((groups, 128, rows_all), bf16),
            pltpu.VMEM((groups, 8, rows_all), f32),
            pltpu.VMEM((groups, 128, rows_all), bf16),
            pltpu.VMEM((groups, 8, rows_all), f32),
            pltpu.VMEM((groups, 128, rows_all), f32),
            pltpu.VMEM((groups, 8, rows_all), f32),
            pltpu.VMEM((tokens + 16, features), bf16),
            pltpu.VMEM((4, depth, wide), bf16),
            pltpu.VMEM((4, 4, tokens + 16, features), bf16),
            pltpu.VMEM((4, tokens, wide), bf16),
            pltpu.VMEM((2, tokens // 2, wide), bf16),
            pltpu.VMEM((2, tokens, wide), bf16),
            pltpu.VMEM((4, 8, 128), f32),
            pltpu.VMEM((3, 8, 128), f32),
            dma((groups,)),
            dma((groups,)),
            dma((3,)),
            dma((4,)),
            dma((groups,)),
            dma((groups,)),
            dma((groups,)),
            dma((groups,)),
            dma((6, 2)),
            dma((4, 2, 2)),
            dma,
            dma((2,)),
            dma((4, 2)),
            dma((4, 2, 2)),
            dma((4, 2)),
            dma((4, 4, 2)),
            dma((4, 4, 2)),
            dma((6, 2)),
            dma((2, 2)),
            dma((2, 2, 2)),
            dma((3,)),
            dma((3,)),
            dma((4,)),
        ],
        compiler_params=pltpu.CompilerParams(collective_id=1, has_side_effects=True),
        name="layer",
    )(
        lengths,
        counts,
        q,
        jnp.asarray(inverse_frequencies(64)),
        page_slots,
        suffix,
        residual,
        gain,
        cache,
        weights,
    )


def on_device(
    queries,
    suffix_key_value,
    residual,
    gain,
    gate_up,
    prefix_cache_slots,
    prefix_page_slots,
    lengths,
    counts,
):
    slots, page_len, heads_kv, lanes = prefix_cache_slots.shape
    return layer(
        lengths.T,
        counts,
        queries,
        prefix_page_slots[None, :],
        suffix_key_value,
        residual,
        gain[None, :],
        prefix_cache_slots.reshape(slots * page_len, heads_kv, lanes),
        gate_up.reshape(gate_up.shape[0], 2 * gate_up.shape[2]),
    )


def solution(mesh):
    placed = (
        P("req", "blk"),
        P("req", None, None),
        P("req", "blk"),
        P("blk"),
        P("blk", None, "req"),
        P("req", None, None, None),
        P(),
        P(),
        P(),
    )
    return jax.shard_map(
        on_device,
        mesh=mesh,
        in_specs=placed,
        out_specs=(P("blk", "req"), P("req", "blk")),
        check_vma=False,
    )
```

```python
import math

import jax
import jax.numpy as jnp
from jax import lax
from jax.experimental import pallas as pl
from jax.experimental.pallas import tpu as pltpu
from jax.sharding import PartitionSpec as P
import numpy as np

D = 8192

MESH = pl.DeviceIdType.MESH

NEGATIVE = -1e30
EPSILON = 1e-05
ROPE_BASE = 500000.0


def inverse_frequencies(half_dim):
    exponent = np.float32(-math.log(ROPE_BASE)) * np.arange(half_dim, dtype=np.float32)
    exponent = exponent * np.float32(2.0) / np.float32(2 * half_dim)
    inverse = np.exp(exponent.astype(np.float64)).astype(np.float32)
    return np.concatenate([inverse, inverse])[None, :]


def remote(src, dst, send_sem, recv_sem, req, blk):
    return pltpu.make_async_remote_copy(
        src_ref=src,
        dst_ref=dst,
        send_sem=send_sem,
        recv_sem=recv_sem,
        device_id=(req, blk),
        device_id_type=MESH,
    )


def place():
    req, blk = lax.axis_index("req"), lax.axis_index("blk")
    y, zl, core = req // 4, (req // 2) % 2, req % 2
    return req, blk, y, zl, core, blk // 4, blk % 4


def weight_pieces(w_ref, w_all, chunk):
    half = w_ref.shape[0] // 2

    def own(part):
        return w_ref.at[pl.ds(part * half, half), chunk]

    def slot(source, part):
        return w_all.at[source, pl.ds(part * half, half), chunk]

    return own, slot


def weight_sends(w_ref, w_all, send, recv, q, chunk):
    req, blk, y, zl, core, zh, x = place()
    own, slot = weight_pieces(w_ref, w_all, chunk)
    return [
        remote(
            own(part),
            slot(x, part),
            send.at[j, q],
            recv.at[x, part, q],
            req,
            zh * 4 + (x + 4 + step) % 4,
        )
        for j, (step, part) in enumerate(((1, 0), (-1, 1), (1, 1), (-1, 0)))
    ]


def weight_relays(w_ref, w_all, send, recv, q, chunk):
    req, blk, y, zl, core, zh, x = place()
    own, slot = weight_pieces(w_ref, w_all, chunk)
    out = []
    for j, (step, part) in enumerate(((1, 0), (-1, 1))):
        source = (x + 4 - step) % 4
        piece = slot(source, part)
        to_blk = zh * 4 + (x + 4 + step) % 4
        out.append(remote(piece, piece, send.at[4 + j, q], recv.at[source, part, q], req, to_blk))
    return out


def weight_wait(w_ref, w_all, send, recv, q, chunk, source, part):
    req, blk, y, zl, core, zh, x = place()
    piece = weight_pieces(w_ref, w_all, chunk)[1](source, part)
    to_blk = zh * 4 + (x + 1) % 4
    remote(piece, piece, send.at[0, q], recv.at[source, part, q], req, to_blk).wait_recv()


def spread_features(
    u_ref, a_all, x_send, z_send, y_send, on_send, core_send, recv, after_hop
):
    req, blk, y, zl, core, zh, x = place()
    target = zl * 2 + core
    home = core == x % 2
    root = x == target
    over_z = y * 4 + (1 - zl) * 2 + core
    sibling = y * 4 + zl * 2 + (1 - core)
    up, down = (y + 1) % 4, (y + 3) % 4
    far = (y + 2) % 4
    req_up, req_down = up * 4 + zl * 2 + core, down * 4 + zl * 2 + core

    rows = u_ref.shape[0]
    halves = (pl.ds(0, 64), pl.ds(64, rows - 64))
    both = range(2)

    def block_copy(yy, xx, h, send, to_req, to_blk):
        piece = a_all.at[yy, xx, halves[h]]
        return remote(piece, piece, send, recv.at[yy, xx, h], to_req, to_blk)

    hops = [
        remote(
            u_ref.at[halves[h]],
            a_all.at[y, x, halves[h]],
            x_send.at[h],
            recv.at[y, x, h],
            req,
            zh * 4 + target,
        )
        for h in both
    ]
    keeps = [
        pltpu.make_async_copy(u_ref.at[halves[h]], a_all.at[y, x, halves[h]], recv.at[y, x, h])
        for h in both
    ]

    @pl.when(root)
    def _():
        for keep in keeps:
            keep.start()

    @pl.when(jnp.logical_not(root))
    def _():
        for hop in hops:
            hop.start()

    after_hop()

    def to_core(yy, xx, h):
        return block_copy(yy, xx, h, core_send.at[yy, xx, h], sibling, blk)

    def to_z(xx, h):
        return block_copy(y, xx, h, z_send.at[xx, h], over_z, blk)

    def to_y(xx, h, way):
        return block_copy(y, xx, h, y_send.at[xx, way, h], (req_up, req_down)[way], blk)

    def onward(xx, h, way):
        return block_copy((down, up)[way], xx, h, on_send.at[xx, h], (req_up, req_down)[way], blk)

    def arrived(yy, xx, h):
        block_copy(yy, xx, h, x_send.at[0], over_z, blk).wait_recv()

    def nearest(i):
        return (x + group_at(i)) % 4

    def own_stage():
        @pl.when(home)
        def _():
            def step(i, carry):
                xx = nearest(i)

                for h in both:

                    @pl.when(root & (i == 0))
                    def _():
                        keeps[h].wait()

                    @pl.when(jnp.logical_not(root & (i == 0)))
                    def _():
                        arrived(y, xx, h)

                    to_y(xx, h, 0).start()
                    to_y(xx, h, 1).start()

                    @pl.when(root)
                    def _():
                        to_z(xx, h).start()

                    to_core(y, xx, h).start()
                return carry

            lax.fori_loop(0, 4, step, 0)

        take(y)

    def near_stage():
        @pl.when(home)
        def _():
            def step(i, carry):
                xx = nearest(i)
                for h in both:
                    arrived(down, xx, h)

                    @pl.when(i % 2 == 0)
                    def _():
                        onward(xx, h, 0).start()

                    to_core(down, xx, h).start()
                    arrived(up, xx, h)

                    @pl.when(i % 2 == 1)
                    def _():
                        onward(xx, h, 1).start()

                    to_core(up, xx, h).start()
                return carry

            lax.fori_loop(0, 4, step, 0)

        take(down)
        take(up)

    def last_stage():
        @pl.when(home)
        def _():
            def step(i, carry):
                xx = nearest(i)
                for h in both:
                    arrived(far, xx, h)
                    to_core(far, xx, h).start()
                return carry

            lax.fori_loop(0, 4, step, 0)

        take(far)

    def take(yy):
        @pl.when(jnp.logical_not(home))
        def _():
            def step(i, carry):
                for h in both:
                    arrived(yy, nearest(i), h)
                return carry

            lax.fori_loop(0, 4, step, 0)

    def drain():
        @pl.when(jnp.logical_not(root))
        def _():
            for hop in hops:
                hop.wait_send()

        @pl.when(home)
        def _():
            def step(i, carry):
                xx = nearest(i)

                for h in both:

                    @pl.when(root)
                    def _():
                        to_z(xx, h).wait_send()

                    to_y(xx, h, 0).wait_send()
                    to_y(xx, h, 1).wait_send()

                    @pl.when(i % 2 == 0)
                    def _():
                        onward(xx, h, 0).wait_send()

                    @pl.when(i % 2 == 1)
                    def _():
                        onward(xx, h, 1).wait_send()

                return carry

            lax.fori_loop(0, 4, step, 0)

            def core_step(i, carry):
                for h in both:
                    to_core(i // 4, i % 4, h).wait_send()
                return carry

            lax.fori_loop(0, 16, core_step, 0)

    return own_stage, near_stage, last_stage, drain


def group_at(j):
    return j + j // 2 - 2 * (j // 3)


def layer_kernel(
    lengths_ref,
    counts_ref,
    q_ref,
    inverse_ref,
    page_slots_ref,
    suffix_ref,
    residual_ref,
    gain_ref,
    cache_ref,
    w_ref,
    hidden_ref,
    updated_ref,
    slab,
    pages_ref,
    fresh_ref,
    hide,
    q_all,
    kv_all,
    values_t,
    scores,
    probs,
    part_out,
    stat_out,
    part_in,
    stat_in,
    held_part,
    held_stat,
    u_ref,
    w_all,
    a_all,
    product,
    relay,
    final,
    square_out,
    square_in,
    query_send,
    query_recv,
    page_send,
    page_recv,
    part_send,
    part_recv,
    stat_send,
    stat_recv,
    w_send,
    w_recv,
    w_local,
    x_send,
    z_send,
    y_send,
    on_send,
    core_send,
    a_recv,
    r_send,
    relay_recv,
    final_recv,
    q_send,
    q_recv,
    slab_recv,
):
    req, blk, y, zl, core, zh, x = place()
    tokens, features = q_ref.shape
    heads = features // 128
    keys_here = slab.shape[0]
    rows_all = heads * tokens
    width = hidden_ref.shape[1]
    sibling = y * 4 + zl * 2 + (1 - core)
    blk_up, blk_far, blk_down = [((zh + i) % 4) * 4 + x for i in (1, 2, 3)]
    turn = (1.0 / math.sqrt(128)) * math.log2(math.e)

    bounds_w = ((0, width), (width, 2 * width))
    chunks_w = tuple(pl.ds(low, high - low) for low, high in bounds_w)
    over_z = y * 4 + (1 - zl) * 2 + core

    def ahead(j):
        return ((y + group_at(j)) % 4) * 4 + zl * 2 + core

    def behind(j):
        return ((y + 4 - group_at(j)) % 4) * 4 + zl * 2 + core

    barrier = pltpu.get_barrier_semaphore()
    peers = [(req, zh * 4 + (x + i) % 4) for i in (1, 2, 3)]
    peers += [(sibling, blk), (req, blk_up), (req, blk_far), (req, blk_down)]
    peers += [(over_z, blk)] + [(ahead(j), blk) for j in range(1, 4)]
    for peer in peers:
        pl.semaphore_signal(barrier, inc=1, device_id=peer, device_id_type=MESH)

    pieces = slab_recv.shape[0]
    keys_piece = keys_here // pieces
    slab_copies = [
        pltpu.make_async_copy(
            cache_ref.at[pl.ds(i * keys_piece, keys_piece)],
            slab.at[pl.ds(i * keys_piece, keys_piece)],
            slab_recv.at[i],
        )
        for i in range(pieces)
    ]
    for copy in slab_copies:
        copy.start()

    own_lengths = [lengths_ref[i, req] for i in range(3)]
    starts = [own_lengths[0], own_lengths[0] + own_lengths[1]]
    starts.append(starts[1] + own_lengths[2])
    down_rows = lax.broadcasted_iota(jnp.int32, (tokens, 128), 0)
    along = lax.broadcasted_iota(jnp.int32, (tokens, 128), 1)

    def begin_of(token):
        begin = jnp.zeros_like(token)
        for start in starts:
            begin = jnp.where(token >= start, start, begin)
        return begin

    begin = begin_of(down_rows)
    position = counts_ref[req] * 128 + (down_rows - begin)
    angle = position.astype(jnp.float32) * inverse_ref[...]
    cosines = jnp.cos(angle)
    sines = jnp.where(along < 64, -1.0, 1.0) * jnp.sin(angle)
    allowed = (begin == begin_of(along)) & (down_rows <= along)

    def turned(vector):
        return (vector * cosines + pltpu.roll(vector, 64, 1) * sines).astype(jnp.bfloat16)

    head = blk // 2
    chosen = lax.broadcasted_iota(jnp.int32, (1, 8, 256), 1) == head
    chosen = chosen.astype(jnp.bfloat16)

    def pick_head(block):
        block = block * chosen
        block = block[:, 0:4] + block[:, 4:8]
        block = block[:, 0:2] + block[:, 2:4]
        return block[:, 0] + block[:, 1]

    for h in range(heads):
        vector = q_ref[:, h * 128 : (h + 1) * 128].astype(jnp.float32)
        q_all[0, h * tokens : (h + 1) * tokens, :] = turned(vector)
    pl.semaphore_wait(barrier, len(peers))

    def part_of(r):
        return ((zl + r // 2) % 2) * 2 + (core + r % 2) % 2

    def page_piece(r, send, to_req):
        piece = kv_all.at[part_of(r)]
        return remote(piece, piece, page_send.at[send], page_recv.at[part_of(r)], to_req, blk)

    own_pages = kv_all.at[part_of(0)]
    page_copies = [
        remote(pages_ref, own_pages, page_send.at[i], page_recv.at[part_of(0)], to_req, blk)
        for i, to_req in enumerate((sibling, over_z))
    ]
    page_on = page_piece(2, 2, sibling)
    query_copies = [
        remote(q_all.at[0], q_all.at[j], query_send.at[j], query_recv.at[j], ahead(j), blk)
        for j in range(1, 4)
    ]
    sends = [weight_sends(w_ref, w_all, w_send, w_recv, q, chunks_w[q]) for q in range(2)]
    for copy in query_copies + sends[0]:
        copy.start()
    local = pltpu.make_async_copy(w_ref, w_all.at[x], w_local)
    local.start()
    for i, copy in enumerate(slab_copies):
        copy.wait()

        def pick(p, carry):
            rows = pl.ds(pl.multiple_of(i * keys_piece + p * 128, 128), 128)
            pages_ref[rows, :] = pick_head(slab[rows])
            return carry

        lax.fori_loop(0, keys_piece // 128, pick, 0)
    for copy in page_copies:
        copy.start()
    kv_all[part_of(0)] = pages_ref[...]

    suffix = pick_head(suffix_ref[...])
    fresh_ref[:, 0:128] = turned(suffix[:, 0:128].astype(jnp.float32))
    fresh_ref[:, 128:256] = suffix[:, 128:256]

    @pl.when(blk % 2 == 0)
    def _():
        updated_ref[...] = fresh_ref[:, 0:128]

    @pl.when(blk % 2 == 1)
    def _():
        updated_ref[...] = fresh_ref[:, 128:256]

    slots_here = 4 * keys_here // 128
    slot_ids = (req // 4) * slots_here + lax.broadcasted_iota(jnp.int32, (slots_here, 128), 0)
    page_ids = lax.broadcasted_iota(jnp.int32, (slots_here, 128), 1).astype(jnp.float32)
    match = page_slots_ref[...] == slot_ids
    page_of = jnp.sum(jnp.where(match, page_ids, 0.0), 1, keepdims=True)
    for j in range(4):
        seen = counts_ref[behind(j)].astype(jnp.float32)
        level = jnp.where(page_of < seen, 0.0, NEGATIVE)
        for part in range(4):
            rows = slice(part * slots_here // 4, (part + 1) * slots_here // 4)
            hide[j, part] = jnp.broadcast_to(level[rows], (slots_here // 4, rows_all))

    def fold(block, op):
        parts = [block[i * 8 : (i + 1) * 8] for i in range(block.shape[0] // 8)]
        while len(parts) > 1:
            parts = [op(a, b) for a, b in zip(parts[::2], parts[1::2])]
        return parts[0]

    def last_fold(rows, op):
        return op(rows, 0, keepdims=True)

    fresh_t = jnp.transpose(fresh_ref[:, 128:256].astype(jnp.float32)).astype(jnp.bfloat16)
    raw = lax.dot_general(
        fresh_ref[:, 0:128],
        q_all[0],
        (((1,), (1,)), ((), ())),
        preferred_element_type=jnp.float32,
    )
    mask = jnp.concatenate([allowed.astype(jnp.float32)] * heads, 1)
    raw = jnp.where(mask > 0, raw, NEGATIVE)
    suffix_max = last_fold(fold(raw, jnp.maximum), jnp.max)
    suffix_probs = jnp.exp2((raw - suffix_max) * turn)
    suffix_sum = last_fold(fold(suffix_probs, jnp.add), jnp.sum)
    suffix_part = jnp.dot(
        fresh_t, suffix_probs.astype(jnp.bfloat16), preferred_element_type=jnp.float32
    )

    def turn_values(r):
        for p in range(keys_here // 128):
            block = kv_all[part_of(r), p * 128 : (p + 1) * 128, 128:256].astype(jnp.float32)
            start = r * keys_here + p * 128
            values_t[0:128, start : start + 128] = jnp.transpose(block).astype(jnp.bfloat16)

    values_t[128:144, :] = jnp.ones((16, values_t.shape[1]), jnp.bfloat16)
    turn_values(0)
    page_piece(1, 2, sibling).wait_recv()
    turn_values(1)

    chunk = 512
    chunks = 2 * keys_here // chunk
    per_core = keys_here // chunk

    def score_chunk(c, j, a, top):
        part = part_of(2 * a + c // per_core)
        inside = c % per_core
        keys = kv_all[part, inside * chunk : (inside + 1) * chunk, 0:128]
        raw = lax.dot_general(
            keys, q_all[j], (((1,), (1,)), ((), ())), preferred_element_type=jnp.float32
        )
        scores[c * chunk : (c + 1) * chunk, :] = raw
        for p in range(chunk // 128):
            page = inside * (chunk // 128) + p
            folded = fold(raw[p * 128 : (p + 1) * 128], jnp.maximum)
            top = jnp.maximum(top, folded + hide[j, part, page : page + 1, :])
        return top

    def weigh_chunk(c, j, a, top, weighted):
        part = part_of(2 * a + c // per_core)
        for p in range(chunk // 128):
            page = (c % per_core) * (chunk // 128) + p
            rows = slice(c * chunk + p * 128, c * chunk + (p + 1) * 128)
            level = top - 4.0 * hide[j, part, page : page + 1, :]
            weights = jnp.exp2((scores[rows, :] - level) * turn)
            probs[rows, :] = weights.astype(jnp.bfloat16)
        columns = pl.ds(pl.multiple_of(a * 2 * keys_here + c * chunk, chunk), chunk)
        product_here = jnp.dot(
            values_t[:, columns],
            probs[c * chunk : (c + 1) * chunk, :],
            preferred_element_type=jnp.float32,
        )
        return product_here if weighted is None else weighted + product_here

    first_row = lax.broadcasted_iota(jnp.int32, (8, rows_all), 0) == 0

    def merge(j, top, total, weighted):
        other_top, other_sum = held_stat[j, 0:1, :], held_stat[j, 1:2, :]
        joint = jnp.maximum(top, other_top)
        here, there = jnp.exp2((top - joint) * turn), jnp.exp2((other_top - joint) * turn)
        return joint, total * here + other_sum * there, weighted * here + held_part[j] * there

    def part_copies(j):
        return (
            remote(
                part_out.at[j], part_in.at[j], part_send.at[j], part_recv.at[j], behind(j), blk
            ),
            remote(
                stat_out.at[j], stat_in.at[j], stat_send.at[j], stat_recv.at[j], behind(j), blk
            ),
        )

    def unit(u):
        v = u - 4
        later = jnp.where(v == 0, 3, jnp.where(v == 3, 0, v))
        return jnp.where(u < 4, u, later), jnp.where(u < 4, 0, 1)

    low = jnp.full((8, rows_all), NEGATIVE, jnp.float32)

    relays = [weight_relays(w_ref, w_all, w_send, w_recv, q, chunks_w[q]) for q in range(2)]

    def relay_chunk(q):
        for (step, part), copy in zip(((1, 0), (-1, 1)), relays[q]):
            source = (x + 4 - step) % 4
            weight_wait(w_ref, w_all, w_send, w_recv, q, chunks_w[q], source, part)
            copy.start()

    def more_weights():
        for copy in sends[1]:
            copy.start()

    def unit_step(u, carry):
        j, a = unit(u)

        @pl.when(u == 4)
        def _():
            relay_chunk(0)

        @pl.when((u > 0) & (u < 4))
        def _():
            remote(
                q_all.at[0], q_all.at[j], query_send.at[1], query_recv.at[j], ahead(1), blk
            ).wait_recv()

        @pl.when(u == 3)
        def _():
            page_piece(2, 2, over_z).wait_recv()
            page_on.start()
            turn_values(2)

        @pl.when(u == 4)
        def _():
            page_piece(3, 2, sibling).wait_recv()
            turn_values(3)

        top, weighted = low, None
        for c in range(chunks):
            top = score_chunk(c, j, a, top)
        top = last_fold(top, jnp.max)
        for c in range(chunks):
            weighted = weigh_chunk(c, j, a, top, weighted)
        total, weighted = weighted[128:129], weighted[0:128]

        @pl.when(u < 4)
        def _():
            held_part[j] = weighted
            held_stat[j] = jnp.where(first_row, top, total)

        @pl.when(u >= 4)
        def _():
            joint, joint_sum, joint_part = merge(j, top, total, weighted)

            @pl.when(u < 7)
            def _():
                part_out[j] = joint_part.astype(jnp.bfloat16)
                stat_out[j] = jnp.where(first_row, joint, joint_sum)
                for copy in part_copies(j):
                    copy.start()

            @pl.when(u == 7)
            def _():
                held_part[0] = joint_part
                held_stat[0] = jnp.where(first_row, joint, joint_sum)

        return carry

    lax.fori_loop(0, 8, unit_step, 0)

    order = (1, 2, 3)
    for j in order:
        part_copies(j)[1].wait_recv()
    tops = [stat_in[j, 0:1, :] for j in order]
    sums = [stat_in[j, 1:2, :] for j in order]
    own_top, own_total = held_stat[0, 0:1, :], held_stat[0, 1:2, :]
    joint = jnp.maximum(suffix_max, own_top)
    for row in tops:
        joint = jnp.maximum(joint, row)
    factor, own_factor = (jnp.exp2((row - joint) * turn) for row in (suffix_max, own_top))
    joint_sum = suffix_sum * factor + own_total * own_factor
    attended = suffix_part * factor + held_part[0] * own_factor
    for j, row, row_sum in zip(order, tops, sums):
        factor = jnp.exp2((row - joint) * turn)
        joint_sum = joint_sum + row_sum * factor
        part_copies(j)[0].wait_recv()
        attended = attended + part_in[j].astype(jnp.float32) * factor
    attended = attended / joint_sum

    squares_here = jnp.zeros((tokens, 128), jnp.float32)
    for h in range(heads):
        cols = slice(h * 128, (h + 1) * 128)
        own = jnp.transpose(attended[:, h * tokens : (h + 1) * tokens])
        stream = (residual_ref[:, cols].astype(jnp.float32) + own).astype(jnp.bfloat16)
        stream = stream.astype(jnp.float32)
        squares_here = squares_here + stream * stream
        u_ref[0:tokens, cols] = (stream * gain_ref[:, cols]).astype(jnp.bfloat16)
    square_row = jnp.sum(jnp.transpose(squares_here), 0, keepdims=True)
    high = square_row.astype(jnp.bfloat16)
    below = (square_row - high.astype(jnp.float32)).astype(jnp.bfloat16)
    u_ref[tokens : tokens + 16, 0:128] = jnp.broadcast_to(high, (16, 128))
    u_ref[tokens : tokens + 16, 128:256] = jnp.broadcast_to(below, (16, 128))
    u_ref[tokens : tokens + 16, 256:features] = jnp.zeros((16, features - 256), jnp.bfloat16)

    own_stage, near_stage, last_stage, drain = spread_features(
        u_ref, a_all, x_send, z_send, y_send, on_send, core_send, a_recv, more_weights
    )

    def multiply(zt, target, q):
        first, end = bounds_w[q]
        for start in range(first, end, 512):
            cols = pl.ds(start, min(512, end - start))
            total = jnp.dot(
                a_all[zt, 0, 0:tokens, :], w_all[0, :, cols], preferred_element_type=jnp.float32
            )
            for xx in range(1, 4):
                total = total + jnp.dot(
                    a_all[zt, xx, 0:tokens, :],
                    w_all[xx, :, cols],
                    preferred_element_type=jnp.float32,
                )
            target[:, cols] = total.astype(target.dtype)

    half = tokens // 2
    top_rows, bottom_rows = pl.ds(0, half), pl.ds(half, half)

    def exchange(q):
        cols = chunks_w[q]

        def piece(i, slot, rows, target, recv, to_blk):
            source = product.at[slot, rows, cols]
            return remote(source, target, r_send.at[i, q], recv, req, to_blk)

        def landing(side, rows):
            return final.at[side, rows, cols]

        return (
            piece(0, 2, top_rows, relay.at[0, :, cols], relay_recv.at[0, q], blk_up),
            piece(1, 2, bottom_rows, relay.at[1, :, cols], relay_recv.at[1, q], blk_down),
            piece(2, 1, bottom_rows, landing(0, bottom_rows), final_recv.at[0, 1, q], blk_up),
            piece(3, 3, top_rows, landing(1, top_rows), final_recv.at[1, 0, q], blk_down),
            piece(4, 1, top_rows, landing(0, top_rows), final_recv.at[0, 0, q], blk_up),
            piece(5, 3, bottom_rows, landing(1, bottom_rows), final_recv.at[1, 1, q], blk_down),
        )

    exchanges = [exchange(0), exchange(1)]

    def wait_weights(q):
        for step, part in ((3, 0), (3, 1), (1, 0), (1, 1), (2, 0), (2, 1)):
            if (step, part) not in ((3, 0), (1, 1)):
                source = (x + step) % 4
                weight_wait(w_ref, w_all, w_send, w_recv, q, chunks_w[q], source, part)

    def add_relay(slot, rows, index, q):
        def tile(n, carry):
            cols = pl.ds(pl.multiple_of(n * 128, 128), 128)
            total = product[slot, rows, cols].astype(jnp.float32) + relay[index, :, cols].astype(
                jnp.float32
            )
            product[slot, rows, cols] = total.astype(jnp.bfloat16)
            return carry

        first, end = bounds_w[q]
        lax.fori_loop(first // 128, end // 128, tile, 0)

    def send_sums(q):
        exchanges[q][0].wait_recv()
        add_relay(1, top_rows, 0, q)
        exchanges[q][4].start()
        exchanges[q][1].wait_recv()
        add_relay(3, bottom_rows, 1, q)
        exchanges[q][5].start()

    def first_step(i, carry):
        @pl.when(i == 0)
        def _():
            own_stage()
            local.wait()
            wait_weights(0)

        @pl.when(i == 1)
        def _():
            near_stage()

        @pl.when(i == 3)
        def _():
            last_stage()

        zt = (y + group_at(i)) % 4
        distance = (zt + 4 - zh) % 4
        multiply(zt, product.at[distance], 0)

        @pl.when(distance == 2)
        def _():
            exchanges[0][0].start()
            exchanges[0][1].start()

        @pl.when(distance == 1)
        def _():
            exchanges[0][2].start()

        @pl.when(distance == 3)
        def _():
            exchanges[0][3].start()

        return carry

    lax.fori_loop(0, 4, first_step, 0)

    def squares(zt, carry):
        total = jnp.zeros((8, 128), jnp.float32)
        for xx in range(4):
            rows = a_all[zt, xx, tokens : tokens + 16, 0:256].astype(jnp.float32)
            total = total + rows[0:8, 0:128] + rows[0:8, 128:256]
        square_out[zt] = total
        return carry

    lax.fori_loop(0, 4, squares, 0)
    square_copies = []
    for i in (1, 2, 3):
        there = (zh + i) % 4
        square_copies.append(
            remote(
                square_out.at[there],
                square_in.at[i - 1],
                q_send.at[i - 1],
                q_recv.at[i - 1],
                req,
                there * 4 + x,
            )
        )
    for copy in square_copies:
        copy.start()

    relay_chunk(1)
    send_sums(0)
    wait_weights(1)
    multiply((zh + 2) % 4, product.at[2], 1)
    exchanges[1][0].start()
    exchanges[1][1].start()
    multiply((zh + 1) % 4, product.at[1], 1)
    exchanges[1][2].start()
    multiply((zh + 3) % 4, product.at[3], 1)
    exchanges[1][3].start()
    multiply(zh, product.at[0], 1)
    send_sums(1)

    for copy in square_copies:
        copy.wait_recv()
    row = square_out[zh] + square_in[0] + square_in[1] + square_in[2]
    spread = jnp.broadcast_to(row[0:1, :], (tokens, tokens))
    diagonal = lax.broadcasted_iota(jnp.int32, (tokens, tokens), 0) == lax.broadcasted_iota(
        jnp.int32, (tokens, tokens), 1
    )
    square_sum = jnp.sum(jnp.where(diagonal, spread, 0.0), 1, keepdims=True)
    scale = jnp.broadcast_to(lax.rsqrt(square_sum / D + EPSILON), (tokens, 128))

    def finish(n, carry):
        def column_sum(start):
            cols = pl.ds(pl.multiple_of(start, 128), 128)
            total = product[0, :, cols].astype(jnp.float32) + final[0, :, cols].astype(jnp.float32)
            return (total + final[1, :, cols].astype(jnp.float32)) * scale

        gate, up = column_sum(n * 128), column_sum(width + n * 128)
        value = gate / (1.0 + jnp.exp(-gate)) * up
        hidden_ref[:, pl.ds(pl.multiple_of(n * 128, 128), 128)] = value.astype(jnp.bfloat16)
        return carry

    for q in range(2):
        for copy in exchanges[q][2:]:
            copy.wait_recv()
    lax.fori_loop(0, width // 128, finish, 0)

    for copy in sends[0] + sends[1] + relays[0] + relays[1] + square_copies:
        copy.wait_send()
    for q in range(2):
        for copy in exchanges[q]:
            copy.wait_send()
    drain()
    for copy in query_copies + page_copies + [page_on]:
        copy.wait_send()
    for j in order:
        for copy in part_copies(j):
            copy.wait_send()


def layer(lengths, counts, q, page_slots, suffix, residual, gain, cache, weights):
    depth, wide = weights.shape
    tokens, features = q.shape
    rows_all = tokens * features // 128
    keys_here, _, lanes = cache.shape
    keys = 2 * keys_here
    groups = 4
    dma = pltpu.SemaphoreType.DMA
    bf16, f32 = jnp.bfloat16, jnp.float32
    vmem = pl.BlockSpec(memory_space=pltpu.VMEM)
    return pl.pallas_call(
        layer_kernel,
        out_shape=(
            jax.ShapeDtypeStruct((tokens, wide // 2), bf16),
            jax.ShapeDtypeStruct((tokens, 128), bf16),
        ),
        in_specs=[pl.BlockSpec(memory_space=pltpu.SMEM)] * 2
        + [vmem] * 6
        + [pl.BlockSpec(memory_space=pl.ANY)] * 2,
        out_specs=(vmem, vmem),
        scratch_shapes=[
            pltpu.VMEM(cache.shape, bf16),
            pltpu.VMEM((keys_here, lanes), bf16),
            pltpu.VMEM((tokens, lanes), bf16),
            pltpu.VMEM((groups, 4, keys_here // 128, rows_all), f32),
            pltpu.VMEM((groups, rows_all, 128), bf16),
            pltpu.VMEM((4, keys_here, lanes), bf16),
            pltpu.VMEM((144, 2 * keys), bf16),
            pltpu.VMEM((keys, rows_all), f32),
            pltpu.VMEM((keys, rows_all), bf16),
            pltpu.VMEM((groups, 128, rows_all), bf16),
            pltpu.VMEM((groups, 8, rows_all), f32),
            pltpu.VMEM((groups, 128, rows_all), bf16),
            pltpu.VMEM((groups, 8, rows_all), f32),
            pltpu.VMEM((groups, 128, rows_all), f32),
            pltpu.VMEM((groups, 8, rows_all), f32),
            pltpu.VMEM((tokens + 16, features), bf16),
            pltpu.VMEM((4, depth, wide), bf16),
            pltpu.VMEM((4, 4, tokens + 16, features), bf16),
            pltpu.VMEM((4, tokens, wide), bf16),
            pltpu.VMEM((2, tokens // 2, wide), bf16),
            pltpu.VMEM((2, tokens, wide), bf16),
            pltpu.VMEM((4, 8, 128), f32),
            pltpu.VMEM((3, 8, 128), f32),
            dma((groups,)),
            dma((groups,)),
            dma((3,)),
            dma((4,)),
            dma((groups,)),
            dma((groups,)),
            dma((groups,)),
            dma((groups,)),
            dma((6, 2)),
            dma((4, 2, 2)),
            dma,
            dma((2,)),
            dma((4, 2)),
            dma((4, 2, 2)),
            dma((4, 2)),
            dma((4, 4, 2)),
            dma((4, 4, 2)),
            dma((6, 2)),
            dma((2, 2)),
            dma((2, 2, 2)),
            dma((3,)),
            dma((3,)),
            dma((4,)),
        ],
        compiler_params=pltpu.CompilerParams(
            collective_id=1, has_side_effects=True, vmem_limit_bytes=48 * 2**20
        ),
        name="layer",
    )(
        lengths,
        counts,
        q,
        jnp.asarray(inverse_frequencies(64)),
        page_slots,
        suffix,
        residual,
        gain,
        cache,
        weights,
    )


def on_device(
    queries,
    suffix_key_value,
    residual,
    gain,
    gate_up,
    prefix_cache_slots,
    prefix_page_slots,
    lengths,
    counts,
):
    slots, page_len, heads_kv, lanes = prefix_cache_slots.shape
    return layer(
        lengths.T,
        counts,
        queries,
        prefix_page_slots[None, :],
        suffix_key_value,
        residual,
        gain[None, :],
        prefix_cache_slots.reshape(slots * page_len, heads_kv, lanes),
        gate_up.reshape(gate_up.shape[0], 2 * gate_up.shape[2]),
    )


def solution(mesh):
    placed = (
        P("req", "blk"),
        P("req", None, None),
        P("req", "blk"),
        P("blk"),
        P("blk", None, "req"),
        P("req", None, None, None),
        P(),
        P(),
        P(),
    )
    return jax.shard_map(
        on_device,
        mesh=mesh,
        in_specs=placed,
        out_specs=(P("blk", "req"), P("req", "blk")),
        check_vma=False,
    )
```

```python
import math

import jax
import jax.numpy as jnp
from jax import lax
from jax.experimental import pallas as pl
from jax.experimental.pallas import tpu as pltpu
from jax.sharding import PartitionSpec as P
import numpy as np

D = 8192

MESH = pl.DeviceIdType.MESH

NEGATIVE = -1e30
EPSILON = 1e-05
ROPE_BASE = 500000.0


def inverse_frequencies(half_dim):
    exponent = np.float32(-math.log(ROPE_BASE)) * np.arange(half_dim, dtype=np.float32)
    exponent = exponent * np.float32(2.0) / np.float32(2 * half_dim)
    inverse = np.exp(exponent.astype(np.float64)).astype(np.float32)
    return np.concatenate([inverse, inverse])[None, :]


def remote(src, dst, send_sem, recv_sem, req, blk):
    return pltpu.make_async_remote_copy(
        src_ref=src,
        dst_ref=dst,
        send_sem=send_sem,
        recv_sem=recv_sem,
        device_id=(req, blk),
        device_id_type=MESH,
    )


def place():
    req, blk = lax.axis_index("req"), lax.axis_index("blk")
    y, zl, core = req // 4, (req // 2) % 2, req % 2
    return req, blk, y, zl, core, blk // 4, blk % 4


def weight_pieces(w_ref, w_all, chunk):
    half = w_ref.shape[0] // 2

    def own(part):
        return w_ref.at[pl.ds(part * half, half), chunk]

    def slot(source, part):
        return w_all.at[source, pl.ds(part * half, half), chunk]

    return own, slot


def weight_sends(w_ref, w_all, send, recv, q, chunk):
    req, blk, y, zl, core, zh, x = place()
    own, slot = weight_pieces(w_ref, w_all, chunk)
    return [
        remote(
            own(part),
            slot(x, part),
            send.at[j, q],
            recv.at[x, part, q],
            req,
            zh * 4 + (x + 4 + step) % 4,
        )
        for j, (step, part) in enumerate(((1, 0), (-1, 1), (1, 1), (-1, 0)))
    ]


def weight_relays(w_ref, w_all, send, recv, q, chunk):
    req, blk, y, zl, core, zh, x = place()
    own, slot = weight_pieces(w_ref, w_all, chunk)
    out = []
    for j, (step, part) in enumerate(((1, 0), (-1, 1))):
        source = (x + 4 - step) % 4
        piece = slot(source, part)
        to_blk = zh * 4 + (x + 4 + step) % 4
        out.append(remote(piece, piece, send.at[4 + j, q], recv.at[source, part, q], req, to_blk))
    return out


def weight_wait(w_ref, w_all, send, recv, q, chunk, source, part):
    req, blk, y, zl, core, zh, x = place()
    piece = weight_pieces(w_ref, w_all, chunk)[1](source, part)
    to_blk = zh * 4 + (x + 1) % 4
    remote(piece, piece, send.at[0, q], recv.at[source, part, q], req, to_blk).wait_recv()


def spread_features(
    u_ref, a_all, x_send, z_send, y_send, on_send, core_send, recv, after_hop
):
    req, blk, y, zl, core, zh, x = place()
    target = zl * 2 + core
    home = core == x % 2
    root = x == target
    over_z = y * 4 + (1 - zl) * 2 + core
    sibling = y * 4 + zl * 2 + (1 - core)
    up, down = (y + 1) % 4, (y + 3) % 4
    far = (y + 2) % 4
    req_up, req_down = up * 4 + zl * 2 + core, down * 4 + zl * 2 + core

    rows = u_ref.shape[0]
    halves = (pl.ds(0, 64), pl.ds(64, rows - 64))
    both = range(2)

    def block_copy(yy, xx, h, send, to_req, to_blk):
        piece = a_all.at[yy, xx, halves[h]]
        return remote(piece, piece, send, recv.at[yy, xx, h], to_req, to_blk)

    hops = [
        remote(
            u_ref.at[halves[h]],
            a_all.at[y, x, halves[h]],
            x_send.at[h],
            recv.at[y, x, h],
            req,
            zh * 4 + target,
        )
        for h in both
    ]
    keeps = [
        pltpu.make_async_copy(u_ref.at[halves[h]], a_all.at[y, x, halves[h]], recv.at[y, x, h])
        for h in both
    ]

    @pl.when(root)
    def _():
        for keep in keeps:
            keep.start()

    @pl.when(jnp.logical_not(root))
    def _():
        for hop in hops:
            hop.start()

    after_hop()

    def to_core(yy, xx, h):
        return block_copy(yy, xx, h, core_send.at[yy, xx, h], sibling, blk)

    def to_z(xx, h):
        return block_copy(y, xx, h, z_send.at[xx, h], over_z, blk)

    def to_y(xx, h, way):
        return block_copy(y, xx, h, y_send.at[xx, way, h], (req_up, req_down)[way], blk)

    def onward(xx, h, way):
        return block_copy((down, up)[way], xx, h, on_send.at[xx, h], (req_up, req_down)[way], blk)

    def arrived(yy, xx, h):
        block_copy(yy, xx, h, x_send.at[0], over_z, blk).wait_recv()

    def nearest(i):
        return (x + group_at(i)) % 4

    def own_stage():
        @pl.when(home)
        def _():
            def step(i, carry):
                xx = nearest(i)

                for h in both:

                    @pl.when(root & (i == 0))
                    def _():
                        keeps[h].wait()

                    @pl.when(jnp.logical_not(root & (i == 0)))
                    def _():
                        arrived(y, xx, h)

                    to_y(xx, h, 0).start()
                    to_y(xx, h, 1).start()

                    @pl.when(root)
                    def _():
                        to_z(xx, h).start()

                    to_core(y, xx, h).start()
                return carry

            lax.fori_loop(0, 4, step, 0)

        take(y)

    def near_stage():
        @pl.when(home)
        def _():
            def step(i, carry):
                xx = nearest(i)
                for h in both:
                    arrived(down, xx, h)

                    @pl.when(i % 2 == 0)
                    def _():
                        onward(xx, h, 0).start()

                    to_core(down, xx, h).start()
                    arrived(up, xx, h)

                    @pl.when(i % 2 == 1)
                    def _():
                        onward(xx, h, 1).start()

                    to_core(up, xx, h).start()
                return carry

            lax.fori_loop(0, 4, step, 0)

        take(down)
        take(up)

    def last_stage():
        @pl.when(home)
        def _():
            def step(i, carry):
                xx = nearest(i)
                for h in both:
                    arrived(far, xx, h)
                    to_core(far, xx, h).start()
                return carry

            lax.fori_loop(0, 4, step, 0)

        take(far)

    def take(yy):
        @pl.when(jnp.logical_not(home))
        def _():
            def step(i, carry):
                for h in both:
                    arrived(yy, nearest(i), h)
                return carry

            lax.fori_loop(0, 4, step, 0)

    def drain():
        @pl.when(jnp.logical_not(root))
        def _():
            for hop in hops:
                hop.wait_send()

        @pl.when(home)
        def _():
            def step(i, carry):
                xx = nearest(i)

                for h in both:

                    @pl.when(root)
                    def _():
                        to_z(xx, h).wait_send()

                    to_y(xx, h, 0).wait_send()
                    to_y(xx, h, 1).wait_send()

                    @pl.when(i % 2 == 0)
                    def _():
                        onward(xx, h, 0).wait_send()

                    @pl.when(i % 2 == 1)
                    def _():
                        onward(xx, h, 1).wait_send()

                return carry

            lax.fori_loop(0, 4, step, 0)

            def core_step(i, carry):
                for h in both:
                    to_core(i // 4, i % 4, h).wait_send()
                return carry

            lax.fori_loop(0, 16, core_step, 0)

    return own_stage, near_stage, last_stage, drain


def group_at(j):
    return j + j // 2 - 2 * (j // 3)


def layer_kernel(
    lengths_ref,
    counts_ref,
    q_ref,
    inverse_ref,
    page_slots_ref,
    suffix_ref,
    residual_ref,
    gain_ref,
    cache_ref,
    w_ref,
    hidden_ref,
    updated_ref,
    slab,
    pages_ref,
    fresh_ref,
    hide,
    q_all,
    kv_all,
    values_t,
    scores,
    probs,
    part_out,
    stat_out,
    part_in,
    stat_in,
    held_part,
    held_stat,
    u_ref,
    w_all,
    a_all,
    product,
    relay,
    final,
    gate_kept,
    square_out,
    square_in,
    query_send,
    query_recv,
    page_send,
    page_recv,
    part_send,
    part_recv,
    stat_send,
    stat_recv,
    w_send,
    w_recv,
    w_local,
    x_send,
    z_send,
    y_send,
    on_send,
    core_send,
    a_recv,
    r_send,
    relay_recv,
    final_recv,
    q_send,
    q_recv,
    slab_recv,
):
    req, blk, y, zl, core, zh, x = place()
    tokens, features = q_ref.shape
    heads = features // 128
    keys_here = slab.shape[0]
    rows_all = heads * tokens
    width = hidden_ref.shape[1]
    sibling = y * 4 + zl * 2 + (1 - core)
    blk_up, blk_far, blk_down = [((zh + i) % 4) * 4 + x for i in (1, 2, 3)]
    turn = (1.0 / math.sqrt(128)) * math.log2(math.e)

    bounds_w = ((0, width), (width, 2 * width))
    chunks_w = tuple(pl.ds(low, high - low) for low, high in bounds_w)
    over_z = y * 4 + (1 - zl) * 2 + core

    def ahead(j):
        return ((y + group_at(j)) % 4) * 4 + zl * 2 + core

    def behind(j):
        return ((y + 4 - group_at(j)) % 4) * 4 + zl * 2 + core

    barrier = pltpu.get_barrier_semaphore()
    peers = [(req, zh * 4 + (x + i) % 4) for i in (1, 2, 3)]
    peers += [(sibling, blk), (req, blk_up), (req, blk_far), (req, blk_down)]
    peers += [(over_z, blk)] + [(ahead(j), blk) for j in range(1, 4)]
    for peer in peers:
        pl.semaphore_signal(barrier, inc=1, device_id=peer, device_id_type=MESH)

    pieces = slab_recv.shape[0]
    keys_piece = keys_here // pieces
    slab_copies = [
        pltpu.make_async_copy(
            cache_ref.at[pl.ds(i * keys_piece, keys_piece)],
            slab.at[pl.ds(i * keys_piece, keys_piece)],
            slab_recv.at[i],
        )
        for i in range(pieces)
    ]
    for copy in slab_copies:
        copy.start()

    own_lengths = [lengths_ref[i, req] for i in range(3)]
    starts = [own_lengths[0], own_lengths[0] + own_lengths[1]]
    starts.append(starts[1] + own_lengths[2])
    down_rows = lax.broadcasted_iota(jnp.int32, (tokens, 128), 0)
    along = lax.broadcasted_iota(jnp.int32, (tokens, 128), 1)

    def begin_of(token):
        begin = jnp.zeros_like(token)
        for start in starts:
            begin = jnp.where(token >= start, start, begin)
        return begin

    begin = begin_of(down_rows)
    position = counts_ref[req] * 128 + (down_rows - begin)
    angle = position.astype(jnp.float32) * inverse_ref[...]
    cosines = jnp.cos(angle)
    sines = jnp.where(along < 64, -1.0, 1.0) * jnp.sin(angle)
    allowed = (begin == begin_of(along)) & (down_rows <= along)

    def turned(vector):
        return (vector * cosines + pltpu.roll(vector, 64, 1) * sines).astype(jnp.bfloat16)

    head = blk // 2
    chosen = lax.broadcasted_iota(jnp.int32, (1, 8, 256), 1) == head
    chosen = chosen.astype(jnp.bfloat16)

    def pick_head(block):
        block = block * chosen
        block = block[:, 0:4] + block[:, 4:8]
        block = block[:, 0:2] + block[:, 2:4]
        return block[:, 0] + block[:, 1]

    for h in range(heads):
        vector = q_ref[:, h * 128 : (h + 1) * 128].astype(jnp.float32)
        q_all[0, h * tokens : (h + 1) * tokens, :] = turned(vector)
    pl.semaphore_wait(barrier, len(peers))

    def part_of(r):
        return ((zl + r // 2) % 2) * 2 + (core + r % 2) % 2

    def page_piece(r, send, to_req):
        piece = kv_all.at[part_of(r)]
        return remote(piece, piece, page_send.at[send], page_recv.at[part_of(r)], to_req, blk)

    own_pages = kv_all.at[part_of(0)]
    page_copies = [
        remote(pages_ref, own_pages, page_send.at[i], page_recv.at[part_of(0)], to_req, blk)
        for i, to_req in enumerate((sibling, over_z))
    ]
    page_on = page_piece(2, 2, sibling)
    query_copies = [
        remote(q_all.at[0], q_all.at[j], query_send.at[j], query_recv.at[j], ahead(j), blk)
        for j in range(1, 4)
    ]
    sends = [weight_sends(w_ref, w_all, w_send, w_recv, q, chunks_w[q]) for q in range(2)]
    for copy in query_copies + sends[0]:
        copy.start()
    local = pltpu.make_async_copy(w_ref, w_all.at[x], w_local)
    local.start()
    for i, copy in enumerate(slab_copies):
        copy.wait()

        def pick(p, carry):
            rows = pl.ds(pl.multiple_of(i * keys_piece + p * 128, 128), 128)
            pages_ref[rows, :] = pick_head(slab[rows])
            return carry

        lax.fori_loop(0, keys_piece // 128, pick, 0)
    for copy in page_copies:
        copy.start()
    kv_all[part_of(0)] = pages_ref[...]

    suffix = pick_head(suffix_ref[...])
    fresh_ref[:, 0:128] = turned(suffix[:, 0:128].astype(jnp.float32))
    fresh_ref[:, 128:256] = suffix[:, 128:256]

    @pl.when(blk % 2 == 0)
    def _():
        updated_ref[...] = fresh_ref[:, 0:128]

    @pl.when(blk % 2 == 1)
    def _():
        updated_ref[...] = fresh_ref[:, 128:256]

    slots_here = 4 * keys_here // 128
    slot_ids = (req // 4) * slots_here + lax.broadcasted_iota(jnp.int32, (slots_here, 128), 0)
    page_ids = lax.broadcasted_iota(jnp.int32, (slots_here, 128), 1).astype(jnp.float32)
    match = page_slots_ref[...] == slot_ids
    page_of = jnp.sum(jnp.where(match, page_ids, 0.0), 1, keepdims=True)
    for j in range(4):
        seen = counts_ref[behind(j)].astype(jnp.float32)
        level = jnp.where(page_of < seen, 0.0, NEGATIVE)
        for part in range(4):
            rows = slice(part * slots_here // 4, (part + 1) * slots_here // 4)
            hide[j, part] = jnp.broadcast_to(level[rows], (slots_here // 4, rows_all))

    def fold(block, op):
        parts = [block[i * 8 : (i + 1) * 8] for i in range(block.shape[0] // 8)]
        while len(parts) > 1:
            parts = [op(a, b) for a, b in zip(parts[::2], parts[1::2])]
        return parts[0]

    def last_fold(rows, op):
        return op(rows, 0, keepdims=True)

    fresh_t = jnp.transpose(fresh_ref[:, 128:256].astype(jnp.float32)).astype(jnp.bfloat16)
    raw = lax.dot_general(
        fresh_ref[:, 0:128],
        q_all[0],
        (((1,), (1,)), ((), ())),
        preferred_element_type=jnp.float32,
    )
    mask = jnp.concatenate([allowed.astype(jnp.float32)] * heads, 1)
    raw = jnp.where(mask > 0, raw, NEGATIVE)
    suffix_max = last_fold(fold(raw, jnp.maximum), jnp.max)
    suffix_probs = jnp.exp2((raw - suffix_max) * turn)
    suffix_sum = last_fold(fold(suffix_probs, jnp.add), jnp.sum)
    suffix_part = jnp.dot(
        fresh_t, suffix_probs.astype(jnp.bfloat16), preferred_element_type=jnp.float32
    )

    def turn_values(r):
        for p in range(keys_here // 128):
            block = kv_all[part_of(r), p * 128 : (p + 1) * 128, 128:256].astype(jnp.float32)
            start = r * keys_here + p * 128
            values_t[0:128, start : start + 128] = jnp.transpose(block).astype(jnp.bfloat16)

    values_t[128:144, :] = jnp.ones((16, values_t.shape[1]), jnp.bfloat16)
    turn_values(0)
    page_piece(1, 2, sibling).wait_recv()
    turn_values(1)

    chunk = 512
    chunks = 2 * keys_here // chunk
    per_core = keys_here // chunk

    def score_chunk(c, j, a, top):
        part = part_of(2 * a + c // per_core)
        inside = c % per_core
        keys = kv_all[part, inside * chunk : (inside + 1) * chunk, 0:128]
        raw = lax.dot_general(
            keys, q_all[j], (((1,), (1,)), ((), ())), preferred_element_type=jnp.float32
        )
        scores[c * chunk : (c + 1) * chunk, :] = raw
        for p in range(chunk // 128):
            page = inside * (chunk // 128) + p
            folded = fold(raw[p * 128 : (p + 1) * 128], jnp.maximum)
            top = jnp.maximum(top, folded + hide[j, part, page : page + 1, :])
        return top

    def weigh_chunk(c, j, a, top, weighted):
        part = part_of(2 * a + c // per_core)
        for p in range(chunk // 128):
            page = (c % per_core) * (chunk // 128) + p
            rows = slice(c * chunk + p * 128, c * chunk + (p + 1) * 128)
            level = top - 4.0 * hide[j, part, page : page + 1, :]
            weights = jnp.exp2((scores[rows, :] - level) * turn)
            probs[rows, :] = weights.astype(jnp.bfloat16)
        columns = pl.ds(pl.multiple_of(a * 2 * keys_here + c * chunk, chunk), chunk)
        product_here = jnp.dot(
            values_t[:, columns],
            probs[c * chunk : (c + 1) * chunk, :],
            preferred_element_type=jnp.float32,
        )
        return product_here if weighted is None else weighted + product_here

    first_row = lax.broadcasted_iota(jnp.int32, (8, rows_all), 0) == 0

    def merge(j, top, total, weighted):
        other_top, other_sum = held_stat[j, 0:1, :], held_stat[j, 1:2, :]
        joint = jnp.maximum(top, other_top)
        here, there = jnp.exp2((top - joint) * turn), jnp.exp2((other_top - joint) * turn)
        return joint, total * here + other_sum * there, weighted * here + held_part[j] * there

    def part_copies(j):
        return (
            remote(
                part_out.at[j], part_in.at[j], part_send.at[j], part_recv.at[j], behind(j), blk
            ),
            remote(
                stat_out.at[j], stat_in.at[j], stat_send.at[j], stat_recv.at[j], behind(j), blk
            ),
        )

    def unit(u):
        v = u - 4
        later = jnp.where(v == 0, 3, jnp.where(v == 3, 0, v))
        return jnp.where(u < 4, u, later), jnp.where(u < 4, 0, 1)

    low = jnp.full((8, rows_all), NEGATIVE, jnp.float32)

    relays = [weight_relays(w_ref, w_all, w_send, w_recv, q, chunks_w[q]) for q in range(2)]

    def relay_chunk(q):
        for (step, part), copy in zip(((1, 0), (-1, 1)), relays[q]):
            source = (x + 4 - step) % 4
            weight_wait(w_ref, w_all, w_send, w_recv, q, chunks_w[q], source, part)
            copy.start()

    def more_weights():
        for copy in sends[1]:
            copy.start()

    def unit_step(u, carry):
        j, a = unit(u)

        @pl.when(u == 4)
        def _():
            relay_chunk(0)

        @pl.when((u > 0) & (u < 4))
        def _():
            remote(
                q_all.at[0], q_all.at[j], query_send.at[1], query_recv.at[j], ahead(1), blk
            ).wait_recv()

        @pl.when(u == 3)
        def _():
            page_piece(2, 2, over_z).wait_recv()
            page_on.start()
            turn_values(2)

        @pl.when(u == 4)
        def _():
            page_piece(3, 2, sibling).wait_recv()
            turn_values(3)

        top, weighted = low, None
        for c in range(chunks):
            top = score_chunk(c, j, a, top)
        top = last_fold(top, jnp.max)
        for c in range(chunks):
            weighted = weigh_chunk(c, j, a, top, weighted)
        total, weighted = weighted[128:129], weighted[0:128]

        @pl.when(u < 4)
        def _():
            held_part[j] = weighted
            held_stat[j] = jnp.where(first_row, top, total)

        @pl.when(u >= 4)
        def _():
            joint, joint_sum, joint_part = merge(j, top, total, weighted)

            @pl.when(u < 7)
            def _():
                part_out[j] = joint_part.astype(jnp.bfloat16)
                stat_out[j] = jnp.where(first_row, joint, joint_sum)
                for copy in part_copies(j):
                    copy.start()

            @pl.when(u == 7)
            def _():
                held_part[0] = joint_part
                held_stat[0] = jnp.where(first_row, joint, joint_sum)

        return carry

    lax.fori_loop(0, 8, unit_step, 0)

    order = (1, 2, 3)
    for j in order:
        part_copies(j)[1].wait_recv()
    tops = [stat_in[j, 0:1, :] for j in order]
    sums = [stat_in[j, 1:2, :] for j in order]
    own_top, own_total = held_stat[0, 0:1, :], held_stat[0, 1:2, :]
    joint = jnp.maximum(suffix_max, own_top)
    for row in tops:
        joint = jnp.maximum(joint, row)
    factor, own_factor = (jnp.exp2((row - joint) * turn) for row in (suffix_max, own_top))
    joint_sum = suffix_sum * factor + own_total * own_factor
    attended = suffix_part * factor + held_part[0] * own_factor
    for j, row, row_sum in zip(order, tops, sums):
        factor = jnp.exp2((row - joint) * turn)
        joint_sum = joint_sum + row_sum * factor
        part_copies(j)[0].wait_recv()
        attended = attended + part_in[j].astype(jnp.float32) * factor
    attended = attended / joint_sum

    squares_here = jnp.zeros((tokens, 128), jnp.float32)
    for h in range(heads):
        cols = slice(h * 128, (h + 1) * 128)
        own = jnp.transpose(attended[:, h * tokens : (h + 1) * tokens])
        stream = (residual_ref[:, cols].astype(jnp.float32) + own).astype(jnp.bfloat16)
        stream = stream.astype(jnp.float32)
        squares_here = squares_here + stream * stream
        u_ref[0:tokens, cols] = (stream * gain_ref[:, cols]).astype(jnp.bfloat16)
    square_row = jnp.sum(jnp.transpose(squares_here), 0, keepdims=True)
    high = square_row.astype(jnp.bfloat16)
    below = (square_row - high.astype(jnp.float32)).astype(jnp.bfloat16)
    u_ref[tokens : tokens + 16, 0:128] = jnp.broadcast_to(high, (16, 128))
    u_ref[tokens : tokens + 16, 128:256] = jnp.broadcast_to(below, (16, 128))
    u_ref[tokens : tokens + 16, 256:features] = jnp.zeros((16, features - 256), jnp.bfloat16)

    own_stage, near_stage, last_stage, drain = spread_features(
        u_ref, a_all, x_send, z_send, y_send, on_send, core_send, a_recv, more_weights
    )

    def multiply(zt, target, q):
        first, end = bounds_w[q]
        for start in range(first, end, 512):
            cols = pl.ds(start, min(512, end - start))
            total = jnp.dot(
                a_all[zt, 0, 0:tokens, :], w_all[0, :, cols], preferred_element_type=jnp.float32
            )
            for xx in range(1, 4):
                total = total + jnp.dot(
                    a_all[zt, xx, 0:tokens, :],
                    w_all[xx, :, cols],
                    preferred_element_type=jnp.float32,
                )
            target[:, cols] = total.astype(target.dtype)

    half = tokens // 2
    top_rows, bottom_rows = pl.ds(0, half), pl.ds(half, half)

    def exchange(q):
        cols = chunks_w[q]

        def piece(i, slot, rows, target, recv, to_blk):
            source = product.at[slot, rows, cols]
            return remote(source, target, r_send.at[i, q], recv, req, to_blk)

        def landing(side, rows):
            return final.at[side, rows, cols]

        return (
            piece(0, 2, top_rows, relay.at[0, :, cols], relay_recv.at[0, q], blk_up),
            piece(1, 2, bottom_rows, relay.at[1, :, cols], relay_recv.at[1, q], blk_down),
            piece(2, 1, bottom_rows, landing(0, bottom_rows), final_recv.at[0, 1, q], blk_up),
            piece(3, 3, top_rows, landing(1, top_rows), final_recv.at[1, 0, q], blk_down),
            piece(4, 1, top_rows, landing(0, top_rows), final_recv.at[0, 0, q], blk_up),
            piece(5, 3, bottom_rows, landing(1, bottom_rows), final_recv.at[1, 1, q], blk_down),
        )

    exchanges = [exchange(0), exchange(1)]

    def wait_weights(q):
        for step, part in ((3, 0), (3, 1), (1, 0), (1, 1), (2, 0), (2, 1)):
            if (step, part) not in ((3, 0), (1, 1)):
                source = (x + step) % 4
                weight_wait(w_ref, w_all, w_send, w_recv, q, chunks_w[q], source, part)

    def add_relay(slot, rows, index, q):
        def tile(n, carry):
            cols = pl.ds(pl.multiple_of(n * 128, 128), 128)
            total = product[slot, rows, cols].astype(jnp.float32) + relay[index, :, cols].astype(
                jnp.float32
            )
            product[slot, rows, cols] = total.astype(jnp.bfloat16)
            return carry

        first, end = bounds_w[q]
        lax.fori_loop(first // 128, end // 128, tile, 0)

    def send_sums(q):
        exchanges[q][0].wait_recv()
        add_relay(1, top_rows, 0, q)
        exchanges[q][4].start()
        exchanges[q][1].wait_recv()
        add_relay(3, bottom_rows, 1, q)
        exchanges[q][5].start()

    def first_step(i, carry):
        @pl.when(i == 0)
        def _():
            own_stage()
            local.wait()
            wait_weights(0)

        @pl.when(i == 1)
        def _():
            near_stage()

        @pl.when(i == 3)
        def _():
            last_stage()

        zt = (y + group_at(i)) % 4
        distance = (zt + 4 - zh) % 4
        multiply(zt, product.at[distance], 0)

        @pl.when(distance == 2)
        def _():
            exchanges[0][0].start()
            exchanges[0][1].start()

        @pl.when(distance == 1)
        def _():
            exchanges[0][2].start()

        @pl.when(distance == 3)
        def _():
            exchanges[0][3].start()

        return carry

    lax.fori_loop(0, 4, first_step, 0)

    def squares(zt, carry):
        total = jnp.zeros((8, 128), jnp.float32)
        for xx in range(4):
            rows = a_all[zt, xx, tokens : tokens + 16, 0:256].astype(jnp.float32)
            total = total + rows[0:8, 0:128] + rows[0:8, 128:256]
        square_out[zt] = total
        return carry

    lax.fori_loop(0, 4, squares, 0)
    square_copies = []
    for i in (1, 2, 3):
        there = (zh + i) % 4
        square_copies.append(
            remote(
                square_out.at[there],
                square_in.at[i - 1],
                q_send.at[i - 1],
                q_recv.at[i - 1],
                req,
                there * 4 + x,
            )
        )
    for copy in square_copies:
        copy.start()

    relay_chunk(1)
    send_sums(0)
    wait_weights(1)
    multiply((zh + 2) % 4, product.at[2], 1)
    exchanges[1][0].start()
    exchanges[1][1].start()
    multiply((zh + 1) % 4, product.at[1], 1)
    exchanges[1][2].start()
    multiply((zh + 3) % 4, product.at[3], 1)
    exchanges[1][3].start()
    multiply(zh, product.at[0], 1)
    send_sums(1)

    for copy in square_copies:
        copy.wait_recv()
    row = square_out[zh] + square_in[0] + square_in[1] + square_in[2]
    spread = jnp.broadcast_to(row[0:1, :], (tokens, tokens))
    diagonal = lax.broadcasted_iota(jnp.int32, (tokens, tokens), 0) == lax.broadcasted_iota(
        jnp.int32, (tokens, tokens), 1
    )
    square_sum = jnp.sum(jnp.where(diagonal, spread, 0.0), 1, keepdims=True)
    scale = jnp.broadcast_to(lax.rsqrt(square_sum / D + EPSILON), (tokens, 128))

    def column_sum(start):
        cols = pl.ds(pl.multiple_of(start, 128), 128)
        total = product[0, :, cols].astype(jnp.float32) + final[0, :, cols].astype(jnp.float32)
        return (total + final[1, :, cols].astype(jnp.float32)) * scale

    def finish_gate(n, carry):
        gate = column_sum(n * 128)
        gate_kept[:, pl.ds(pl.multiple_of(n * 128, 128), 128)] = gate / (1.0 + jnp.exp(-gate))
        return carry

    def finish_up(n, carry):
        cols = pl.ds(pl.multiple_of(n * 128, 128), 128)
        value = gate_kept[:, cols] * column_sum(width + n * 128)
        hidden_ref[:, cols] = value.astype(jnp.bfloat16)
        return carry

    for q, finish in enumerate((finish_gate, finish_up)):
        for copy in exchanges[q][2:]:
            copy.wait_recv()
        lax.fori_loop(0, width // 128, finish, 0)

    for copy in sends[0] + sends[1] + relays[0] + relays[1] + square_copies:
        copy.wait_send()
    for q in range(2):
        for copy in exchanges[q]:
            copy.wait_send()
    drain()
    for copy in query_copies + page_copies + [page_on]:
        copy.wait_send()
    for j in order:
        for copy in part_copies(j):
            copy.wait_send()


def layer(lengths, counts, q, page_slots, suffix, residual, gain, cache, weights):
    depth, wide = weights.shape
    tokens, features = q.shape
    rows_all = tokens * features // 128
    keys_here, _, lanes = cache.shape
    keys = 2 * keys_here
    groups = 4
    dma = pltpu.SemaphoreType.DMA
    bf16, f32 = jnp.bfloat16, jnp.float32
    vmem = pl.BlockSpec(memory_space=pltpu.VMEM)
    return pl.pallas_call(
        layer_kernel,
        out_shape=(
            jax.ShapeDtypeStruct((tokens, wide // 2), bf16),
            jax.ShapeDtypeStruct((tokens, 128), bf16),
        ),
        in_specs=[pl.BlockSpec(memory_space=pltpu.SMEM)] * 2
        + [vmem] * 6
        + [pl.BlockSpec(memory_space=pl.ANY)] * 2,
        out_specs=(vmem, vmem),
        scratch_shapes=[
            pltpu.VMEM(cache.shape, bf16),
            pltpu.VMEM((keys_here, lanes), bf16),
            pltpu.VMEM((tokens, lanes), bf16),
            pltpu.VMEM((groups, 4, keys_here // 128, rows_all), f32),
            pltpu.VMEM((groups, rows_all, 128), bf16),
            pltpu.VMEM((4, keys_here, lanes), bf16),
            pltpu.VMEM((144, 2 * keys), bf16),
            pltpu.VMEM((keys, rows_all), f32),
            pltpu.VMEM((keys, rows_all), bf16),
            pltpu.VMEM((groups, 128, rows_all), bf16),
            pltpu.VMEM((groups, 8, rows_all), f32),
            pltpu.VMEM((groups, 128, rows_all), bf16),
            pltpu.VMEM((groups, 8, rows_all), f32),
            pltpu.VMEM((groups, 128, rows_all), f32),
            pltpu.VMEM((groups, 8, rows_all), f32),
            pltpu.VMEM((tokens + 16, features), bf16),
            pltpu.VMEM((4, depth, wide), bf16),
            pltpu.VMEM((4, 4, tokens + 16, features), bf16),
            pltpu.VMEM((4, tokens, wide), bf16),
            pltpu.VMEM((2, tokens // 2, wide), bf16),
            pltpu.VMEM((2, tokens, wide), bf16),
            pltpu.VMEM((tokens, wide // 2), f32),
            pltpu.VMEM((4, 8, 128), f32),
            pltpu.VMEM((3, 8, 128), f32),
            dma((groups,)),
            dma((groups,)),
            dma((3,)),
            dma((4,)),
            dma((groups,)),
            dma((groups,)),
            dma((groups,)),
            dma((groups,)),
            dma((6, 2)),
            dma((4, 2, 2)),
            dma,
            dma((2,)),
            dma((4, 2)),
            dma((4, 2, 2)),
            dma((4, 2)),
            dma((4, 4, 2)),
            dma((4, 4, 2)),
            dma((6, 2)),
            dma((2, 2)),
            dma((2, 2, 2)),
            dma((3,)),
            dma((3,)),
            dma((4,)),
        ],
        compiler_params=pltpu.CompilerParams(
            collective_id=1, has_side_effects=True, vmem_limit_bytes=48 * 2**20
        ),
        name="layer",
    )(
        lengths,
        counts,
        q,
        jnp.asarray(inverse_frequencies(64)),
        page_slots,
        suffix,
        residual,
        gain,
        cache,
        weights,
    )


def on_device(
    queries,
    suffix_key_value,
    residual,
    gain,
    gate_up,
    prefix_cache_slots,
    prefix_page_slots,
    lengths,
    counts,
):
    slots, page_len, heads_kv, lanes = prefix_cache_slots.shape
    return layer(
        lengths.T,
        counts,
        queries,
        prefix_page_slots[None, :],
        suffix_key_value,
        residual,
        gain[None, :],
        prefix_cache_slots.reshape(slots * page_len, heads_kv, lanes),
        gate_up.reshape(gate_up.shape[0], 2 * gate_up.shape[2]),
    )


def solution(mesh):
    placed = (
        P("req", "blk"),
        P("req", None, None),
        P("req", "blk"),
        P("blk"),
        P("blk", None, "req"),
        P("req", None, None, None),
        P(),
        P(),
        P(),
    )
    return jax.shard_map(
        on_device,
        mesh=mesh,
        in_specs=placed,
        out_specs=(P("blk", "req"), P("req", "blk")),
        check_vma=False,
    )
```
